32 devices in a mesh: dp: 16 (over z, x, core), tensor: 2 (over y).
Axes of the slice: x: 2, y: 2, z: 4, core: 2. Of those that a mesh axis runs over, the one named last changes fastest.
Arguments:
- inputs: bfloat16 [4, 8192, 768], P(None, ('dp', 'tensor')), may hold values from -6 to 6
- segments: int32 [4, 8192], P(None, 'dp'), may hold values from 0 to 127, as said below
- padding: int32 [4, 8192], P(None, 'dp'), may hold values from 0 to 1, as said below
- query_weight: bfloat16 [768, 768], P(None, 'tensor'), may hold values from -0.21875 to 0.21875
- query_bias: bfloat16 [768], P('tensor'), may hold values from -3 to 3
- key_weight: bfloat16 [768, 768], P(None, 'tensor'), may hold values from -0.21875 to 0.21875
- value_weight: bfloat16 [768, 768], P(None, 'tensor'), may hold values from -0.21875 to 0.21875
- value_bias: bfloat16 [768], P('tensor'), may hold values from -3 to 3
- output_weight: bfloat16 [768, 768], P('tensor'), may hold values from -0.875 to 0.875
- output_bias: bfloat16 [768], replicated, may hold values from -1.75 to 1.75
- first_gain: bfloat16 [768], replicated, may hold values from 0.25 to 1.75
- first_shift: bfloat16 [768], replicated, may hold values from -1.75 to 1.75
- expand_weight: bfloat16 [768, 3072], P(None, 'tensor'), may hold values from -0.21875 to 0.21875
- expand_bias: bfloat16 [3072], P('tensor'), may hold values from -3 to 3
- reduce_weight: bfloat16 [3072, 768], P('tensor'), may hold values from -0.109375 to 0.109375
- reduce_bias: bfloat16 [768], replicated, may hold values from -1.75 to 1.75
- second_gain: bfloat16 [768], replicated, may hold values from 0.25 to 1.75
- second_shift: bfloat16 [768], replicated, may hold values from -1.75 to 1.75
- cotangent: bfloat16 [4, 8192, 768], P(None, ('dp', 'tensor')), may hold values from -6 to 6
Outputs:
- layer_output: float32 [4, 8192, 768], P(None, ('dp', 'tensor'))
- input_gradient: float32 [4, 8192, 768], P(None, ('dp', 'tensor'))
- query_weight_gradient: float32 [768, 768], P(None, 'tensor')
- query_bias_gradient: float32 [768], P('tensor')
- key_weight_gradient: float32 [768, 768], P(None, 'tensor')
- value_weight_gradient: float32 [768, 768], P(None, 'tensor')
- value_bias_gradient: float32 [768], P('tensor')
- output_weight_gradient: float32 [768, 768], P('tensor')
- output_bias_gradient: float32 [768], replicated
- first_gain_gradient: float32 [768], replicated
- first_shift_gradient: float32 [768], replicated
- expand_weight_gradient: float32 [768, 3072], P(None, 'tensor')
- expand_bias_gradient: float32 [3072], P('tensor')
- reduce_weight_gradient: float32 [3072, 768], P('tensor')
- reduce_bias_gradient: float32 [768], replicated
- second_gain_gradient: float32 [768], replicated
- second_shift_gradient: float32 [768], replicated
The draws below stay inside these ranges and needn't reach their ends.
Inputs may be any that keep to these rules, and one draw needn't show every extreme that they name: `segments`: each aligned window of 128 positions of a micro-batch holds one sequence of 128 positions, two of 64, or one of 64 followed by 64 padding positions; padding positions carry the segment of the sequence before them. Segments are equal exactly within one sequence and its padding, and differ between windows. 0 exactly at the padding positions described for segments.
All inputs are finite; a program needn't handle non-finite values.
Results may differ from the reference program's by a relative error of at most 0.014.
The reference program's roundings to bfloat16 on the way count: a program that leaves them out, or rounds other values in their place, can miss the bound.
Values may be sent and summed in bfloat16 or wider, within the bound.
A program may use at most 192 MiB of HBM per device.

```python
import math
import jax
import jax.numpy as jnp
from jax import lax

D = 768
HEADS = 12
HD = 64
FF = 3072
WIN = 128
MB = 4
TOKENS = 8192


def window_layout(key):
    window_count = TOKENS // WIN
    window_kind = jax.random.randint(jax.random.fold_in(key, 11), (MB, window_count), 0, 3)
    window_kind = window_kind.at[0, window_count - 1].set(1)
    position = jnp.arange(WIN)
    upper_half = (position >= WIN // 2)[None, None, :]
    first_id = (2 * jnp.arange(window_count))[None, :, None]
    second_sequence = (window_kind == 1)[:, :, None] & upper_half
    padded = (window_kind == 2)[:, :, None] & upper_half
    segment_number = (first_id + second_sequence.astype(jnp.int32)).reshape(MB, TOKENS)
    live_rows = (1 - padded.astype(jnp.int32)).reshape(MB, TOKENS)
    return (segment_number, live_rows)


def draw_segments(key, part):
    return window_layout(key)[0].astype(jnp.int32)


def draw_padding(key, part):
    return window_layout(key)[1].astype(jnp.int32)


def block_levels(key, dims, cuts, smallest, top_value):
    level = 1.0
    for axis_at, parts in cuts:
        steps = jax.random.uniform(jax.random.fold_in(jax.random.fold_in(key, 6), axis_at), (parts,), jnp.float32, smallest / len(cuts), top_value / len(cuts))
        level = level * jnp.repeat(jnp.exp(steps), dims[axis_at] // parts).reshape((-1,) + (1,) * (len(dims) - 1 - axis_at))
    return level


def bell_draw(key, extent, width, bound, cuts=(), kind=jnp.bfloat16):
    loudness = block_levels(key, extent, cuts, -0.22, 0.18) if cuts else 1.0
    entries = jax.random.normal(key, extent, jnp.float32) * width * loudness
    return jnp.minimum(jnp.maximum(entries, -bound), bound).astype(kind)


def setup_inputs(seed: int = 0) -> dict:
    key_of = jax.random.split(jax.random.key(seed), 20)
    inputs = bell_draw(key_of[0], (MB, TOKENS, D), 1.0, 6.0, ((1, 32),))
    segments = draw_segments(jax.random.fold_in(key_of[19], 71), 0)
    padding = draw_padding(jax.random.fold_in(key_of[19], 71), 0)
    query_weight = bell_draw(key_of[3], (D, D), D ** -0.5, 0.21875, ((1, 2),))
    query_bias = bell_draw(key_of[4], (D,), 0.5, 3.0, ((0, 2),))
    key_weight = bell_draw(key_of[5], (D, D), D ** -0.5, 0.21875, ((1, 2),))
    value_weight = bell_draw(key_of[6], (D, D), D ** -0.5, 0.21875, ((1, 2),))
    value_bias = bell_draw(key_of[7], (D,), 0.5, 3.0, ((0, 2),))
    output_weight = bell_draw(key_of[8], (D, D), (D // 16) ** -0.5, 0.875, ((0, 2),))
    output_bias = bell_draw(key_of[9], (D,), 0.3, 1.75)
    first_gain = jnp.clip(1.0 + 0.15 * jax.random.normal(key_of[10], (D,), jnp.float32), 0.25, 1.75).astype(jnp.bfloat16)
    first_shift = bell_draw(key_of[11], (D,), 0.3, 1.75)
    expand_weight = bell_draw(key_of[12], (D, FF), D ** -0.5, 0.21875, ((1, 2),))
    expand_bias = bell_draw(key_of[13], (FF,), 0.5, 3.0, ((0, 2),))
    reduce_weight = bell_draw(key_of[14], (FF, D), FF ** -0.5, 0.109375, ((0, 2),))
    reduce_bias = bell_draw(key_of[15], (D,), 0.3, 1.75)
    second_gain = jnp.clip(1.0 + 0.15 * jax.random.normal(key_of[16], (D,), jnp.float32), 0.25, 1.75).astype(jnp.bfloat16)
    second_shift = bell_draw(key_of[17], (D,), 0.3, 1.75)
    cotangent = bell_draw(key_of[18], (MB, TOKENS, D), 1.0, 6.0, ((1, 32),))
    return dict(inputs=inputs, segments=segments, padding=padding, query_weight=query_weight, query_bias=query_bias, key_weight=key_weight, value_weight=value_weight, value_bias=value_bias, output_weight=output_weight, output_bias=output_bias, first_gain=first_gain, first_shift=first_shift, expand_weight=expand_weight, expand_bias=expand_bias, reduce_weight=reduce_weight, reduce_bias=reduce_bias, second_gain=second_gain, second_shift=second_shift, cotangent=cotangent)


@jax.custom_vjp
def low(v):
    return lax.optimization_barrier(v.astype(jnp.bfloat16)).astype(jnp.float32)

@jax.custom_vjp
def low_back(v):
    return v

def low_keep(v):
    return (low(v), None)

def low_pass(kept, grad):
    return (grad,)

def back_keep(v):
    return (v, None)

def back_low(kept, grad):
    return (low(grad),)
low.defvjp(low_keep, low_pass)
low_back.defvjp(back_keep, back_low)
norm_epsilon = 1e-12

def matmul(left, right):
    return jnp.dot(left, right, precision=lax.Precision.HIGHEST, preferred_element_type=jnp.float32)

def layer_norm(hidden, gain, shift):
    center = hidden - lax.optimization_barrier(jnp.mean(hidden, axis=-1, keepdims=True))
    variance = lax.optimization_barrier(jnp.mean(center * center, axis=-1, keepdims=True))
    return center * lax.rsqrt(variance + norm_epsilon) * gain + shift

def block(params, hidden, segment_rows, padding_rows):
    query_weight, query_bias, key_weight, value_weight, value_bias, output_weight, output_bias, first_gain, first_shift, expand_weight, expand_bias, reduce_weight, reduce_bias, second_gain, second_shift = params
    total = hidden.shape[0]
    windows = total // WIN
    queries = low_back(low(matmul(hidden, query_weight) + query_bias)).reshape(windows, WIN, HEADS, HD)
    key_rows = low_back(low(matmul(hidden, key_weight))).reshape(windows, WIN, HEADS, HD)
    values = low_back(low(matmul(hidden, value_weight) + value_bias)).reshape(windows, WIN, HEADS, HD)
    raw = jnp.einsum('wqhd,wkhd->whqk', queries, key_rows, precision=lax.Precision.HIGHEST) * HD ** (-0.5)
    scores = low_back(raw)
    seg_window = segment_rows.reshape(windows, WIN)
    pad_window = padding_rows.reshape(windows, WIN)
    allowed = (seg_window[:, :, None] == seg_window[:, None, :]) & (pad_window[:, None, :] > 0)
    scores = jnp.where(allowed[:, None, :, :], scores, -1e+30)
    probs = low(jax.nn.softmax(scores, axis=-1))
    mixed = jnp.einsum('whqk,wkhd->wqhd', probs, values, precision=lax.Precision.HIGHEST).reshape(total, D)
    mixed = low_back(low(mixed))
    attended = low_back(matmul(mixed, output_weight))
    first = layer_norm(hidden + attended + output_bias, first_gain, first_shift)
    inner = low_back(matmul(low(first), expand_weight) + expand_bias)
    activated = low(jax.nn.gelu(inner, approximate=False))
    reduced = low_back(matmul(activated, reduce_weight))
    return layer_norm(first + reduced + reduce_bias, second_gain, second_shift)

def reference(inputs, segments, padding, query_weight, query_bias, key_weight, value_weight, value_bias, output_weight, output_bias, first_gain, first_shift, expand_weight, expand_bias, reduce_weight, reduce_bias, second_gain, second_shift, cotangent):
    params = tuple((member.astype(jnp.float32) for member in (query_weight, query_bias, key_weight, value_weight, value_bias, output_weight, output_bias, first_gain, first_shift, expand_weight, expand_bias, reduce_weight, reduce_bias, second_gain, second_shift)))
    total_rows = MB * TOKENS
    group_rows = math.gcd(total_rows, 4096)
    hidden = inputs.reshape(total_rows, D).astype(jnp.float32)
    segment_rows = segments.reshape(total_rows // group_rows, group_rows).astype(jnp.int32)
    padding_rows = padding.reshape(total_rows // group_rows, group_rows).astype(jnp.int32)
    stepper = jax.checkpoint(block)

    def forward(weights, rows_in):

        def advance(carried, pieces):
            return (carried, stepper(weights, pieces[0], pieces[1], pieces[2]))
        unused, outputs = lax.scan(advance, jnp.zeros((), jnp.float32), (rows_in.reshape(total_rows // group_rows, group_rows, D), segment_rows, padding_rows))
        return outputs.reshape(total_rows, D)
    result, pullback = jax.vjp(forward, params, hidden)
    weight_grads, input_grads = pullback(cotangent.reshape(total_rows, D).astype(jnp.float32))
    return (result.reshape(MB, TOKENS, D), input_grads.reshape(MB, TOKENS, D), weight_grads[0], weight_grads[1], weight_grads[2], weight_grads[3], weight_grads[4], weight_grads[5], weight_grads[6], weight_grads[7], weight_grads[8], weight_grads[9], weight_grads[10], weight_grads[11], weight_grads[12], weight_grads[13], weight_grads[14])
```

```python
import functools

import jax
import jax.numpy as jnp
from jax import lax
from jax.experimental import pallas as pl
from jax.experimental.pallas import tpu as pltpu
from jax.sharding import PartitionSpec as P

WIN = 128
BLOCKS = 4
ROWS = 256
TOTAL = BLOCKS * ROWS
WIDTH = 768
HALF = 384
HIDDEN = 1536
CHUNKS = 12
EPS = 1e-12
BF = jnp.bfloat16
F32 = jnp.float32
MESH = pl.DeviceIdType.MESH


def mm(a, b):
    return lax.dot_general(a, b, (((1,), (0,)), ((), ())), preferred_element_type=F32)


def mm_nt(a, b):
    return lax.dot_general(a, b, (((1,), (1,)), ((), ())), preferred_element_type=F32)


def mm_tn(a, b):
    return lax.dot_general(a, b, (((0,), (0,)), ((), ())), preferred_element_type=F32)


def row_mean(a):
    return jnp.sum(a, axis=-1, keepdims=True) * (1.0 / WIDTH)


def col_sum(a):
    return jnp.sum(a, axis=0, keepdims=True)


def kernel(
    bits,
    x_ref, cot_hbm, seg_ref, pad_ref, own_ref, rep_ref, wq_hbm, wk_hbm, wv_hbm, wo_hbm, w1_hbm, w2_hbm,
    out_hbm, gin_hbm, grad_hbm, vec_out,
    wqkv, wo, w1, w2, hv, A, probs, normed, spread, acc, FL, FLT, GT, bias, stage, cot, sums, got, hsum,
    R0, R1, R2, R3, R4, RX,
    lsem, osem, fsem, wsend, wrecv, gsend, grecv, vsend, vrecv, psem,
):
    t = lax.axis_index("tensor")
    me = lax.axis_index("dp")
    bit = [lax.rem(me // (1 << i), 2) for i in range(bits)]
    split = min(bits, 4)

    def mate(i):
        return (me + (1 << i) * (1 - 2 * bit[i]), t)

    across = (me, 1 - t)
    partners = [across] + [mate(i) for i in range(bits)]

    barrier = pltpu.get_barrier_semaphore()
    for who in partners:
        pl.semaphore_signal(barrier, inc=1, device_id=who, device_id_type=MESH)

    locals_ = [
        (wq_hbm, wqkv.at[t, :, pl.ds(0, HALF)]),
        (wk_hbm, wqkv.at[t, :, pl.ds(HALF, HALF)]),
        (wv_hbm, wqkv.at[t, :, pl.ds(2 * HALF, HALF)]),
        (wo_hbm, wo.at[t]),
        (w1_hbm, w1.at[t]),
        (w2_hbm, w2.at[t]),
    ]
    loads = [pltpu.make_async_copy(s, d, lsem.at[i]) for i, (s, d) in enumerate(locals_)]
    for cp in loads:
        cp.start()
    hv[t] = own_ref[...]
    pl.semaphore_wait(barrier, len(partners))

    quarter = 2 * bit[1] + bit[0]
    far = 2 * (1 - bit[1]) + bit[0]

    def rows_at(q, n, s, parts):
        return pl.ds(pl.multiple_of(q * n + s * (n // parts), 32), n // parts)

    pieces = [
        (wq_hbm, lambda sl, r: wqkv.at[sl, r, pl.ds(0, HALF)], 192, 0, 1),
        (wk_hbm, lambda sl, r: wqkv.at[sl, r, pl.ds(HALF, HALF)], 192, 0, 1),
        (wv_hbm, lambda sl, r: wqkv.at[sl, r, pl.ds(2 * HALF, HALF)], 192, 0, 1),
        (wo_hbm, lambda sl, r: wo.at[sl, r, :], 96, 0, 1),
        (w1_hbm, lambda sl, r: w1.at[sl, r, :], 192, 0, 2),
        (w1_hbm, lambda sl, r: w1.at[sl, r, :], 192, 1, 2),
        (w2_hbm, lambda sl, r: w2.at[sl, r, :], 384, 0, 2),
        (w2_hbm, lambda sl, r: w2.at[sl, r, :], 384, 1, 2),
    ]

    def weight_copy(step, g):
        hbm, place, n, s, parts = pieces[g]
        if step == 0:
            r = rows_at(quarter, n, s, parts)
            src, dst, who = hbm.at[r, :], place(t, r), across
        else:
            r = rows_at(far if step == 3 else quarter, n, s, parts)
            src = dst = place(1 - t, r)
            who = mate(1) if step == 1 else mate(0)
        return pltpu.make_async_remote_copy(
            src_ref=src, dst_ref=dst, send_sem=wsend.at[step, g], recv_sem=wrecv.at[step, g],
            device_id=who, device_id_type=MESH,
        )

    bias_copy = pltpu.make_async_remote_copy(
        src_ref=own_ref, dst_ref=hv.at[t], send_sem=wsend.at[4, 0], recv_sem=wrecv.at[4, 0],
        device_id=across, device_id_type=MESH,
    )
    bias_copy.start()
    for g in range(len(pieces)):
        weight_copy(0, g).start()

    def forward(g):
        weight_copy(0, g).wait()
        weight_copy(1, g).start()
        weight_copy(2, g).start()

    def relay(g):
        weight_copy(1, g).wait()
        weight_copy(3, g).start()

    def ready(g):
        weight_copy(2, g).wait()
        weight_copy(3, g).wait()

    sums[0] = jnp.zeros((24, HALF), F32)
    hsum[...] = jnp.zeros_like(hsum)
    lane = lax.broadcasted_iota(jnp.int32, (1, 128), 1)
    low = lane < 64
    mask0 = jnp.where(low, 1.0, 0.0).astype(BF)
    mask1 = jnp.where(low, 0.0, 1.0).astype(BF)
    sc0 = jnp.where(low, 0.125, 0.0).astype(BF)
    sc1 = jnp.where(low, 0.0, 0.125).astype(BF)

    for b in range(BLOCKS):
        for wi in range(2):
            cols = pl.ds(pl.multiple_of(t * ROWS + wi * WIN, WIN), WIN)
            seg = jnp.broadcast_to(seg_ref[b : b + 1, cols].astype(F32), (WIN, WIN))
            live = jnp.broadcast_to(pad_ref[b : b + 1, cols].astype(F32), (WIN, WIN))
            bias[2 * b + wi] = jnp.where((seg == seg.T) & (live > 0.5), 0.0, -1e30)

    def stacked(a, m0, m1):
        return jnp.concatenate([a * m0, a * m1], axis=0)

    def at(loop_index, step, action):
        @pl.when(loop_index == step)
        def _():
            action()

    def block_rows(b):
        return pl.ds(pl.multiple_of(b * ROWS, ROWS), ROWS)

    for cp in loads[:3]:
        cp.wait()

    def attend(i, carry):
        b = lax.rem(i, BLOCKS)
        h = t + (i // BLOCKS) * (1 - 2 * t)
        rows = block_rows(b)
        pr = mm(x_ref[b], wqkv[h])
        q = (pr[:, :HALF] + hv[h, 1:2, 0:HALF]).astype(BF)
        k = pr[:, HALF : 2 * HALF].astype(BF)
        v = (pr[:, 2 * HALF :] + hv[h, 1:2, HALF : 2 * HALF]).astype(BF)
        A[9, h, rows, :] = q
        A[10, h, rows, :] = k
        A[11, h, rows, :] = v
        for wi in range(2):
            r = slice(wi * WIN, (wi + 1) * WIN)
            bb = bias[b * 2 + wi]
            bb = jnp.concatenate([bb, bb], axis=0)
            for p in range(3):
                c = slice(p * 128, (p + 1) * 128)
                s = mm_nt(stacked(q[r, c], sc0, sc1), k[r, c]) + bb
                e = jnp.exp(s - jnp.max(s, axis=-1, keepdims=True))
                pb = (e * (1.0 / jnp.sum(e, axis=-1, keepdims=True))).astype(BF)
                probs[b * 2 + wi, h, p] = pb
                o = mm(pb, v[r, c])
                o = jnp.where(low, o[:WIN], o[WIN:])
                A[8, h, pl.ds(pl.multiple_of(b * ROWS + wi * WIN, WIN), WIN), c] = o.astype(BF)

        def between():
            forward(2)
            relay(0)
            relay(1)
            forward(3)
            relay(2)
            bias_copy.wait()
            for g in range(3):
                ready(g)

        at(i, 1, lambda: forward(0))
        at(i, 2, lambda: forward(1))
        at(i, 3, between)
        at(i, 4, lambda: relay(3))
        at(i, 6, lambda: forward(4))
        return carry

    lax.fori_loop(0, 2 * BLOCKS, attend, 0)

    def joined(k, rows):
        return jnp.concatenate([A[k, 0, rows, :], A[k, 1, rows, :]], axis=1)

    def normalize(hidden):
        center = hidden - row_mean(hidden)
        rs = lax.rsqrt(row_mean(center * center) + EPS)
        return center * rs, rs

    def add_vec(row, value):
        sums[0, row : row + 1, :] += value[:, :HALF]
        sums[0, row + 1 : row + 2, :] += value[:, HALF:]

    out_b, gain1, shift1 = rep_ref[0:1, :], rep_ref[1:2, :], rep_ref[2:3, :]
    red_b, gain2, shift2 = rep_ref[3:4, :], rep_ref[4:5, :], rep_ref[5:6, :]

    loads[3].wait()
    ready(3)

    def first_norm(b, carry):
        rows = block_rows(b)
        mixed = joined(8, rows)
        att = mm(mixed[:, :HALF], wo[0]) + mm(mixed[:, HALF:], wo[1])
        n, rs = normalize(x_ref[b].astype(F32) + att + out_b)
        normed[rows, :] = n
        spread[rows, :] = rs
        first = n * gain1 + shift1
        FL[rows, :] = first.astype(BF)
        at(b, 1, lambda: forward(5))
        at(b, 3, lambda: relay(4))
        return carry

    lax.fori_loop(0, BLOCKS, first_norm, 0)
    loads[4].wait()

    def expand(i, carry):
        b = lax.rem(i, BLOCKS)
        h = t + (i // BLOCKS) * (1 - 2 * t)
        rows = block_rows(b)
        inner_all = mm(FL[rows, :], w1[h]) + hv[h, 0:1, :]
        for k in range(4):
            inner = inner_all[:, k * HALF : (k + 1) * HALF]
            phi = 0.5 + 0.5 * lax.erf(inner * 0.7071067811865476)
            slope = phi + inner * jnp.exp(-0.5 * inner * inner) * 0.3989422804014327
            A[k, h, rows, :] = (inner * phi).astype(BF)
            A[4 + k, h, rows, :] = slope.astype(BF)

        def between():
            relay(5)
            ready(4)
            ready(5)

        at(i, 2, lambda: forward(6))
        at(i, 3, between)
        at(i, 6, lambda: forward(7))
        at(i, 7, lambda: relay(6))
        return carry

    lax.fori_loop(0, 2 * BLOCKS, expand, 0)
    loads[5].wait()

    def reduce_half(b, h):
        rows = block_rows(b)
        return mm(jnp.concatenate([A[k, h, rows, :] for k in range(4)], axis=1), w2[h])

    def reduce_own(b, carry):
        acc[block_rows(b), :] = reduce_half(b, t)
        return carry

    def cot_copy(b):
        return pltpu.make_async_copy(cot_hbm.at[b], cot.at[lax.rem(b, 2)], psem.at[lax.rem(b, 2)])

    cot_copy(0).start()
    cot_copy(1).start()
    lax.fori_loop(0, BLOCKS, reduce_own, 0)
    relay(7)
    ready(6)
    ready(7)

    def second_norm(b, carry):
        rows = block_rows(b)
        red = acc[rows, :] + reduce_half(b, 1 - t)
        n, rs = normalize(normed[rows, :] * gain1 + shift1 + red + red_b)
        slot = lax.rem(b, 2)

        @pl.when(b >= 2)
        def _():
            pltpu.make_async_copy(stage.at[slot], out_hbm.at[b - 2], osem.at[slot]).wait()

        stage[slot] = n * gain2 + shift2
        pltpu.make_async_copy(stage.at[slot], out_hbm.at[b], osem.at[slot]).start()
        cot_copy(b).wait()
        c = cot[slot].astype(F32)

        @pl.when(b + 2 < BLOCKS)
        def _():
            cot_copy(b + 2).start()

        add_vec(14, col_sum(c))
        add_vec(12, col_sum(c * n))
        u = c * gain2
        gs = rs * (u - row_mean(u) - n * row_mean(u * n))
        add_vec(10, col_sum(gs))
        acc[rows, :] = gs
        return carry

    lax.fori_loop(0, BLOCKS, second_norm, 0)
    for b in range(2):
        pltpu.make_async_copy(stage.at[b], out_hbm.at[b + 2], osem.at[b]).wait()

    def span(i):
        return WIDTH >> (i + 1)

    def own_lo(i):
        return sum((bit[j] * span(j) for j in range(i + 1)), 0)

    def ds(lo, n):
        return pl.ds(pl.multiple_of(lo, 16), n)

    halving = [R2, R3, R4][: split - 1]
    extra = bits - split
    names = [("core", 0), ("tensor", 0)] + [("half", i) for i in range(1, split)]
    names += [("swap", i) for i in range(extra)] + [("gather", i) for i in reversed(range(split))]

    def piece_copy(k, s):
        kind, i = names[s]
        if kind == "core":
            src, dst, who = A.at[k, :, ds((1 - bit[0]) * span(0), span(0)), :], R0.at[k % 4], mate(0)
        elif kind == "tensor":
            src, dst, who = A.at[k, 1 - t, ds(own_lo(0), span(0)), :], R1.at[k], across
        elif kind == "half":
            src = A.at[k, t, ds(own_lo(i - 1) + (1 - bit[i]) * span(i), span(i)), :]
            dst, who = halving[i - 1].at[k], mate(i)
        elif kind == "swap":
            src, dst, who = A.at[k, t, ds(own_lo(split - 1), span(split - 1)), :], RX.at[i, k], mate(split + i)
        else:
            r = ds(own_lo(i), span(i))
            src = A.at[k, t, r, :] if i == split - 1 else grad_hbm.at[k, r, :]
            dst, who = grad_hbm.at[k, r, :], mate(i)
        return pltpu.make_async_remote_copy(
            src_ref=src, dst_ref=dst, send_sem=gsend.at[s, k], recv_sem=grecv.at[s, k],
            device_id=who, device_id_type=MESH,
        )

    def keep_copy(k):
        r = ds(own_lo(split - 1), span(split - 1))
        return pltpu.make_async_copy(A.at[k, t, r, :], grad_hbm.at[k, r, :], fsem.at[k])

    def settle(k, s):
        piece_copy(k, s).wait()
        kind, i = names[s]
        if kind == "core":
            r = ds(own_lo(0), span(0))
            A[k, :, r, :] = A[k, :, r, :] + R0[k % 4]
        elif kind == "tensor":
            r = ds(own_lo(0), span(0))
            A[k, t, r, :] = A[k, t, r, :] + R1[k]
        elif kind == "half":
            r = ds(own_lo(i), span(i))
            A[k, t, r, :] = A[k, t, r, :] + halving[i - 1][k]
        elif kind == "swap":
            r = ds(own_lo(split - 1), span(split - 1))
            A[k, t, r, :] = A[k, t, r, :] + RX[i, k]
        elif i == split - 1:
            keep_copy(k).wait()
        if s + 1 < len(names) and names[s + 1] == ("gather", split - 1):
            keep_copy(k).start()

    place = [0] * CHUNKS

    def adv(*which):
        for k in which:
            s = place[k]
            if s > len(names):
                continue
            if s > 0:
                settle(k, s - 1)
            if s < len(names):
                piece_copy(k, s).start()
            place[k] = s + 1

    swaps = [across] + [mate(i) for i in range(bits)]
    vec_place = [0]

    def adv_vec():
        s = vec_place[0]

        def cp(j):
            return pltpu.make_async_remote_copy(
                src_ref=sums.at[j], dst_ref=got.at[j], send_sem=vsend.at[j], recv_sem=vrecv.at[j],
                device_id=swaps[j], device_id_type=MESH,
            )

        if s > len(swaps):
            return
        if s > 0:
            cp(s - 1).wait()
            sums[s] = sums[s - 1] + got[s - 1]
        if s < len(swaps):
            cp(s).start()
        vec_place[0] = s + 1

    def transpose_into(dst, get):
        for b in range(BLOCKS):
            dst[:, b * ROWS : (b + 1) * ROWS] = get(b).T

    def rows_of(b):
        return slice(b * ROWS, (b + 1) * ROWS)

    def chunk_grad(k, left):
        full = mm(left[...], joined(k, slice(None)))
        A[k, 0, 0:WIDTH, :] = full[:, :HALF].astype(BF)
        A[k, 1, 0:WIDTH, :] = full[:, HALF:].astype(BF)

    def chunk_loop(first, count, left, hooks):
        def one(j, carry):
            chunk_grad(first + j, left)
            for i, which in enumerate(hooks):
                at(j, i, lambda which=which: adv(*which))
            return carry

        lax.fori_loop(0, count, one, 0)

    transpose_into(GT, lambda b: acc[rows_of(b), :].astype(BF))
    chunk_loop(0, 4, GT, [(0,), (1, 0), (2, 1), (3, 2)])
    transpose_into(FLT, lambda b: FL[rows_of(b), :])
    adv(3)

    def feed_back(b, carry):
        rows = block_rows(b)
        gs = acc[rows, :]
        gl = gs.astype(BF)
        gf = gs
        for h in range(2):
            da = mm_nt(gl, w2[h])
            gis = []
            for k in range(4):
                gi = (da[:, k * HALF : (k + 1) * HALF] * A[4 + k, h, rows, :].astype(F32)).astype(BF)
                A[4 + k, h, rows, :] = gi
                sums[0, 16 + 4 * h + k : 17 + 4 * h + k, :] += col_sum(gi.astype(F32))
                gis.append(gi)
            gf = gf + mm_nt(jnp.concatenate(gis, axis=1), w1[h])
        n = normed[rows, :]
        add_vec(6, col_sum(gf * n))
        add_vec(8, col_sum(gf))
        u = gf * gain1
        gh = spread[rows, :] * (u - row_mean(u) - n * row_mean(u * n))
        add_vec(4, col_sum(gh))
        acc[rows, :] = gh
        gm = gh.astype(BF)
        FL[rows, 0:HALF] = mm_nt(gm, wo[0]).astype(BF)
        FL[rows, HALF:] = mm_nt(gm, wo[1]).astype(BF)
        at(b, 1, lambda: adv(0))
        at(b, 3, lambda: adv(0, 1))
        return carry

    lax.fori_loop(0, BLOCKS, feed_back, 0)
    chunk_loop(4, 4, FLT, [(4,), (5, 4), (0, 1, 6, 5), (0, 2, 7, 6)])
    transpose_into(GT, lambda b: acc[rows_of(b), :].astype(BF))
    adv(7)
    chunk_grad(8, GT)
    adv(8, 0, 1, 2)
    transpose_into(FLT, lambda b: x_ref[b])
    adv(8)

    def attend_back(i, carry):
        h, w = i // (2 * BLOCKS), lax.rem(i, 2 * BLOCKS)
        rows = pl.ds(pl.multiple_of(w * WIN, WIN), WIN)
        for p in range(3):
            c = slice(p * 128, (p + 1) * 128)
            q, k, v = A[9, h, rows, c], A[10, h, rows, c], A[11, h, rows, c]
            do = FL[rows, pl.ds(pl.multiple_of(h * HALF + p * 128, 128), 128)]
            pb = probs[w, h, p]
            do2 = stacked(do, mask0, mask1)
            dv = mm_tn(pb, do2).astype(BF)
            dp = mm_nt(do2, v)
            pf = pb.astype(F32)
            dsc = (pf * (dp - jnp.sum(pf * dp, axis=-1, keepdims=True))).astype(BF)
            dq = mm(dsc, k)
            dq = (jnp.where(low, dq[:WIN], dq[WIN:]) * 0.125).astype(BF)
            dk = mm_tn(dsc, stacked(q, sc0, sc1)).astype(BF)
            A[9, h, rows, c] = dq
            A[10, h, rows, c] = dk
            A[11, h, rows, c] = dv
            hsum[h, 0:1, c] += col_sum(dq.astype(F32))
            hsum[h, 1:2, c] += col_sum(dv.astype(F32))
        for step, which in (
            (1, (0, 3)), (3, (0, 1, 2)), (5, (3, 0, 1)), (7, (4, 2, 1)), (9, (0, 3, 1, 2)), (11, (4, 3, 2)), (13, (5, 1, 2, 3, 4)),
        ):
            at(i, step, lambda which=which: adv(*which))
        return carry

    lax.fori_loop(0, 4 * BLOCKS, attend_back, 0)
    for h in range(2):
        sums[0, h : h + 1, :] = hsum[h, 0:1, :]
        sums[0, 2 + h : 3 + h, :] = hsum[h, 1:2, :]
    adv_vec()

    def input_grad(b, carry):
        rows = block_rows(b)
        g = acc[rows, :]
        for h in range(2):
            gp = jnp.concatenate([A[9 + i, h, rows, :] for i in range(3)], axis=1)
            g = g + mm_nt(gp, wqkv[h])
        slot = lax.rem(b, 2)

        @pl.when(b >= 2)
        def _():
            pltpu.make_async_copy(stage.at[slot], gin_hbm.at[b - 2], osem.at[slot]).wait()

        stage[slot] = g
        pltpu.make_async_copy(stage.at[slot], gin_hbm.at[b], osem.at[slot]).start()
        at(b, 1, lambda: adv(2, 3, 4, 5))
        at(b, 3, lambda: adv(6, 3, 4, 5))
        return carry

    lax.fori_loop(0, BLOCKS, input_grad, 0)
    adv_vec()
    chunk_loop(9, 3, FLT, [(9,), (10, 9), (11, 10)])
    adv(11)
    adv_vec()
    for b in range(2):
        pltpu.make_async_copy(stage.at[b], gin_hbm.at[b + 2], osem.at[b]).wait()
    while min(place) <= len(names):
        adv_vec()
        adv(*[k for k in range(CHUNKS) if place[k] <= len(names)])
    while vec_place[0] <= len(swaps):
        adv_vec()
    vec_out[...] = sums[len(swaps)]


def layer(n_dp, x, cot, seg, pad, own, rep, wq, wk, wv, wo, w1, w2):
    vm = pl.BlockSpec(memory_space=pltpu.VMEM)
    hbm = pl.BlockSpec(memory_space=pl.ANY)
    bits = n_dp.bit_length() - 1
    split = min(bits, 4)
    stages = 1 + bits + split
    dma = pltpu.SemaphoreType.DMA
    return pl.pallas_call(
        functools.partial(kernel, bits),
        out_shape=(
            jax.ShapeDtypeStruct((BLOCKS, ROWS, WIDTH), F32),
            jax.ShapeDtypeStruct((BLOCKS, ROWS, WIDTH), F32),
            jax.ShapeDtypeStruct((CHUNKS, WIDTH, HALF), BF),
            jax.ShapeDtypeStruct((24, HALF), F32),
        ),
        in_specs=[vm, hbm] + [vm] * 4 + [hbm] * 6,
        out_specs=(hbm, hbm, hbm, vm),
        scratch_shapes=[
            pltpu.VMEM((2, WIDTH, 3 * HALF), BF),
            pltpu.VMEM((2, HALF, WIDTH), BF),
            pltpu.VMEM((2, WIDTH, HIDDEN), BF),
            pltpu.VMEM((2, HIDDEN, WIDTH), BF),
            pltpu.VMEM((2, 8, HIDDEN), F32),
            pltpu.VMEM((CHUNKS, 2, TOTAL, HALF), BF),
            pltpu.VMEM((2 * BLOCKS, 2, 3, 2 * WIN, WIN), BF),
            pltpu.VMEM((TOTAL, WIDTH), F32),
            pltpu.VMEM((TOTAL, 1), F32),
            pltpu.VMEM((TOTAL, WIDTH), F32),
            pltpu.VMEM((TOTAL, WIDTH), BF),
            pltpu.VMEM((WIDTH, TOTAL), BF),
            pltpu.VMEM((WIDTH, TOTAL), BF),
            pltpu.VMEM((2 * BLOCKS, WIN, WIN), F32),
            pltpu.VMEM((2, ROWS, WIDTH), F32),
            pltpu.VMEM((2, ROWS, WIDTH), BF),
            pltpu.VMEM((bits + 2, 24, HALF), F32),
            pltpu.VMEM((bits + 1, 24, HALF), F32),
            pltpu.VMEM((2, 8, HALF), F32),
            pltpu.VMEM((4, 2, WIDTH // 2, HALF), BF),
            pltpu.VMEM((CHUNKS, WIDTH // 2, HALF), BF),
            pltpu.VMEM((CHUNKS, WIDTH // 4, HALF), BF),
            pltpu.VMEM((CHUNKS, WIDTH // 8, HALF), BF),
            pltpu.VMEM((CHUNKS, WIDTH // 16, HALF), BF),
            pltpu.VMEM((max(bits - split, 1), CHUNKS, WIDTH >> split, HALF), BF),
            dma((6,)),
            dma((2,)),
            dma((CHUNKS,)),
            dma((5, 8)),
            dma((5, 8)),
            dma((stages, CHUNKS)),
            dma((stages, CHUNKS)),
            dma((bits + 1,)),
            dma((bits + 1,)),
            dma((2,)),
        ],
        compiler_params=pltpu.CompilerParams(
            vmem_limit_bytes=67043328, collective_id=0, has_side_effects=True
        ),
    )(x, cot, seg, pad, own, rep, wq, wk, wv, wo, w1, w2)


def local(
    n_dp, inputs, segments, padding, query_weight, query_bias, key_weight, value_weight, value_bias,
    output_weight, output_bias, first_gain, first_shift, expand_weight, expand_bias,
    reduce_weight, reduce_bias, second_gain, second_shift, cotangent,
):
    small = jnp.concatenate((query_bias, value_bias, jnp.zeros((HIDDEN - 2 * HALF,), BF))).astype(F32)
    own = jnp.stack([expand_bias.astype(F32), small] + [jnp.zeros((HIDDEN,), F32)] * 6)
    rep = jnp.stack(
        [v.astype(F32) for v in (output_bias, first_gain, first_shift, reduce_bias, second_gain, second_shift)]
        + [jnp.zeros((WIDTH,), F32)] * 2
    )
    out, gin, grads, vec = layer(
        n_dp, inputs, cotangent, segments, padding, own, rep, query_weight, key_weight, value_weight,
        output_weight, expand_weight, reduce_weight,
    )
    grads = grads.astype(F32)
    t = lax.axis_index("tensor")
    half = lambda r: lax.dynamic_slice(vec, (r + t, 0), (1, HALF)).reshape(HALF)
    whole = lambda r: vec[r : r + 2].reshape(WIDTH)
    w2g = jnp.transpose(grads[0:4], (0, 2, 1)).reshape(HIDDEN, WIDTH)
    w1g = jnp.transpose(grads[4:8], (1, 0, 2)).reshape(WIDTH, HIDDEN)
    b1g = lax.dynamic_slice(vec, (16 + 4 * t, 0), (4, HALF)).reshape(HIDDEN)
    return (
        out, gin, grads[9], half(0), grads[10], grads[11], half(2), grads[8].T, whole(4),
        whole(6), whole(8), w1g, b1g, w2g, whole(10), whole(12), whole(14),
    )


def solution(mesh):
    tokens = P(None, ("dp", "tensor"), None)
    return jax.shard_map(
        functools.partial(local, mesh.shape["dp"]),
        mesh=mesh,
        in_specs=(
            tokens, P(None, "dp"), P(None, "dp"), P(None, "tensor"), P("tensor"), P(None, "tensor"),
            P(None, "tensor"), P("tensor"), P("tensor", None), P(), P(), P(), P(None, "tensor"),
            P("tensor"), P("tensor", None), P(), P(), P(), tokens,
        ),
        out_specs=(
            tokens, tokens, P(None, "tensor"), P("tensor"), P(None, "tensor"), P(None, "tensor"),
            P("tensor"), P("tensor", None), P(), P(), P(), P(None, "tensor"), P("tensor"),
            P("tensor", None), P(), P(), P(),
        ),
        check_vma=False,
    )
```

```python
import functools

import jax
import jax.numpy as jnp
from jax import lax
from jax.experimental import pallas as pl
from jax.experimental.pallas import tpu as pltpu
from jax.sharding import PartitionSpec as P

WIN = 128
BLOCKS = 4
ROWS = 256
TOTAL = BLOCKS * ROWS
WIDTH = 768
HALF = 384
HIDDEN = 1536
CHUNKS = 12
EPS = 1e-12
BF = jnp.bfloat16
F32 = jnp.float32
MESH = pl.DeviceIdType.MESH


def mm(a, b):
    return lax.dot_general(a, b, (((1,), (0,)), ((), ())), preferred_element_type=F32)


def mm_nt(a, b):
    return lax.dot_general(a, b, (((1,), (1,)), ((), ())), preferred_element_type=F32)


def mm_tn(a, b):
    return lax.dot_general(a, b, (((0,), (0,)), ((), ())), preferred_element_type=F32)


def row_mean(a):
    return jnp.sum(a, axis=-1, keepdims=True) * (1.0 / WIDTH)


def col_sum(a):
    return jnp.sum(a, axis=0, keepdims=True)

WAYS = ((2, 1, 0), (1, 2, 0), (1, 0), (2, 1, 0), (2, 1, 0), (2, 0), (1, 2, 0), (2, 1, 0), (1, 0), (2, 0), (1, 2, 0), (1, 0))
PARTS = ((0, 0, 384), (1, 0, 384), (2, 0, 384), (3, 0, 384), (4, 0, 384), (5, 0, 384), (6, 0, 384), (7, 0, 384), (8, 0, 384), (9, 0, 384), (10, 0, 384), (11, 0, 128), (11, 128, 128), (11, 256, 128))
ORDERS = ((0, 1, 2, 3), (0, 1, 2, 3), (0, 2, 1, 3), (0, 2, 1, 3), (0, 1, 2, 3), (0, 2, 3, 1), (0, 2, 3, 1), (0, 1, 2, 3), (0, 2, 1, 3), (0, 1, 2, 3), (0, 2, 1, 3), (0, 1, 2, 3), (0, 1, 2, 3), (0, 1, 2, 3))
PLAN = {
    "attend": ((2, (0,)), (3, (1, 0, 2, 1, 3, 4, 0, 1, 0, 5, 3, 1, 2, 6, 4, 2)), (4, (7,)), (6, (3, 5)), (7, (3, 6, 7, 8)),),
    "norm1": ((0, (5,)), (1, (9,)), (2, (4,)), (3, (10,)),),
    "expand": ((0, (4, 6)), (1, (7, 6, 11)), (2, (7, 9)), (3, (8, 9)), (4, (8, 10)), (6, (11,)),),
    "rown": ((0, (11,)), (1, (10,)),),
    "pre_reduce": ((0, (10,)),),
    "dw2": ((0, (20,)), (1, (21,)), (2, (20, 22)), (3, (21, 23)),),
    "back": ((0, (22, 23)), (1, (20,)), (3, (20, 21)),),
    "dw1": ((0, (24,)), (1, (25,)), (2, (24, 26, 20, 22)), (3, (25, 27, 21, 26)),),
    "dwo": ((0, (27, 28, 20)),),
    "attb": ((0, (22, 23, 28, 21)), (2, (20, 22)), (4, (21, 23, 24)), (5, (20, 22)), (7, (21, 23)), (9, (22, 24, 25)), (10, (21, 23)), (11, (20, 24)), (12, (20, 22)), (13, (23, 26, 25)), (14, (21, 24)), (15, (23, 21, 22)),),
    "dwq": ((0, (29,)), (1, (30, 22, 25, 27, 29, 26)), (2, (30, 31, 32, 33, 24, 25)),),
    "gin": ((0, (31, 32, 33, 23)), (1, (24, 25, 23, 26, 27, 28)),),
    "tail": ((0, (27, 24, 26, 25, 24, 29, 28, 26, 27, 25, 29, 25, 30, 28, 26, 29, 31, 27, 32, 28, 31, 30, 29, 33, 32, 26, 28, 30, 33, 27, 26, 29, 31, 32, 28, 33, 30, 31, 29, 32, 27, 33, 27, 28, 30, 31, 32, 28, 33, 29, 31, 30, 29, 32, 33, 31, 32, 31, 33, 32, 30, 33, 30)),),
}


def kernel(
    bits,
    x_ref, cot_hbm, seg_ref, pad_ref, qb_ref, vb_ref, eb_ref, ob_ref, g1_ref, s1_ref, rb_ref, g2_ref, s2_ref,
    wq_hbm, wk_hbm, wv_hbm, wo_hbm, w1_hbm, w2_hbm,
    out_hbm, gin_hbm, grad_hbm, vec_out,
    wqkv, wo, w1, w2, hv, A, probs, normed, spread, acc, FL, FLT, GT, bias, stage, cot, sums, got, hsum,
    R0, R1, R2, R3, R4, RX,
    lsem, osem, fsem, wsend, wrecv, gsend, grecv, vsend, vrecv, bsem, psem,
):
    t = lax.axis_index("tensor")
    me = lax.axis_index("dp")
    bit = [lax.rem(me // (1 << i), 2) for i in range(bits)]
    split = min(bits, 4)

    def mate(i):
        return (me + (1 << i) * (1 - 2 * bit[i]), t)

    across = (me, 1 - t)
    partners = [across] + [mate(i) for i in range(bits)]

    barrier = pltpu.get_barrier_semaphore()
    for who in partners:
        pl.semaphore_signal(barrier, inc=1, device_id=who, device_id_type=MESH)

    locals_ = [
        (wq_hbm, wqkv.at[t, :, pl.ds(0, HALF)]),
        (wk_hbm, wqkv.at[t, :, pl.ds(HALF, HALF)]),
        (wv_hbm, wqkv.at[t, :, pl.ds(2 * HALF, HALF)]),
        (wo_hbm, wo.at[t]),
        (w1_hbm, w1.at[t]),
        (w2_hbm, w2.at[t]),
    ]
    loads = [pltpu.make_async_copy(s, d, lsem.at[i]) for i, (s, d) in enumerate(locals_)]
    for cp in loads:
        cp.start()

    def row(ref):
        return ref[...].astype(F32).reshape(1, ref.shape[0])

    hv[t] = jnp.zeros((8, HIDDEN), F32)
    hv[t, 0:1, :] = row(eb_ref)
    hv[t, 1:2, 0:HALF] = row(qb_ref)
    hv[t, 1:2, HALF : 2 * HALF] = row(vb_ref)
    out_b, gain1, shift1 = row(ob_ref), row(g1_ref), row(s1_ref)
    red_b, gain2, shift2 = row(rb_ref), row(g2_ref), row(s2_ref)
    pl.semaphore_wait(barrier, len(partners))

    def part_rows(base, n, ways, fixed):
        size = n // (1 << len(ways))
        at_ = sum((bit[w] * (size << j) for j, w in enumerate(ways)), 0)
        free = len(ways) - fixed
        at_ = sum((bit[w] * (size << j) for j, w in enumerate(ways) if j >= free), 0)
        return pl.ds(pl.multiple_of(base + at_, 16), size << free)

    def cols(i):
        return pl.ds(i * HALF, HALF)

    every = pl.ds(0, WIDTH)
    pieces = [(src, every, wqkv, cols(i), 0, WIDTH) for i, src in enumerate((wq_hbm, wk_hbm, wv_hbm))]
    pieces = [(src, pl.ds(0, HALF), dst, c, base, n) for src, _, dst, c, base, n in pieces]
    pieces += [(wo_hbm, every, wo, every, 0, HALF)]
    pieces += [(w1_hbm, cols(i), w1, cols(i), 0, WIDTH) for i in range(4)]
    pieces += [(w2_hbm, every, w2, every, i * HALF, HALF) for i in range(4)]

    def weight_copy(g, s):
        hbm, hc, dst, dc, base, n = pieces[g]
        ways = WAYS[g]
        r = part_rows(base, n, ways, len(ways) - max(s - 1, 0))
        if s == 0:
            src, to, who = hbm.at[r, hc], dst.at[t, r, dc], across
        else:
            src = to = dst.at[1 - t, r, dc]
            who = mate(ways[s - 1])
        return pltpu.make_async_remote_copy(
            src_ref=src, dst_ref=to, send_sem=wsend.at[s, g], recv_sem=wrecv.at[s, g],
            device_id=who, device_id_type=MESH,
        )

    wplace = [0] * len(pieces)

    def adv_weight(g):
        s, last = wplace[g], len(WAYS[g])
        if s > 0:
            weight_copy(g, s - 1).wait()
        if s <= last:
            weight_copy(g, s).start()
        wplace[g] = s + 1

    def weights_ready(which):
        while min(wplace[g] - len(WAYS[g]) for g in which) < 2:
            for g in which:
                if wplace[g] < len(WAYS[g]) + 2:
                    adv_weight(g)

    bias_copy = pltpu.make_async_remote_copy(
        src_ref=hv.at[t], dst_ref=hv.at[t], send_sem=bsem.at[0], recv_sem=bsem.at[1],
        device_id=across, device_id_type=MESH,
    )
    for g in range(3):
        adv_weight(g)
    bias_copy.start()
    for g in range(3, len(pieces)):
        adv_weight(g)

    def run(ops):
        for op in ops:
            if op < 20:
                adv_weight(op)
            elif op < 40:
                adv(op - 20)
            else:
                adv_vec()

    def at(loop_index, step, action):
        @pl.when(loop_index == step)
        def _():
            action()

    def hook(name, loop_index=None):
        for step, ops in PLAN.get(name, ()):
            if loop_index is None:
                run(ops)
            else:
                at(loop_index, step, lambda ops=ops: run(ops))

    sums[0] = jnp.zeros((24, HALF), F32)
    hsum[...] = jnp.zeros_like(hsum)
    lane = lax.broadcasted_iota(jnp.int32, (1, 128), 1)
    low = lane < 64
    mask0 = jnp.where(low, 1.0, 0.0).astype(BF)
    mask1 = jnp.where(low, 0.0, 1.0).astype(BF)
    sc0 = jnp.where(low, 0.125, 0.0).astype(BF)
    sc1 = jnp.where(low, 0.0, 0.125).astype(BF)

    for b in range(BLOCKS):
        for wi in range(2):
            cols = pl.ds(pl.multiple_of(t * ROWS + wi * WIN, WIN), WIN)
            seg = jnp.broadcast_to(seg_ref[b : b + 1, cols].astype(F32), (WIN, WIN))
            live = jnp.broadcast_to(pad_ref[b : b + 1, cols].astype(F32), (WIN, WIN))
            bias[2 * b + wi] = jnp.where((seg == seg.T) & (live > 0.5), 0.0, -1e30)

    def stacked(a, m0, m1):
        return jnp.concatenate([a * m0, a * m1], axis=0)

    def block_rows(b):
        return pl.ds(pl.multiple_of(b * ROWS, ROWS), ROWS)

    for cp in loads[:3]:
        cp.wait()

    def attend(i, carry):
        b = lax.rem(i, BLOCKS)
        h = t + (i // BLOCKS) * (1 - 2 * t)
        rows = block_rows(b)
        pr = mm(x_ref[b], wqkv[h])
        q = (pr[:, :HALF] + hv[h, 1:2, 0:HALF]).astype(BF)
        k = pr[:, HALF : 2 * HALF].astype(BF)
        v = (pr[:, 2 * HALF :] + hv[h, 1:2, HALF : 2 * HALF]).astype(BF)
        A[9, h, rows, :] = q
        A[10, h, rows, :] = k
        A[11, h, rows, :] = v
        for wi in range(2):
            r = slice(wi * WIN, (wi + 1) * WIN)
            bb = bias[b * 2 + wi]
            bb = jnp.concatenate([bb, bb], axis=0)
            for p in range(3):
                c = slice(p * 128, (p + 1) * 128)
                s = mm_nt(stacked(q[r, c], sc0, sc1), k[r, c]) + bb
                e = jnp.exp(s - jnp.max(s, axis=-1, keepdims=True))
                pb = (e * (1.0 / jnp.sum(e, axis=-1, keepdims=True))).astype(BF)
                probs[b * 2 + wi, h, p] = pb
                o = mm(pb, v[r, c])
                o = jnp.where(low, o[:WIN], o[WIN:])
                A[8, h, pl.ds(pl.multiple_of(b * ROWS + wi * WIN, WIN), WIN), c] = o.astype(BF)

        hook("attend", i)
        at(i, 3, own_done)
        return carry

    def own_done():
        weights_ready([0, 1, 2])
        bias_copy.wait()

    lax.fori_loop(0, 2 * BLOCKS, attend, 0)

    def joined(k, rows):
        return jnp.concatenate([A[k, 0, rows, :], A[k, 1, rows, :]], axis=1)

    def normalize(hidden):
        center = hidden - row_mean(hidden)
        rs = lax.rsqrt(row_mean(center * center) + EPS)
        return center * rs, rs

    def add_vec(row, value):
        sums[0, row : row + 1, :] += value[:, :HALF]
        sums[0, row + 1 : row + 2, :] += value[:, HALF:]


    loads[3].wait()
    hook("pre_norm")
    weights_ready([3])

    def first_norm(b, carry):
        rows = block_rows(b)
        mixed = joined(8, rows)
        att = mm(mixed[:, :HALF], wo[0]) + mm(mixed[:, HALF:], wo[1])
        n, rs = normalize(x_ref[b].astype(F32) + att + out_b)
        normed[rows, :] = n
        spread[rows, :] = rs
        first = n * gain1 + shift1
        FL[rows, :] = first.astype(BF)
        hook("norm1", b)
        return carry

    lax.fori_loop(0, BLOCKS, first_norm, 0)
    loads[4].wait()

    def expand(i, carry):
        b = lax.rem(i, BLOCKS)
        h = t + (i // BLOCKS) * (1 - 2 * t)
        rows = block_rows(b)
        inner_all = mm(FL[rows, :], w1[h]) + hv[h, 0:1, :]
        for k in range(4):
            inner = inner_all[:, k * HALF : (k + 1) * HALF]
            phi = 0.5 + 0.5 * lax.erf(inner * 0.7071067811865476)
            slope = phi + inner * jnp.exp(-0.5 * inner * inner) * 0.3989422804014327
            A[k, h, rows, :] = (inner * phi).astype(BF)
            A[4 + k, h, rows, :] = slope.astype(BF)

        hook("expand", i)
        at(i, 3, lambda: weights_ready([4, 5, 6, 7]))
        return carry

    lax.fori_loop(0, 2 * BLOCKS, expand, 0)
    loads[5].wait()

    def reduce_half(b, h):
        rows = block_rows(b)
        return mm(jnp.concatenate([A[k, h, rows, :] for k in range(4)], axis=1), w2[h])

    def reduce_own(b, carry):
        acc[block_rows(b), :] = reduce_half(b, t)
        hook("rown", b)
        return carry

    def cot_copy(b):
        return pltpu.make_async_copy(cot_hbm.at[b], cot.at[lax.rem(b, 2)], psem.at[lax.rem(b, 2)])

    cot_copy(0).start()
    cot_copy(1).start()
    lax.fori_loop(0, BLOCKS, reduce_own, 0)
    hook("pre_reduce")
    weights_ready([8, 9, 10, 11])

    def second_norm(b, carry):
        rows = block_rows(b)
        red = acc[rows, :] + reduce_half(b, 1 - t)
        n, rs = normalize(normed[rows, :] * gain1 + shift1 + red + red_b)
        slot = lax.rem(b, 2)

        @pl.when(b >= 2)
        def _():
            pltpu.make_async_copy(stage.at[slot], out_hbm.at[b - 2], osem.at[slot]).wait()

        stage[slot] = n * gain2 + shift2
        pltpu.make_async_copy(stage.at[slot], out_hbm.at[b], osem.at[slot]).start()
        cot_copy(b).wait()
        c = cot[slot].astype(F32)

        @pl.when(b + 2 < BLOCKS)
        def _():
            cot_copy(b + 2).start()

        add_vec(14, col_sum(c))
        add_vec(12, col_sum(c * n))
        u = c * gain2
        gs = rs * (u - row_mean(u) - n * row_mean(u * n))
        add_vec(10, col_sum(gs))
        acc[rows, :] = gs
        return carry

    lax.fori_loop(0, BLOCKS, second_norm, 0)
    for b in range(2):
        pltpu.make_async_copy(stage.at[b], out_hbm.at[b + 2], osem.at[b]).wait()

    def span(i):
        return WIDTH >> (i + 1)

    def lo(j, i):
        return sum((bit[ORDERS[j][n]] * span(n) for n in range(i + 1)), 0)

    def ds(at_, n):
        return pl.ds(pl.multiple_of(at_, 16), n)

    def held(j, h, r):
        k, first, width = PARTS[j]
        if k < 9:
            return A, (k, h, r, pl.ds(first, width))
        return w1, (h, r, pl.ds((k - 9) * HALF + first, width))

    def add_in(j, h, r, value):
        ref, at_ = held(j, h, r)
        ref[at_] = ref[at_] + value

    def view(j, h, r):
        ref, at_ = held(j, h, r)
        return ref.at[at_]

    def landing(j, p):
        k, first, width = PARTS[j]
        c = pl.ds(first, width)
        if p == 0:
            return R0, (k % 4, slice(None), slice(None), c)
        return (R1, R2, R3, R4)[p - 1], (k, slice(None), c)

    names = [("core", 0), ("tensor", 0)] + [("half", i) for i in range(1, split)]
    names += [("swap", i) for i in range(bits - split)] + [("gather", i) for i in reversed(range(split))]

    def piece_copy(j, s):
        kind, i = names[s]
        way = ORDERS[j]
        k, first, width = PARTS[j]
        if kind == "core":
            src, who = view(j, slice(None), ds((1 - bit[way[0]]) * span(0), span(0))), mate(way[0])
            land, at_ = landing(j, 0)
            dst = land.at[at_]
        elif kind == "tensor":
            src, who = view(j, 1 - t, ds(lo(j, 0), span(0))), across
            land, at_ = landing(j, 1)
            dst = land.at[at_]
        elif kind == "half":
            src = view(j, t, ds(lo(j, i - 1) + (1 - bit[way[i]]) * span(i), span(i)))
            who = mate(way[i])
            land, at_ = landing(j, i + 1)
            dst = land.at[at_]
        elif kind == "swap":
            src, who = view(j, t, ds(lo(j, split - 1), span(split - 1))), mate(split + i)
            dst = RX.at[i, k, :, pl.ds(first, width)]
        else:
            r = ds(lo(j, i), span(i))
            dst, who = grad_hbm.at[k, r, pl.ds(first, width)], mate(way[i])
            src = view(j, t, r) if i == split - 1 else dst
        return pltpu.make_async_remote_copy(
            src_ref=src, dst_ref=dst, send_sem=gsend.at[s, j], recv_sem=grecv.at[s, j],
            device_id=who, device_id_type=MESH,
        )

    def keep_copy(j):
        k, first, width = PARTS[j]
        r = ds(lo(j, split - 1), span(split - 1))
        return pltpu.make_async_copy(view(j, t, r), grad_hbm.at[k, r, pl.ds(first, width)], fsem.at[j])

    def settle(j, s):
        piece_copy(j, s).wait()
        kind, i = names[s]
        k, first, width = PARTS[j]
        if kind == "core":
            land, at_ = landing(j, 0)
            add_in(j, slice(None), ds(lo(j, 0), span(0)), land[at_])
        elif kind == "tensor":
            land, at_ = landing(j, 1)
            add_in(j, t, ds(lo(j, 0), span(0)), land[at_])
        elif kind == "half":
            land, at_ = landing(j, i + 1)
            add_in(j, t, ds(lo(j, i), span(i)), land[at_])
        elif kind == "swap":
            add_in(j, t, ds(lo(j, split - 1), span(split - 1)), RX[i, k, :, pl.ds(first, width)])
        elif i == split - 1:
            keep_copy(j).wait()
        if s + 1 < len(names) and names[s + 1] == ("gather", split - 1):
            keep_copy(j).start()

    place = [0] * len(PARTS)

    def adv(*which):
        for k in which:
            s = place[k]
            if s > len(names):
                continue
            if s > 0:
                settle(k, s - 1)
            if s < len(names):
                piece_copy(k, s).start()
            place[k] = s + 1

    swaps = [across] + [mate(i) for i in range(bits)]
    vec_place = [0]

    def adv_vec():
        s = vec_place[0]

        def cp(j):
            return pltpu.make_async_remote_copy(
                src_ref=sums.at[j], dst_ref=got.at[j], send_sem=vsend.at[j], recv_sem=vrecv.at[j],
                device_id=swaps[j], device_id_type=MESH,
            )

        if s > len(swaps):
            return
        if s > 0:
            cp(s - 1).wait()
            sums[s] = sums[s - 1] + got[s - 1]
        if s < len(swaps):
            cp(s).start()
        vec_place[0] = s + 1

    def transpose_into(dst, get):
        for b in range(BLOCKS):
            dst[:, b * ROWS : (b + 1) * ROWS] = get(b).T

    def rows_of(b):
        return slice(b * ROWS, (b + 1) * ROWS)

    def chunk_loop(name, first, count, left):
        def one(j, carry):
            k = first + j
            full = mm(left[...], joined(k, slice(None)))
            for h in range(2):
                part = full[:, h * HALF : (h + 1) * HALF].astype(BF)
                if first < 9:
                    A[k, h, 0:WIDTH, :] = part
                else:
                    w1[h, :, pl.ds(pl.multiple_of(j * HALF, HALF), HALF)] = part
            hook(name, j)
            return carry

        lax.fori_loop(0, count, one, 0)

    transpose_into(GT, lambda b: acc[rows_of(b), :].astype(BF))
    chunk_loop("dw2", 0, 4, GT)
    transpose_into(FLT, lambda b: FL[rows_of(b), :])
    hook("mid")

    def feed_back(b, carry):
        rows = block_rows(b)
        gs = acc[rows, :]
        gl = gs.astype(BF)
        gf = gs
        for h in range(2):
            da = mm_nt(gl, w2[h])
            gis = []
            for k in range(4):
                gi = (da[:, k * HALF : (k + 1) * HALF] * A[4 + k, h, rows, :].astype(F32)).astype(BF)
                A[4 + k, h, rows, :] = gi
                sums[0, 16 + 4 * h + k : 17 + 4 * h + k, :] += col_sum(gi.astype(F32))
                gis.append(gi)
            gf = gf + mm_nt(jnp.concatenate(gis, axis=1), w1[h])
        n = normed[rows, :]
        add_vec(6, col_sum(gf * n))
        add_vec(8, col_sum(gf))
        u = gf * gain1
        gh = spread[rows, :] * (u - row_mean(u) - n * row_mean(u * n))
        add_vec(4, col_sum(gh))
        acc[rows, :] = gh
        gm = gh.astype(BF)
        FL[rows, 0:HALF] = mm_nt(gm, wo[0]).astype(BF)
        FL[rows, HALF:] = mm_nt(gm, wo[1]).astype(BF)
        hook("back", b)
        return carry

    lax.fori_loop(0, BLOCKS, feed_back, 0)
    chunk_loop("dw1", 4, 4, FLT)
    transpose_into(GT, lambda b: acc[rows_of(b), :].astype(BF))
    chunk_loop("dwo", 8, 1, GT)
    transpose_into(FLT, lambda b: x_ref[b])

    def attend_back(i, carry):
        h, w = i // (2 * BLOCKS), lax.rem(i, 2 * BLOCKS)
        rows = pl.ds(pl.multiple_of(w * WIN, WIN), WIN)
        for p in range(3):
            c = slice(p * 128, (p + 1) * 128)
            q, k, v = A[9, h, rows, c], A[10, h, rows, c], A[11, h, rows, c]
            do = FL[rows, pl.ds(pl.multiple_of(h * HALF + p * 128, 128), 128)]
            pb = probs[w, h, p]
            do2 = stacked(do, mask0, mask1)
            dv = mm_tn(pb, do2).astype(BF)
            dp = mm_nt(do2, v)
            pf = pb.astype(F32)
            dsc = (pf * (dp - jnp.sum(pf * dp, axis=-1, keepdims=True))).astype(BF)
            dq = mm(dsc, k)
            dq = (jnp.where(low, dq[:WIN], dq[WIN:]) * 0.125).astype(BF)
            dk = mm_tn(dsc, stacked(q, sc0, sc1)).astype(BF)
            A[9, h, rows, c] = dq
            A[10, h, rows, c] = dk
            A[11, h, rows, c] = dv
            hsum[h, 0:1, c] += col_sum(dq.astype(F32))
            hsum[h, 1:2, c] += col_sum(dv.astype(F32))
        hook("attb", i)
        return carry

    lax.fori_loop(0, 4 * BLOCKS, attend_back, 0)
    for h in range(2):
        sums[0, h : h + 1, :] = hsum[h, 0:1, :]
        sums[0, 2 + h : 3 + h, :] = hsum[h, 1:2, :]
    adv_vec()
    chunk_loop("dwq", 9, 3, FLT)

    def input_grad(b, carry):
        rows = block_rows(b)
        g = acc[rows, :]
        for h in range(2):
            gp = jnp.concatenate([A[9 + i, h, rows, :] for i in range(3)], axis=1)
            g = g + mm_nt(gp, wqkv[h])
        slot = lax.rem(b, 2)

        @pl.when(b >= 2)
        def _():
            pltpu.make_async_copy(stage.at[slot], gin_hbm.at[b - 2], osem.at[slot]).wait()

        stage[slot] = g
        pltpu.make_async_copy(stage.at[slot], gin_hbm.at[b], osem.at[slot]).start()
        hook("gin", b)
        return carry

    lax.fori_loop(0, BLOCKS, input_grad, 0)
    hook("tail")
    for b in range(2):
        pltpu.make_async_copy(stage.at[b], gin_hbm.at[b + 2], osem.at[b]).wait()
    while min(place) <= len(names):
        adv_vec()
        adv(*[j for j in range(len(PARTS)) if place[j] <= len(names)])
    while vec_place[0] <= len(swaps):
        adv_vec()
    vec_out[...] = sums[len(swaps)]


def layer(n_dp, *operands):
    vm = pl.BlockSpec(memory_space=pltpu.VMEM)
    hbm = pl.BlockSpec(memory_space=pl.ANY)
    bits = n_dp.bit_length() - 1
    split = min(bits, 4)
    stages = 1 + bits + split
    dma = pltpu.SemaphoreType.DMA
    return pl.pallas_call(
        functools.partial(kernel, bits),
        out_shape=(
            jax.ShapeDtypeStruct((BLOCKS, ROWS, WIDTH), F32),
            jax.ShapeDtypeStruct((BLOCKS, ROWS, WIDTH), F32),
            jax.ShapeDtypeStruct((CHUNKS, WIDTH, HALF), BF),
            jax.ShapeDtypeStruct((24, HALF), F32),
        ),
        in_specs=[vm, hbm] + [vm] * 11 + [hbm] * 6,
        out_specs=(hbm, hbm, hbm, vm),
        scratch_shapes=[
            pltpu.VMEM((2, WIDTH, 3 * HALF), BF),
            pltpu.VMEM((2, HALF, WIDTH), BF),
            pltpu.VMEM((2, WIDTH, HIDDEN), BF),
            pltpu.VMEM((2, HIDDEN, WIDTH), BF),
            pltpu.VMEM((2, 8, HIDDEN), F32),
            pltpu.VMEM((CHUNKS, 2, TOTAL, HALF), BF),
            pltpu.VMEM((2 * BLOCKS, 2, 3, 2 * WIN, WIN), BF),
            pltpu.VMEM((TOTAL, WIDTH), F32),
            pltpu.VMEM((TOTAL, 1), F32),
            pltpu.VMEM((TOTAL, WIDTH), F32),
            pltpu.VMEM((TOTAL, WIDTH), BF),
            pltpu.VMEM((WIDTH, TOTAL), BF),
            pltpu.VMEM((WIDTH, TOTAL), BF),
            pltpu.VMEM((2 * BLOCKS, WIN, WIN), F32),
            pltpu.VMEM((2, ROWS, WIDTH), F32),
            pltpu.VMEM((2, ROWS, WIDTH), BF),
            pltpu.VMEM((bits + 2, 24, HALF), F32),
            pltpu.VMEM((bits + 1, 24, HALF), F32),
            pltpu.VMEM((2, 8, HALF), F32),
            pltpu.VMEM((4, 2, WIDTH // 2, HALF), BF),
            pltpu.VMEM((CHUNKS, WIDTH // 2, HALF), BF),
            pltpu.VMEM((CHUNKS, WIDTH // 4, HALF), BF),
            pltpu.VMEM((CHUNKS, WIDTH // 8, HALF), BF),
            pltpu.VMEM((CHUNKS, WIDTH // 16, HALF), BF),
            pltpu.VMEM((max(bits - split, 1), CHUNKS, WIDTH >> split, HALF), BF),
            dma((6,)),
            dma((2,)),
            dma((len(PARTS),)),
            dma((4, 12)),
            dma((4, 12)),
            dma((stages, len(PARTS))),
            dma((stages, len(PARTS))),
            dma((bits + 1,)),
            dma((bits + 1,)),
            dma((2,)),
            dma((2,)),
        ],
        compiler_params=pltpu.CompilerParams(
            vmem_limit_bytes=67043328, collective_id=0, has_side_effects=True
        ),
    )(*operands)


def finish_kernel(
    grad_hbm, vec, wqg, wkg, wvg, wog, w1g, w2g, qbg, vbg, obg, g1g, s1g, ebg, rbg, g2g, s2g,
    low, wide, turned, isem, osem,
):
    t = lax.axis_index("tensor")
    fetch = [pltpu.make_async_copy(grad_hbm.at[k], low.at[k], isem.at[k]) for k in range(CHUNKS)]
    order = list(range(9, 12)) + list(range(4, 8)) + [8] + list(range(4))
    for k in order:
        fetch[k].start()

    def pick(r):
        return jnp.where(t == 0, vec[r : r + 1, :], vec[r + 1 : r + 2, :]).reshape(HALF)

    def whole(r):
        return jnp.concatenate([vec[r : r + 1, :], vec[r + 1 : r + 2, :]], axis=1).reshape(WIDTH)

    qbg[...] = pick(0)
    vbg[...] = pick(2)
    for ref, r in ((obg, 4), (g1g, 6), (s1g, 8), (rbg, 10), (g2g, 12), (s2g, 14)):
        ref[...] = whole(r)
    lines = [jnp.where(t == 0, vec[16 + k : 17 + k, :], vec[20 + k : 21 + k, :]) for k in range(4)]
    ebg[...] = jnp.concatenate(lines, axis=1).reshape(HIDDEN)

    sends = []
    for k in order:
        fetch[k].wait()
        if k >= 9:
            wide[k - 5] = low[k].astype(F32)
            src, dst = wide.at[k - 5], (wqg, wkg, wvg)[k - 9]
        elif k >= 4 and k < 8:
            wide[k - 4] = low[k].astype(F32)
            src, dst = wide.at[k - 4], w1g.at[:, pl.ds((k - 4) * HALF, HALF)]
        elif k == 8:
            turned[4] = low[k].astype(F32).T
            src, dst = turned.at[4], wog
        else:
            turned[k] = low[k].astype(F32).T
            src, dst = turned.at[k], w2g.at[pl.ds(k * HALF, HALF), :]
        cp = pltpu.make_async_copy(src, dst, osem.at[k])
        cp.start()
        sends.append(cp)
    for cp in sends:
        cp.wait()


def finish(grads, vec):
    vm = pl.BlockSpec(memory_space=pltpu.VMEM)
    hbm = pl.BlockSpec(memory_space=pl.ANY)
    f = lambda *shape: jax.ShapeDtypeStruct(shape, F32)
    return pl.pallas_call(
        finish_kernel,
        out_shape=(f(WIDTH, HALF), f(WIDTH, HALF), f(WIDTH, HALF), f(HALF, WIDTH), f(WIDTH, HIDDEN), f(HIDDEN, WIDTH),
                   f(HALF), f(HALF), f(WIDTH), f(WIDTH), f(WIDTH), f(HIDDEN), f(WIDTH), f(WIDTH), f(WIDTH)),
        in_specs=[hbm, vm],
        out_specs=(hbm,) * 6 + (vm,) * 9,
        scratch_shapes=[
            pltpu.VMEM((CHUNKS, WIDTH, HALF), BF),
            pltpu.VMEM((7, WIDTH, HALF), F32),
            pltpu.VMEM((5, HALF, WIDTH), F32),
            pltpu.SemaphoreType.DMA((CHUNKS,)),
            pltpu.SemaphoreType.DMA((CHUNKS,)),
        ],
        compiler_params=pltpu.CompilerParams(vmem_limit_bytes=50 * 1024 * 1024),
    )(grads, vec)


def local(
    n_dp, inputs, segments, padding, query_weight, query_bias, key_weight, value_weight, value_bias,
    output_weight, output_bias, first_gain, first_shift, expand_weight, expand_bias,
    reduce_weight, reduce_bias, second_gain, second_shift, cotangent,
):
    out, gin, grads, vec = layer(
        n_dp, inputs, cotangent, segments, padding, query_bias, value_bias, expand_bias, output_bias, first_gain,
        first_shift, reduce_bias, second_gain, second_shift, query_weight, key_weight, value_weight,
        output_weight, expand_weight, reduce_weight,
    )
    wq, wk, wv, wo, w1, w2, qb, vb, ob, g1, s1, eb, rb, g2, s2 = finish(grads, vec)
    return (out, gin, wq, qb, wk, wv, vb, wo, ob, g1, s1, w1, eb, w2, rb, g2, s2)


def solution(mesh):
    tokens = P(None, ("dp", "tensor"), None)
    return jax.shard_map(
        functools.partial(local, mesh.shape["dp"]),
        mesh=mesh,
        in_specs=(
            tokens, P(None, "dp"), P(None, "dp"), P(None, "tensor"), P("tensor"), P(None, "tensor"),
            P(None, "tensor"), P("tensor"), P("tensor", None), P(), P(), P(), P(None, "tensor"),
            P("tensor"), P("tensor", None), P(), P(), P(), tokens,
        ),
        out_specs=(
            tokens, tokens, P(None, "tensor"), P("tensor"), P(None, "tensor"), P(None, "tensor"),
            P("tensor"), P("tensor", None), P(), P(), P(), P(None, "tensor"), P("tensor"),
            P("tensor", None), P(), P(), P(),
        ),
        check_vma=False,
    )
```

```python
import functools

import jax
import jax.numpy as jnp
from jax import lax
from jax.experimental import pallas as pl
from jax.experimental.pallas import tpu as pltpu
from jax.sharding import PartitionSpec as P

WIN = 128
BLOCKS = 4
ROWS = 256
TOTAL = BLOCKS * ROWS
WIDTH = 768
HALF = 384
HIDDEN = 1536
CHUNKS = 12
EPS = 1e-12
BF = jnp.bfloat16
F32 = jnp.float32
MESH = pl.DeviceIdType.MESH


def mm(a, b):
    return lax.dot_general(a, b, (((1,), (0,)), ((), ())), preferred_element_type=F32)


def mm_nt(a, b):
    return lax.dot_general(a, b, (((1,), (1,)), ((), ())), preferred_element_type=F32)


def mm_tn(a, b):
    return lax.dot_general(a, b, (((0,), (0,)), ((), ())), preferred_element_type=F32)


def row_mean(a):
    return jnp.sum(a, axis=-1, keepdims=True) * (1.0 / WIDTH)


def col_sum(a):
    return jnp.sum(a, axis=0, keepdims=True)

WAYS = ((2, 1, 0), (1, 2, 0), (2, 1, 0), (2, 0), (0,), (1, 0), (2, 1, 0), (1, 2, 0), (1, 0), (2, 1, 0), (0,), (1, 0))
FIRST = (0, 1, 2, 3, 7, 6, 5, 9, 11, 4, 8, 10)
PARTS = ((0, 0, 384), (1, 0, 384), (2, 0, 384), (3, 0, 384), (4, 0, 384), (5, 0, 384), (6, 0, 384), (7, 0, 384), (8, 0, 384), (9, 0, 384), (10, 0, 384), (11, 0, 128), (11, 128, 128), (11, 256, 128))
ORDERS = ((0, 2, 3, 1), (0, 2, 3, 1), (0, 2, 1, 3), (0, 2, 1, 3), (0, 2, 1, 3), (0, 1, 2, 3), (0, 1, 2, 3), (0, 1, 2, 3), (0, 1, 2, 3), (0, 1, 2, 3), (0, 2, 1, 3), (0, 1, 2, 3), (0, 1, 2, 3), (0, 1, 2, 3))
PLAN = {
    "attend": ((2, (0,)), (3, (1, 2, 0, 1, 3, 2, 7, 0, 6, 1, 0, 1, 2, 5, 3, 7, 2)), (4, (3, 6, 9)), (6, (5, 11)), (7, (7,)),),
    "norm1": ((0, (5,)), (1, (6, 7, 9)), (3, (6,)),),
    "expand": ((0, (4, 11)), (2, (4, 8, 11)), (3, (9,)), (5, (9,)), (6, (8,)), (7, (10,)),),
    "rown": ((0, (8,)), (2, (10,)),),
    "dw2": ((0, (20,)), (1, (21,)), (2, (20, 22)), (3, (21, 23)),),
    "back": ((0, (22, 23)), (1, (20,)), (3, (20, 21)),),
    "dw1": ((0, (24,)), (1, (25,)), (2, (24, 26, 22)), (3, (25, 27, 20, 26, 21)),),
    "dwo": ((0, (27, 28)),),
    "attb": ((0, (20, 22, 23)), (1, (28,)), (2, (20, 21)), (3, (22,)), (4, (23, 21, 24)), (6, (20,)), (7, (21, 22, 23)), (8, (24,)), (9, (25,)), (11, (20, 24)), (12, (21,)), (13, (20, 22)), (14, (23, 25, 26)), (15, (24,)),),
    "dwq": ((0, (29, 21, 22)), (1, (30, 23, 25)), (2, (29, 31, 32, 33, 21, 24, 26, 30, 27, 31, 32, 33, 22, 23, 25)),),
    "gin": ((0, (24, 26, 22)), (2, (28, 40, 27, 25)), (3, (23, 40)),),
    "tail": ((0, (26, 23, 24, 28, 40, 27, 24, 29, 26, 25, 28, 40, 27, 26, 29, 30, 28, 31, 25, 40, 29, 25, 27, 32, 26, 28, 30, 33, 31, 26, 29, 32, 27, 28, 30, 31, 32, 33, 29, 33, 27, 30, 31, 32, 29, 27, 33, 28, 30, 28, 31, 32, 33, 29, 31, 30, 32, 29, 33, 31, 32, 31, 33, 32, 30, 33, 30)),),
}


def kernel(
    bits,
    x_ref, cot_hbm, seg_ref, pad_ref, qb_ref, vb_ref, eb_ref, ob_ref, g1_ref, s1_ref, rb_ref, g2_ref, s2_ref,
    wq_hbm, wk_hbm, wv_hbm, wo_hbm, w1_hbm, w2_hbm,
    out_hbm, gin_hbm, grad_hbm, vec_out,
    wqkv, wo, w1, w2, hv, A, probs, normed, spread, acc, FL, FLT, GT, bias, stage, cot, sums, got, hsum,
    R0, R1, R2, R3, R4, RX,
    lsem, osem, fsem, wsend, wrecv, gsend, grecv, vsend, vrecv, bsem, psem,
):
    t = lax.axis_index("tensor")
    me = lax.axis_index("dp")
    bit = [lax.rem(me // (1 << i), 2) for i in range(bits)]
    split = min(bits, 4)

    def mate(i):
        return (me + (1 << i) * (1 - 2 * bit[i]), t)

    across = (me, 1 - t)
    partners = [across] + [mate(i) for i in range(bits)]

    barrier = pltpu.get_barrier_semaphore()
    for who in partners:
        pl.semaphore_signal(barrier, inc=1, device_id=who, device_id_type=MESH)

    locals_ = [
        (wq_hbm, wqkv.at[t, :, pl.ds(0, HALF)]),
        (wk_hbm, wqkv.at[t, :, pl.ds(HALF, HALF)]),
        (wv_hbm, wqkv.at[t, :, pl.ds(2 * HALF, HALF)]),
        (wo_hbm, wo.at[t]),
        (w1_hbm, w1.at[t]),
        (w2_hbm, w2.at[t]),
    ]
    loads = [pltpu.make_async_copy(s, d, lsem.at[i]) for i, (s, d) in enumerate(locals_)]
    for cp in loads:
        cp.start()

    def row(ref):
        return ref[...].astype(F32).reshape(1, ref.shape[0])

    hv[t] = jnp.zeros((8, HIDDEN), F32)
    hv[t, 0:1, :] = row(eb_ref)
    hv[t, 1:2, 0:HALF] = row(qb_ref)
    hv[t, 1:2, HALF : 2 * HALF] = row(vb_ref)
    out_b, gain1, shift1 = row(ob_ref), row(g1_ref), row(s1_ref)
    red_b, gain2, shift2 = row(rb_ref), row(g2_ref), row(s2_ref)
    pl.semaphore_wait(barrier, len(partners))

    def part_rows(base, n, ways, fixed):
        size = n // (1 << len(ways))
        at_ = sum((bit[w] * (size << j) for j, w in enumerate(ways)), 0)
        free = len(ways) - fixed
        at_ = sum((bit[w] * (size << j) for j, w in enumerate(ways) if j >= free), 0)
        return pl.ds(pl.multiple_of(base + at_, 16), size << free)

    def cols(i):
        return pl.ds(i * HALF, HALF)

    every = pl.ds(0, WIDTH)
    pieces = [(src, every, wqkv, cols(i), 0, WIDTH) for i, src in enumerate((wq_hbm, wk_hbm, wv_hbm))]
    pieces = [(src, pl.ds(0, HALF), dst, c, base, n) for src, _, dst, c, base, n in pieces]
    pieces += [(wo_hbm, every, wo, every, 0, HALF)]
    pieces += [(w1_hbm, cols(i), w1, cols(i), 0, WIDTH) for i in range(4)]
    pieces += [(w2_hbm, every, w2, every, i * HALF, HALF) for i in range(4)]

    def weight_copy(g, s):
        hbm, hc, dst, dc, base, n = pieces[g]
        ways = WAYS[g]
        r = part_rows(base, n, ways, len(ways) - max(s - 1, 0))
        if s == 0:
            src, to, who = hbm.at[r, hc], dst.at[t, r, dc], across
        else:
            src = to = dst.at[1 - t, r, dc]
            who = mate(ways[s - 1])
        return pltpu.make_async_remote_copy(
            src_ref=src, dst_ref=to, send_sem=wsend.at[s, g], recv_sem=wrecv.at[s, g],
            device_id=who, device_id_type=MESH,
        )

    wplace = [0] * len(pieces)

    def adv_weight(g):
        s, last = wplace[g], len(WAYS[g])
        if s > 0:
            weight_copy(g, s - 1).wait()
        if s <= last:
            weight_copy(g, s).start()
        wplace[g] = s + 1

    def weights_ready(which):
        while min(wplace[g] - len(WAYS[g]) for g in which) < 2:
            for g in which:
                if wplace[g] < len(WAYS[g]) + 2:
                    adv_weight(g)

    bias_copy = pltpu.make_async_remote_copy(
        src_ref=hv.at[t], dst_ref=hv.at[t], send_sem=bsem.at[0], recv_sem=bsem.at[1],
        device_id=across, device_id_type=MESH,
    )
    bias_copy.start()
    for g in FIRST:
        adv_weight(g)

    def run(ops):
        for op in ops:
            if op < 20:
                adv_weight(op)
            elif op < 40:
                adv(op - 20)
            else:
                adv_vec()

    def at(loop_index, step, action):
        @pl.when(loop_index == step)
        def _():
            action()

    def hook(name, loop_index=None):
        for step, ops in PLAN.get(name, ()):
            if loop_index is None:
                run(ops)
            else:
                at(loop_index, step, lambda ops=ops: run(ops))

    sums[0] = jnp.zeros((24, HALF), F32)
    hsum[...] = jnp.zeros_like(hsum)
    lane = lax.broadcasted_iota(jnp.int32, (1, 128), 1)
    low = lane < 64
    mask0 = jnp.where(low, 1.0, 0.0).astype(BF)
    mask1 = jnp.where(low, 0.0, 1.0).astype(BF)
    sc0 = jnp.where(low, 0.125, 0.0).astype(BF)
    sc1 = jnp.where(low, 0.0, 0.125).astype(BF)

    for b in range(BLOCKS):
        for wi in range(2):
            cols = pl.ds(pl.multiple_of(t * ROWS + wi * WIN, WIN), WIN)
            seg = jnp.broadcast_to(seg_ref[b : b + 1, cols].astype(F32), (WIN, WIN))
            live = jnp.broadcast_to(pad_ref[b : b + 1, cols].astype(F32), (WIN, WIN))
            bias[2 * b + wi] = jnp.where((seg == seg.T) & (live > 0.5), 0.0, -1e30)

    def stacked(a, m0, m1):
        return jnp.concatenate([a * m0, a * m1], axis=0)

    def block_rows(b):
        return pl.ds(pl.multiple_of(b * ROWS, ROWS), ROWS)

    for cp in loads[:3]:
        cp.wait()

    def attend(i, carry):
        b = lax.rem(i, BLOCKS)
        h = t + (i // BLOCKS) * (1 - 2 * t)
        rows = block_rows(b)
        pr = mm(x_ref[b], wqkv[h])
        q = (pr[:, :HALF] + hv[h, 1:2, 0:HALF]).astype(BF)
        k = pr[:, HALF : 2 * HALF].astype(BF)
        v = (pr[:, 2 * HALF :] + hv[h, 1:2, HALF : 2 * HALF]).astype(BF)
        A[9, h, rows, :] = q
        A[10, h, rows, :] = k
        A[11, h, rows, :] = v
        for wi in range(2):
            r = slice(wi * WIN, (wi + 1) * WIN)
            bb = bias[b * 2 + wi]
            bb = jnp.concatenate([bb, bb], axis=0)
            for p in range(3):
                c = slice(p * 128, (p + 1) * 128)
                s = mm_nt(stacked(q[r, c], sc0, sc1), k[r, c]) + bb
                e = jnp.exp(s - jnp.max(s, axis=-1, keepdims=True))
                pb = (e * (1.0 / jnp.sum(e, axis=-1, keepdims=True))).astype(BF)
                probs[b * 2 + wi, h, p] = pb
                o = mm(pb, v[r, c])
                o = jnp.where(low, o[:WIN], o[WIN:])
                A[8, h, pl.ds(pl.multiple_of(b * ROWS + wi * WIN, WIN), WIN), c] = o.astype(BF)

        hook("attend", i)
        at(i, 3, own_done)
        return carry

    def own_done():
        weights_ready([0, 1, 2])
        bias_copy.wait()

    lax.fori_loop(0, 2 * BLOCKS, attend, 0)

    def joined(k, rows):
        return jnp.concatenate([A[k, 0, rows, :], A[k, 1, rows, :]], axis=1)

    def normalize(hidden):
        center = hidden - row_mean(hidden)
        rs = lax.rsqrt(row_mean(center * center) + EPS)
        return center * rs, rs

    def add_vec(row, value):
        sums[0, row : row + 1, :] += value[:, :HALF]
        sums[0, row + 1 : row + 2, :] += value[:, HALF:]


    loads[3].wait()
    hook("pre_norm")
    weights_ready([3])

    def first_norm(b, carry):
        rows = block_rows(b)
        mixed = joined(8, rows)
        att = mm(mixed[:, :HALF], wo[0]) + mm(mixed[:, HALF:], wo[1])
        n, rs = normalize(x_ref[b].astype(F32) + att + out_b)
        normed[rows, :] = n
        spread[rows, :] = rs
        first = n * gain1 + shift1
        FL[rows, :] = first.astype(BF)
        hook("norm1", b)
        return carry

    lax.fori_loop(0, BLOCKS, first_norm, 0)
    loads[4].wait()

    def expand(i, carry):
        b = lax.rem(i, BLOCKS)
        h = t + (i // BLOCKS) * (1 - 2 * t)
        rows = block_rows(b)
        inner_all = mm(FL[rows, :], w1[h]) + hv[h, 0:1, :]
        for k in range(4):
            inner = inner_all[:, k * HALF : (k + 1) * HALF]
            phi = 0.5 + 0.5 * lax.erf(inner * 0.7071067811865476)
            slope = phi + inner * jnp.exp(-0.5 * inner * inner) * 0.3989422804014327
            A[k, h, rows, :] = (inner * phi).astype(BF)
            A[4 + k, h, rows, :] = slope.astype(BF)

        hook("expand", i)
        at(i, 3, lambda: weights_ready([4, 5, 6, 7]))
        return carry

    lax.fori_loop(0, 2 * BLOCKS, expand, 0)
    loads[5].wait()

    def reduce_half(b, h):
        rows = block_rows(b)
        return mm(jnp.concatenate([A[k, h, rows, :] for k in range(4)], axis=1), w2[h])

    def reduce_own(b, carry):
        acc[block_rows(b), :] = reduce_half(b, t)
        hook("rown", b)
        return carry

    def cot_copy(b):
        return pltpu.make_async_copy(cot_hbm.at[b], cot.at[lax.rem(b, 2)], psem.at[lax.rem(b, 2)])

    cot_copy(0).start()
    cot_copy(1).start()
    lax.fori_loop(0, BLOCKS, reduce_own, 0)
    hook("pre_reduce")
    weights_ready([8, 9, 10, 11])

    def second_norm(b, carry):
        rows = block_rows(b)
        red = acc[rows, :] + reduce_half(b, 1 - t)
        n, rs = normalize(normed[rows, :] * gain1 + shift1 + red + red_b)
        slot = lax.rem(b, 2)

        @pl.when(b >= 2)
        def _():
            pltpu.make_async_copy(stage.at[slot], out_hbm.at[b - 2], osem.at[slot]).wait()

        stage[slot] = n * gain2 + shift2
        pltpu.make_async_copy(stage.at[slot], out_hbm.at[b], osem.at[slot]).start()
        cot_copy(b).wait()
        c = cot[slot].astype(F32)

        @pl.when(b + 2 < BLOCKS)
        def _():
            cot_copy(b + 2).start()

        add_vec(14, col_sum(c))
        add_vec(12, col_sum(c * n))
        u = c * gain2
        gs = rs * (u - row_mean(u) - n * row_mean(u * n))
        add_vec(10, col_sum(gs))
        acc[rows, :] = gs
        return carry

    lax.fori_loop(0, BLOCKS, second_norm, 0)
    for b in range(2):
        pltpu.make_async_copy(stage.at[b], out_hbm.at[b + 2], osem.at[b]).wait()

    def span(i):
        return WIDTH >> (i + 1)

    def lo(j, i):
        return sum((bit[ORDERS[j][n]] * span(n) for n in range(i + 1)), 0)

    def ds(at_, n):
        return pl.ds(pl.multiple_of(at_, 16), n)

    def held(j, h, r):
        k, first, width = PARTS[j]
        if k < 9:
            return A, (k, h, r, pl.ds(first, width))
        return w1, (h, r, pl.ds((k - 9) * HALF + first, width))

    def add_in(j, h, r, value):
        ref, at_ = held(j, h, r)
        ref[at_] = ref[at_] + value

    def view(j, h, r):
        ref, at_ = held(j, h, r)
        return ref.at[at_]

    def landing(j, p):
        k, first, width = PARTS[j]
        c = pl.ds(first, width)
        if p == 0:
            return R0, (k % 4, slice(None), slice(None), c)
        return (R1, R2, R3, R4)[p - 1], (k, slice(None), c)

    names = [("core", 0), ("tensor", 0)] + [("half", i) for i in range(1, split)]
    names += [("swap", i) for i in range(bits - split)] + [("gather", i) for i in reversed(range(split))]

    def piece_copy(j, s):
        kind, i = names[s]
        way = ORDERS[j]
        k, first, width = PARTS[j]
        if kind == "core":
            src, who = view(j, slice(None), ds((1 - bit[way[0]]) * span(0), span(0))), mate(way[0])
            land, at_ = landing(j, 0)
            dst = land.at[at_]
        elif kind == "tensor":
            src, who = view(j, 1 - t, ds(lo(j, 0), span(0))), across
            land, at_ = landing(j, 1)
            dst = land.at[at_]
        elif kind == "half":
            src = view(j, t, ds(lo(j, i - 1) + (1 - bit[way[i]]) * span(i), span(i)))
            who = mate(way[i])
            land, at_ = landing(j, i + 1)
            dst = land.at[at_]
        elif kind == "swap":
            src, who = view(j, t, ds(lo(j, split - 1), span(split - 1))), mate(split + i)
            dst = RX.at[i, k, :, pl.ds(first, width)]
        else:
            r = ds(lo(j, i), span(i))
            dst, who = grad_hbm.at[k, r, pl.ds(first, width)], mate(way[i])
            src = view(j, t, r) if i == split - 1 else dst
        return pltpu.make_async_remote_copy(
            src_ref=src, dst_ref=dst, send_sem=gsend.at[s, j], recv_sem=grecv.at[s, j],
            device_id=who, device_id_type=MESH,
        )

    def keep_copy(j):
        k, first, width = PARTS[j]
        r = ds(lo(j, split - 1), span(split - 1))
        return pltpu.make_async_copy(view(j, t, r), grad_hbm.at[k, r, pl.ds(first, width)], fsem.at[j])

    def settle(j, s):
        piece_copy(j, s).wait()
        kind, i = names[s]
        k, first, width = PARTS[j]
        if kind == "core":
            land, at_ = landing(j, 0)
            add_in(j, slice(None), ds(lo(j, 0), span(0)), land[at_])
        elif kind == "tensor":
            land, at_ = landing(j, 1)
            add_in(j, t, ds(lo(j, 0), span(0)), land[at_])
        elif kind == "half":
            land, at_ = landing(j, i + 1)
            add_in(j, t, ds(lo(j, i), span(i)), land[at_])
        elif kind == "swap":
            add_in(j, t, ds(lo(j, split - 1), span(split - 1)), RX[i, k, :, pl.ds(first, width)])
        elif i == split - 1:
            keep_copy(j).wait()
        if s + 1 < len(names) and names[s + 1] == ("gather", split - 1):
            keep_copy(j).start()

    place = [0] * len(PARTS)

    def adv(*which):
        for k in which:
            s = place[k]
            if s > len(names):
                continue
            if s > 0:
                settle(k, s - 1)
            if s < len(names):
                piece_copy(k, s).start()
            place[k] = s + 1

    swaps = [across] + [mate(i) for i in range(bits)]
    vec_place = [0]

    def adv_vec():
        s = vec_place[0]

        def cp(j):
            return pltpu.make_async_remote_copy(
                src_ref=sums.at[j], dst_ref=got.at[j], send_sem=vsend.at[j], recv_sem=vrecv.at[j],
                device_id=swaps[j], device_id_type=MESH,
            )

        if s > len(swaps):
            return
        if s > 0:
            cp(s - 1).wait()
            sums[s] = sums[s - 1] + got[s - 1]
        if s < len(swaps):
            cp(s).start()
        vec_place[0] = s + 1

    def transpose_into(dst, get):
        for b in range(BLOCKS):
            dst[:, b * ROWS : (b + 1) * ROWS] = get(b).T

    def rows_of(b):
        return slice(b * ROWS, (b + 1) * ROWS)

    def chunk_loop(name, first, count, left):
        def one(j, carry):
            k = first + j
            full = mm(left[...], joined(k, slice(None)))
            for h in range(2):
                part = full[:, h * HALF : (h + 1) * HALF].astype(BF)
                if first < 9:
                    A[k, h, 0:WIDTH, :] = part
                else:
                    w1[h, :, pl.ds(pl.multiple_of(j * HALF, HALF), HALF)] = part
            hook(name, j)
            return carry

        lax.fori_loop(0, count, one, 0)

    transpose_into(GT, lambda b: acc[rows_of(b), :].astype(BF))
    chunk_loop("dw2", 0, 4, GT)
    transpose_into(FLT, lambda b: FL[rows_of(b), :])
    hook("mid")

    def feed_back(b, carry):
        rows = block_rows(b)
        gs = acc[rows, :]
        gl = gs.astype(BF)
        gf = gs
        for h in range(2):
            da = mm_nt(gl, w2[h])
            gis = []
            for k in range(4):
                gi = (da[:, k * HALF : (k + 1) * HALF] * A[4 + k, h, rows, :].astype(F32)).astype(BF)
                A[4 + k, h, rows, :] = gi
                sums[0, 16 + 4 * h + k : 17 + 4 * h + k, :] += col_sum(gi.astype(F32))
                gis.append(gi)
            gf = gf + mm_nt(jnp.concatenate(gis, axis=1), w1[h])
        n = normed[rows, :]
        add_vec(6, col_sum(gf * n))
        add_vec(8, col_sum(gf))
        u = gf * gain1
        gh = spread[rows, :] * (u - row_mean(u) - n * row_mean(u * n))
        add_vec(4, col_sum(gh))
        acc[rows, :] = gh
        gm = gh.astype(BF)
        FL[rows, 0:HALF] = mm_nt(gm, wo[0]).astype(BF)
        FL[rows, HALF:] = mm_nt(gm, wo[1]).astype(BF)
        hook("back", b)
        return carry

    lax.fori_loop(0, BLOCKS, feed_back, 0)
    chunk_loop("dw1", 4, 4, FLT)
    transpose_into(GT, lambda b: acc[rows_of(b), :].astype(BF))
    chunk_loop("dwo", 8, 1, GT)
    transpose_into(FLT, lambda b: x_ref[b])

    def attend_back(i, carry):
        h, w = i // (2 * BLOCKS), lax.rem(i, 2 * BLOCKS)
        rows = pl.ds(pl.multiple_of(w * WIN, WIN), WIN)
        for p in range(3):
            c = slice(p * 128, (p + 1) * 128)
            q, k, v = A[9, h, rows, c], A[10, h, rows, c], A[11, h, rows, c]
            do = FL[rows, pl.ds(pl.multiple_of(h * HALF + p * 128, 128), 128)]
            pb = probs[w, h, p]
            do2 = stacked(do, mask0, mask1)
            dv = mm_tn(pb, do2).astype(BF)
            dp = mm_nt(do2, v)
            pf = pb.astype(F32)
            dsc = (pf * (dp - jnp.sum(pf * dp, axis=-1, keepdims=True))).astype(BF)
            dq = mm(dsc, k)
            dq = (jnp.where(low, dq[:WIN], dq[WIN:]) * 0.125).astype(BF)
            dk = mm_tn(dsc, stacked(q, sc0, sc1)).astype(BF)
            A[9, h, rows, c] = dq
            A[10, h, rows, c] = dk
            A[11, h, rows, c] = dv
            hsum[h, 0:1, c] += col_sum(dq.astype(F32))
            hsum[h, 1:2, c] += col_sum(dv.astype(F32))
        hook("attb", i)
        return carry

    lax.fori_loop(0, 4 * BLOCKS, attend_back, 0)
    for h in range(2):
        sums[0, h : h + 1, :] = hsum[h, 0:1, :]
        sums[0, 2 + h : 3 + h, :] = hsum[h, 1:2, :]
    adv_vec()
    chunk_loop("dwq", 9, 3, FLT)

    def input_grad(b, carry):
        rows = block_rows(b)
        g = acc[rows, :]
        for h in range(2):
            gp = jnp.concatenate([A[9 + i, h, rows, :] for i in range(3)], axis=1)
            g = g + mm_nt(gp, wqkv[h])
        slot = lax.rem(b, 2)

        @pl.when(b >= 2)
        def _():
            pltpu.make_async_copy(stage.at[slot], gin_hbm.at[b - 2], osem.at[slot]).wait()

        stage[slot] = g
        pltpu.make_async_copy(stage.at[slot], gin_hbm.at[b], osem.at[slot]).start()
        hook("gin", b)
        return carry

    lax.fori_loop(0, BLOCKS, input_grad, 0)
    hook("tail")
    for b in range(2):
        pltpu.make_async_copy(stage.at[b], gin_hbm.at[b + 2], osem.at[b]).wait()
    while min(place) <= len(names):
        adv_vec()
        adv(*[j for j in range(len(PARTS)) if place[j] <= len(names)])
    while vec_place[0] <= len(swaps):
        adv_vec()
    vec_out[...] = sums[len(swaps)]


def layer(n_dp, *operands):
    vm = pl.BlockSpec(memory_space=pltpu.VMEM)
    hbm = pl.BlockSpec(memory_space=pl.ANY)
    bits = n_dp.bit_length() - 1
    split = min(bits, 4)
    stages = 1 + bits + split
    dma = pltpu.SemaphoreType.DMA
    return pl.pallas_call(
        functools.partial(kernel, bits),
        out_shape=(
            jax.ShapeDtypeStruct((BLOCKS, ROWS, WIDTH), F32),
            jax.ShapeDtypeStruct((BLOCKS, ROWS, WIDTH), F32),
            jax.ShapeDtypeStruct((CHUNKS, WIDTH, HALF), BF),
            jax.ShapeDtypeStruct((24, HALF), F32),
        ),
        in_specs=[vm, hbm] + [vm] * 11 + [hbm] * 6,
        out_specs=(hbm, hbm, hbm, vm),
        scratch_shapes=[
            pltpu.VMEM((2, WIDTH, 3 * HALF), BF),
            pltpu.VMEM((2, HALF, WIDTH), BF),
            pltpu.VMEM((2, WIDTH, HIDDEN), BF),
            pltpu.VMEM((2, HIDDEN, WIDTH), BF),
            pltpu.VMEM((2, 8, HIDDEN), F32),
            pltpu.VMEM((CHUNKS, 2, TOTAL, HALF), BF),
            pltpu.VMEM((2 * BLOCKS, 2, 3, 2 * WIN, WIN), BF),
            pltpu.VMEM((TOTAL, WIDTH), F32),
            pltpu.VMEM((TOTAL, 1), F32),
            pltpu.VMEM((TOTAL, WIDTH), F32),
            pltpu.VMEM((TOTAL, WIDTH), BF),
            pltpu.VMEM((WIDTH, TOTAL), BF),
            pltpu.VMEM((WIDTH, TOTAL), BF),
            pltpu.VMEM((2 * BLOCKS, WIN, WIN), F32),
            pltpu.VMEM((2, ROWS, WIDTH), F32),
            pltpu.VMEM((2, ROWS, WIDTH), BF),
            pltpu.VMEM((bits + 2, 24, HALF), F32),
            pltpu.VMEM((bits + 1, 24, HALF), F32),
            pltpu.VMEM((2, 8, HALF), F32),
            pltpu.VMEM((4, 2, WIDTH // 2, HALF), BF),
            pltpu.VMEM((CHUNKS, WIDTH // 2, HALF), BF),
            pltpu.VMEM((CHUNKS, WIDTH // 4, HALF), BF),
            pltpu.VMEM((CHUNKS, WIDTH // 8, HALF), BF),
            pltpu.VMEM((CHUNKS, WIDTH // 16, HALF), BF),
            pltpu.VMEM((max(bits - split, 1), CHUNKS, WIDTH >> split, HALF), BF),
            dma((6,)),
            dma((2,)),
            dma((len(PARTS),)),
            dma((4, 12)),
            dma((4, 12)),
            dma((stages, len(PARTS))),
            dma((stages, len(PARTS))),
            dma((bits + 1,)),
            dma((bits + 1,)),
            dma((2,)),
            dma((2,)),
        ],
        compiler_params=pltpu.CompilerParams(
            vmem_limit_bytes=67043328, collective_id=0, has_side_effects=True
        ),
    )(*operands)


def finish_kernel(
    grad_hbm, out_low, gin_low, vec, outg, ging, wqg, wkg, wvg, wog, w1g, w2g, qbg, vbg, obg, g1g, s1g, ebg, rbg, g2g, s2g,
    low, wide, turned, rows, isem, osem, rsem, ssem,
):
    t = lax.axis_index("tensor")
    fetch = [pltpu.make_async_copy(grad_hbm.at[k], low.at[k], isem.at[k]) for k in range(CHUNKS)]
    order = list(range(9, 12)) + list(range(4, 8)) + [8] + list(range(4))
    for k in order:
        fetch[k].start()
    passed = []
    for i, ref in enumerate((out_low, gin_low)):
        cp = pltpu.make_async_copy(ref, rows.at[i], rsem.at[i])
        cp.start()
        passed.append(cp)

    def pick(r):
        return jnp.where(t == 0, vec[r : r + 1, :], vec[r + 1 : r + 2, :]).reshape(HALF)

    def whole(r):
        return jnp.concatenate([vec[r : r + 1, :], vec[r + 1 : r + 2, :]], axis=1).reshape(WIDTH)

    qbg[...] = pick(0)
    vbg[...] = pick(2)
    for ref, r in ((obg, 4), (g1g, 6), (s1g, 8), (rbg, 10), (g2g, 12), (s2g, 14)):
        ref[...] = whole(r)
    lines = [jnp.where(t == 0, vec[16 + k : 17 + k, :], vec[20 + k : 21 + k, :]) for k in range(4)]
    ebg[...] = jnp.concatenate(lines, axis=1).reshape(HIDDEN)

    sends = []
    for k in order:
        fetch[k].wait()
        if k >= 9:
            wide[k - 5] = low[k].astype(F32)
            src, dst = wide.at[k - 5], (wqg, wkg, wvg)[k - 9]
        elif k >= 4 and k < 8:
            wide[k - 4] = low[k].astype(F32)
            src, dst = wide.at[k - 4], w1g.at[:, pl.ds((k - 4) * HALF, HALF)]
        elif k == 8:
            turned[4] = low[k].astype(F32).T
            src, dst = turned.at[4], wog
        else:
            turned[k] = low[k].astype(F32).T
            src, dst = turned.at[k], w2g.at[pl.ds(k * HALF, HALF), :]
        cp = pltpu.make_async_copy(src, dst, osem.at[k])
        cp.start()
        sends.append(cp)
    for i, ref in enumerate((outg, ging)):
        passed[i].wait()
        cp = pltpu.make_async_copy(rows.at[i], ref, ssem.at[i])
        cp.start()
        sends.append(cp)
    for cp in sends:
        cp.wait()


def finish(out, gin, grads, vec):
    vm = pl.BlockSpec(memory_space=pltpu.VMEM)
    hbm = pl.BlockSpec(memory_space=pl.ANY)
    f = lambda *shape: jax.ShapeDtypeStruct(shape, F32)
    return pl.pallas_call(
        finish_kernel,
        out_shape=(f(BLOCKS, ROWS, WIDTH), f(BLOCKS, ROWS, WIDTH), f(WIDTH, HALF), f(WIDTH, HALF), f(WIDTH, HALF), f(HALF, WIDTH), f(WIDTH, HIDDEN), f(HIDDEN, WIDTH),
                   f(HALF), f(HALF), f(WIDTH), f(WIDTH), f(WIDTH), f(HIDDEN), f(WIDTH), f(WIDTH), f(WIDTH)),
        in_specs=[hbm, hbm, hbm, vm],
        out_specs=(hbm,) * 8 + (vm,) * 9,
        scratch_shapes=[
            pltpu.VMEM((CHUNKS, WIDTH, HALF), BF),
            pltpu.VMEM((7, WIDTH, HALF), F32),
            pltpu.VMEM((5, HALF, WIDTH), F32),
            pltpu.VMEM((2, BLOCKS, ROWS, WIDTH), F32),
            pltpu.SemaphoreType.DMA((CHUNKS,)),
            pltpu.SemaphoreType.DMA((CHUNKS,)),
            pltpu.SemaphoreType.DMA((2,)),
            pltpu.SemaphoreType.DMA((2,)),
        ],
        compiler_params=pltpu.CompilerParams(vmem_limit_bytes=50 * 1024 * 1024),
    )(grads, out, gin, vec)


def local(
    n_dp, inputs, segments, padding, query_weight, query_bias, key_weight, value_weight, value_bias,
    output_weight, output_bias, first_gain, first_shift, expand_weight, expand_bias,
    reduce_weight, reduce_bias, second_gain, second_shift, cotangent,
):
    out, gin, grads, vec = layer(
        n_dp, inputs, cotangent, segments, padding, query_bias, value_bias, expand_bias, output_bias, first_gain,
        first_shift, reduce_bias, second_gain, second_shift, query_weight, key_weight, value_weight,
        output_weight, expand_weight, reduce_weight,
    )
    out, gin, wq, wk, wv, wo, w1, w2, qb, vb, ob, g1, s1, eb, rb, g2, s2 = finish(out, gin, grads, vec)
    return (out, gin, wq, qb, wk, wv, vb, wo, ob, g1, s1, w1, eb, w2, rb, g2, s2)


def solution(mesh):
    tokens = P(None, ("dp", "tensor"), None)
    return jax.shard_map(
        functools.partial(local, mesh.shape["dp"]),
        mesh=mesh,
        in_specs=(
            tokens, P(None, "dp"), P(None, "dp"), P(None, "tensor"), P("tensor"), P(None, "tensor"),
            P(None, "tensor"), P("tensor"), P("tensor", None), P(), P(), P(), P(None, "tensor"),
            P("tensor"), P("tensor", None), P(), P(), P(), tokens,
        ),
        out_specs=(
            tokens, tokens, P(None, "tensor"), P("tensor"), P(None, "tensor"), P(None, "tensor"),
            P("tensor"), P("tensor", None), P(), P(), P(), P(None, "tensor"), P("tensor"),
            P("tensor", None), P(), P(), P(),
        ),
        check_vma=False,
    )
```

```python
import functools

import jax
import jax.numpy as jnp
from jax import lax
from jax.experimental import pallas as pl
from jax.experimental.pallas import tpu as pltpu
from jax.sharding import PartitionSpec as P

WIN = 128
BLOCKS = 4
ROWS = 256
TOTAL = BLOCKS * ROWS
WIDTH = 768
HALF = 384
HIDDEN = 1536
CHUNKS = 12
EPS = 1e-12
BF = jnp.bfloat16
F32 = jnp.float32
MESH = pl.DeviceIdType.MESH


def mm(a, b):
    return lax.dot_general(a, b, (((1,), (0,)), ((), ())), preferred_element_type=F32)


def mm_nt(a, b):
    return lax.dot_general(a, b, (((1,), (1,)), ((), ())), preferred_element_type=F32)


def mm_tn(a, b):
    return lax.dot_general(a, b, (((0,), (0,)), ((), ())), preferred_element_type=F32)


def row_mean(a):
    return jnp.sum(a, axis=-1, keepdims=True) * (1.0 / WIDTH)


def col_sum(a):
    return jnp.sum(a, axis=0, keepdims=True)

WAYS = ((2, 1, 0), (1, 2, 0), (2, 1, 0), (2, 1, 0), (2, 0), (1, 0), (2, 1, 0), (1, 2, 0), (0,), (2, 0), (2, 1, 0), (2, 0))
FIRST = (2, 1, 0, 3, 6, 7, 11, 5, 10, 4, 9, 8)
PARTS = ((0, 0, 384), (1, 0, 384), (2, 0, 384), (3, 0, 384), (4, 0, 384), (5, 0, 384), (6, 0, 384), (7, 0, 384), (8, 0, 128), (8, 128, 128), (8, 256, 128), (9, 0, 384), (10, 0, 128), (10, 128, 128), (10, 256, 128), (11, 0, 128), (11, 128, 128), (11, 256, 128))
ORDERS = ((0, 2, 3, 1), (0, 2, 3, 1), (0, 1, 2, 3), (0, 1, 2, 3), (0, 2, 1, 3), (0, 1, 2, 3), (0, 2, 1, 3), (0, 2, 1, 3), (0, 2, 1, 3), (0, 2, 1, 3), (0, 2, 1, 3), (0, 1, 2, 3), (0, 1, 2, 3), (0, 1, 2, 3), (0, 1, 2, 3), (0, 1, 2, 3), (0, 1, 2, 3), (0, 1, 2, 3))
LATE = (0, 1, 4, 5, 7, 11)
SEQUENCE = (0, 1, 2, 3, 4, 5, 6, 7, 9, 10, 11, 8)
FIRST_EXPAND = 4
DIRECT = ()
DIRECT_WIDTH = 128
PLAN = {
    "attend": ((2, (2,)), (3, (1, 0, 2, 3, 1, 6, 0, 7, 3, 2, 2, 11, 1, 0, 6, 1, 7, 0)), (4, (5,)), (5, (10, 11, 3)), (6, (11,)), (7, (3, 4, 7)),),
    "norm1": ((0, (6,)), (1, (7, 10)), (2, (6, 9)), (3, (5,)),),
    "own": ((0, (4, 5)), (1, (4, 10)), (2, (9, 10, 8)), (3, (9, 8)),),
    "dw2": ((0, (20,)), (1, (21,)), (2, (20, 22)), (3, (21, 23)),),
    "back": ((0, (22, 23)), (1, (20,)), (3, (21, 22)),),
    "dw1": ((0, (24,)), (1, (25, 23)), (2, (24, 26)), (3, (25, 27, 22, 20)),),
    "attb": ((0, (26,)), (1, (27, 23)), (2, (21,)), (5, (20,)), (6, (24,)), (7, (22,)),),
    "dwq": ((0, (31, 20, 21, 25, 26)), (1, (32, 33, 34)), (2, (31, 32, 33, 34, 35, 36, 37, 20, 21, 22, 24, 27, 40)),),
    "dwo": ((0, (35, 36, 37, 28, 29, 30, 21, 23, 25, 40)),),
    "gin": ((0, (28, 29, 30, 24, 26)), (1, (20, 35, 25)), (2, (22,)), (3, (31, 36)),),
    "tail": ((0, (21, 37, 32, 40, 20, 23, 26, 22, 33, 20, 24, 25, 34, 31, 21, 23, 40, 32, 21, 26, 27, 31, 24, 22, 28, 23, 33, 25, 32, 22, 34, 29, 40, 28, 27, 33, 26, 30, 24, 25, 35, 31, 34, 32, 36, 29, 37, 27, 30, 23, 33, 28, 23, 31, 26, 34, 24, 32, 35, 36, 37, 27, 24, 33, 25, 28, 29, 31, 34, 30, 35, 25, 36, 37, 27, 28, 26, 29, 32, 30, 33, 35, 34, 26, 36, 31, 37, 28, 29, 32, 31, 30, 27, 33, 32, 35, 36, 34, 37, 29, 27, 33, 30, 34, 28, 35, 28, 36, 29, 35, 37, 30, 36, 29, 37, 30)),),
}


def kernel(
    bits,
    x_hbm, cot_hbm, seg_ref, pad_ref, qb_ref, vb_ref, eb_ref, ob_ref, g1_ref, s1_ref, rb_ref, g2_ref, s2_ref,
    wq_hbm, wk_hbm, wv_hbm, wo_hbm, w1_hbm, w2_hbm,
    out_hbm, gin_hbm, grad_hbm, vec_out,
    x_ref, wqkv, wo, w1, w2, hv, A, probs, normed, spread, acc, FL, FLT, GT, bias, stage, cot, sums, got, hsum,
    R0, R1, RB, R2, R3, R4, RX, RD,
    lsem, osem, fsem, wsend, wrecv, gsend, grecv, vsend, vrecv, bsem, psem, dsend, drecv,
):
    t = lax.axis_index("tensor")
    me = lax.axis_index("dp")
    bit = [lax.rem(me // (1 << i), 2) for i in range(bits)]
    split = min(bits, 4)

    def mate(i):
        return (me + (1 << i) * (1 - 2 * bit[i]), t)

    across = (me, 1 - t)
    partners = [across] + [mate(i) for i in range(bits)]

    barrier = pltpu.get_barrier_semaphore()
    for who in partners:
        pl.semaphore_signal(barrier, inc=1, device_id=who, device_id_type=MESH)

    locals_ = [
        (x_hbm, x_ref),
        (wq_hbm, wqkv.at[t, :, pl.ds(0, HALF)]),
        (wk_hbm, wqkv.at[t, :, pl.ds(HALF, HALF)]),
        (wv_hbm, wqkv.at[t, :, pl.ds(2 * HALF, HALF)]),
        (wo_hbm, wo.at[t]),
        (w1_hbm, w1.at[t]),
        (w2_hbm, w2.at[t]),
    ]
    loads = [pltpu.make_async_copy(s, d, lsem.at[i]) for i, (s, d) in enumerate(locals_)]
    for cp in loads:
        cp.start()

    def row(ref):
        return ref[...].astype(F32).reshape(1, ref.shape[0])

    hv[t] = jnp.zeros((8, HIDDEN), F32)
    hv[t, 0:1, :] = row(eb_ref)
    hv[t, 1:2, 0:HALF] = row(qb_ref)
    hv[t, 1:2, HALF : 2 * HALF] = row(vb_ref)
    out_b, gain1, shift1 = row(ob_ref), row(g1_ref), row(s1_ref)
    red_b, gain2, shift2 = row(rb_ref), row(g2_ref), row(s2_ref)
    sums[0] = jnp.zeros((24, HALF), F32)
    hsum[...] = jnp.zeros_like(hsum)
    lane = lax.broadcasted_iota(jnp.int32, (1, 128), 1)
    low = lane < 64
    mask0 = jnp.where(low, 1.0, 0.0).astype(BF)
    mask1 = jnp.where(low, 0.0, 1.0).astype(BF)
    sc0 = jnp.where(low, 0.125, 0.0).astype(BF)
    sc1 = jnp.where(low, 0.0, 0.125).astype(BF)

    for b in range(BLOCKS):
        for wi in range(2):
            cols = pl.ds(pl.multiple_of(t * ROWS + wi * WIN, WIN), WIN)
            seg = jnp.broadcast_to(seg_ref[b : b + 1, cols].astype(F32), (WIN, WIN))
            live = jnp.broadcast_to(pad_ref[b : b + 1, cols].astype(F32), (WIN, WIN))
            bias[2 * b + wi] = jnp.where((seg == seg.T) & (live.T > 0.5), 0.0, -1e30)

    pl.semaphore_wait(barrier, len(partners))

    def part_rows(base, n, ways, fixed):
        size = n // (1 << len(ways))
        at_ = sum((bit[w] * (size << j) for j, w in enumerate(ways)), 0)
        free = len(ways) - fixed
        at_ = sum((bit[w] * (size << j) for j, w in enumerate(ways) if j >= free), 0)
        return pl.ds(pl.multiple_of(base + at_, 16), size << free)

    def cols(i):
        return pl.ds(i * HALF, HALF)

    every = pl.ds(0, WIDTH)
    pieces = [(src, every, wqkv, cols(i), 0, WIDTH) for i, src in enumerate((wq_hbm, wk_hbm, wv_hbm))]
    pieces = [(src, pl.ds(0, HALF), dst, c, base, n) for src, _, dst, c, base, n in pieces]
    pieces += [(wo_hbm, every, wo, every, 0, HALF)]
    pieces += [(w1_hbm, cols(i), w1, cols(i), 0, WIDTH) for i in range(4)]
    pieces += [(w2_hbm, every, w2, every, i * HALF, HALF) for i in range(4)]

    def weight_copy(g, s):
        hbm, hc, dst, dc, base, n = pieces[g]
        ways = WAYS[g]
        r = part_rows(base, n, ways, len(ways) - max(s - 1, 0))
        if s == 0:
            src, to, who = hbm.at[r, hc], dst.at[t, r, dc], across
        else:
            src = to = dst.at[1 - t, r, dc]
            who = mate(ways[s - 1])
        return pltpu.make_async_remote_copy(
            src_ref=src, dst_ref=to, send_sem=wsend.at[s, g], recv_sem=wrecv.at[s, g],
            device_id=who, device_id_type=MESH,
        )

    wplace = [0] * len(pieces)

    def adv_weight(g):
        s, last = wplace[g], len(WAYS[g])
        if s > 0:
            weight_copy(g, s - 1).wait()
        if s <= last:
            weight_copy(g, s).start()
        wplace[g] = s + 1

    def weights_ready(which):
        while min(wplace[g] - len(WAYS[g]) for g in which) < 2:
            for g in which:
                if wplace[g] < len(WAYS[g]) + 2:
                    adv_weight(g)

    bias_copy = pltpu.make_async_remote_copy(
        src_ref=hv.at[t], dst_ref=hv.at[t], send_sem=bsem.at[0], recv_sem=bsem.at[1],
        device_id=across, device_id_type=MESH,
    )
    bias_copy.start()
    for g in FIRST:
        adv_weight(g)

    def run(ops):
        for op in ops:
            if op < 20:
                adv_weight(op)
            elif op < 40:
                adv(op - 20)
            else:
                adv_vec()

    def at(loop_index, step, action):
        @pl.when(loop_index == step)
        def _():
            action()

    def hook(name, loop_index=None):
        for step, ops in PLAN.get(name, ()):
            if loop_index is None:
                run(ops)
            else:
                at(loop_index, step, lambda ops=ops: run(ops))

    def stacked(a, m0, m1):
        return jnp.concatenate([a * m0, a * m1], axis=0)

    def block_rows(b):
        return pl.ds(pl.multiple_of(b * ROWS, ROWS), ROWS)

    for cp in loads[:4]:
        cp.wait()

    def attend(i, carry):
        b = lax.rem(i, BLOCKS)
        h = t + (i // BLOCKS) * (1 - 2 * t)
        rows = block_rows(b)
        pr = mm(x_ref[b], wqkv[h])
        q = (pr[:, :HALF] + hv[h, 1:2, 0:HALF]).astype(BF)
        k = pr[:, HALF : 2 * HALF].astype(BF)
        v = (pr[:, 2 * HALF :] + hv[h, 1:2, HALF : 2 * HALF]).astype(BF)
        A[9, h, rows, :] = q
        A[10, h, rows, :] = k
        A[11, h, rows, :] = v
        units = [(wi, p) for wi in range(2) for p in range(3)]
        for g in range(0, 6, 6):
            part = units[g : g + 6]
            scores = []
            for wi, p in part:
                r, c = slice(wi * WIN, (wi + 1) * WIN), slice(p * 128, (p + 1) * 128)
                bb = bias[b * 2 + wi]
                scores.append(mm_nt(k[r, c], stacked(q[r, c], sc0, sc1)) + jnp.concatenate([bb, bb], axis=1))
            expo = [jnp.exp(s - jnp.max(s, axis=0, keepdims=True)) for s in scores]
            pbs = [(e * (1.0 / jnp.sum(e, axis=0, keepdims=True))).astype(BF) for e in expo]
            for (wi, p), pb in zip(part, pbs):
                r, c = slice(wi * WIN, (wi + 1) * WIN), slice(p * 128, (p + 1) * 128)
                probs[b * 2 + wi, h, p] = pb
                o = mm_tn(pb, v[r, c])
                o = jnp.where(low, o[:WIN], o[WIN:])
                A[8, h, pl.ds(pl.multiple_of(b * ROWS + wi * WIN, WIN), WIN), c] = o.astype(BF)

        hook("attend", i)
        at(i, 3, own_done)
        return carry

    def own_done():
        weights_ready([0, 1, 2])
        bias_copy.wait()

    lax.fori_loop(0, 2 * BLOCKS, attend, 0)

    def joined(k, rows):
        return jnp.concatenate([A[k, 0, rows, :], A[k, 1, rows, :]], axis=1)

    def normalize(hidden):
        center = hidden - row_mean(hidden)
        rs = lax.rsqrt(row_mean(center * center) + EPS)
        return center * rs, rs

    def add_vec(row, value):
        sums[0, row : row + 1, :] += value[:, :HALF]
        sums[0, row + 1 : row + 2, :] += value[:, HALF:]


    loads[4].wait()
    hook("pre_norm")
    weights_ready([3])

    def first_norm(b, carry):
        rows = block_rows(b)
        mixed = joined(8, rows)
        att = mm(mixed[:, :HALF], wo[0]) + mm(mixed[:, HALF:], wo[1])
        n, rs = normalize(x_ref[b].astype(F32) + att + out_b)
        normed[rows, :] = n
        spread[rows, :] = rs
        first = n * gain1 + shift1
        FL[0, rows, :] = first[:, :HALF].astype(BF)
        FL[1, rows, :] = first[:, HALF:].astype(BF)
        hook("norm1", b)
        return carry

    lax.fori_loop(0, BLOCKS, first_norm, 0)
    loads[5].wait()
    loads[6].wait()

    def low_rows(rows):
        return jnp.concatenate([FL[0, rows, :], FL[1, rows, :]], axis=1)

    def half_feed(b, h):
        rows = block_rows(b)
        inner_all = mm(low_rows(rows), w1[h]) + hv[h, 0:1, :]
        acts = []
        for k in range(4):
            inner = inner_all[:, k * HALF : (k + 1) * HALF]
            phi = 0.5 + 0.5 * lax.erf(inner * 0.7071067811865476)
            slope = phi + inner * jnp.exp(-0.5 * inner * inner) * 0.3989422804014327
            act = (inner * phi).astype(BF)
            A[k, h, rows, :] = act
            A[4 + k, h, rows, :] = slope.astype(BF)
            acts.append(act)
        return mm(jnp.concatenate(acts, axis=1), w2[h])

    def cot_copy(b):
        return pltpu.make_async_copy(cot_hbm.at[b], cot.at[lax.rem(b, 2)], psem.at[lax.rem(b, 2)])

    cot_copy(0).start()
    cot_copy(1).start()

    def feed_own(b, carry):
        acc[block_rows(b), :] = half_feed(b, t)
        hook("own", b)
        return carry

    lax.fori_loop(0, BLOCKS, feed_own, 0)
    hook("pre_other")
    weights_ready([4, 5, 6, 7, 8, 9, 10, 11])

    def second_norm(b, carry):
        rows = block_rows(b)
        red = acc[rows, :] + half_feed(b, 1 - t)
        n, rs = normalize(normed[rows, :] * gain1 + shift1 + red + red_b)
        slot = lax.rem(b, 2)

        @pl.when(b >= 2)
        def _():
            pltpu.make_async_copy(stage.at[slot], out_hbm.at[b - 2], osem.at[slot]).wait()

        stage[slot] = n * gain2 + shift2
        pltpu.make_async_copy(stage.at[slot], out_hbm.at[b], osem.at[slot]).start()
        cot_copy(b).wait()
        c = cot[slot].astype(F32)

        @pl.when(b + 2 < BLOCKS)
        def _():
            cot_copy(b + 2).start()

        add_vec(14, col_sum(c))
        add_vec(12, col_sum(c * n))
        u = c * gain2
        gs = rs * (u - row_mean(u) - n * row_mean(u * n))
        add_vec(10, col_sum(gs))
        acc[rows, :] = gs
        return carry

    lax.fori_loop(0, BLOCKS, second_norm, 0)
    for b in range(2):
        pltpu.make_async_copy(stage.at[b], out_hbm.at[b + 2], osem.at[b]).wait()

    def span(i):
        return WIDTH >> (i + 1)

    def lo(j, i):
        return sum((bit[ORDERS[j][n]] * span(n) for n in range(i + 1)), 0)

    def ds(at_, n):
        return pl.ds(pl.multiple_of(at_, 16), n)

    def held(j, h, r):
        k, first, width = PARTS[j]
        if k < 9:
            return A, (k, h, r, pl.ds(first, width))
        return w1, (h, r, pl.ds((k - 9) * HALF + first, width))

    def add_in(j, h, r, value):
        ref, at_ = held(j, h, r)
        ref[at_] = ref[at_] + value

    def view(j, h, r):
        ref, at_ = held(j, h, r)
        return ref.at[at_]

    def landing(j, p):
        k, first, width = PARTS[j]
        c = pl.ds(first, width)
        if p == 0:
            return R0, (SEQUENCE.index(k) % 4, slice(None), slice(None), c)
        if p == 1 and k in LATE:
            return RB, (LATE.index(k), slice(None), slice(None), c)
        if p == 1:
            return R1, (k - sum(n < k for n in LATE), slice(None), c)
        return (R2, R3, R4)[p - 2], (k, slice(None), c)

    halves = [("half", i) for i in range(1, split)]
    swaps_ = [("swap", i) for i in range(bits - split)]
    gathers = [("gather", i) for i in reversed(range(1, split))]

    def names_of(j):
        if j in DIRECT:
            mid = [("spread", 0)] + swaps_ + [("share", 0)]
        else:
            mid = halves + swaps_ + gathers
        if PARTS[j][0] in LATE:
            return [("core", 0), ("both", 1), ("tensor", 1)] + mid[1:] + [("gather", 0)]
        return [("core", 0), ("tensor", 0)] + mid + [("gather", 0)]

    others = range(1, 1 << (split - 1))

    def peer(p):
        step = sum(((1 << (n + 1)) * (1 - 2 * bit[n + 1]) for n in range(split - 1) if p >> n & 1), 0)
        place_ = sum(
            ((1 - bit[n + 1] if p >> n & 1 else bit[n + 1]) * span(n + 1) for n in range(split - 1)), bit[0] * span(0)
        )
        return (me + step, t), ds(place_, span(split - 1))

    def peer_copy(j, s, p):
        kind, _ = names_of(j)[s]
        k, first, width = PARTS[j]
        who, r = peer(p)
        n = DIRECT.index(j)
        if kind == "spread":
            src, dst, m = view(j, t, r), RD.at[n, p - 1, :, pl.ds(0, width)], 0
        else:
            r = ds(lo(j, split - 1), span(split - 1))
            src, dst, m = view(j, t, r), grad_hbm.at[k, r, pl.ds(first, width)], 1
        return pltpu.make_async_remote_copy(
            src_ref=src, dst_ref=dst, send_sem=dsend.at[2 * n + m, p - 1], recv_sem=drecv.at[2 * n + m, p - 1],
            device_id=who, device_id_type=MESH,
        )

    def begin(j, s):
        if names_of(j)[s][0] in ("spread", "share"):
            for p in others:
                peer_copy(j, s, p).start()
        else:
            piece_copy(j, s).start()

    def piece_copy(j, s):
        kind, i = names_of(j)[s]
        way = ORDERS[j]
        k, first, width = PARTS[j]
        if kind == "core":
            src, who = view(j, slice(None), ds((1 - bit[way[0]]) * span(0), span(0))), mate(way[0])
            land, at_ = landing(j, 0)
            dst = land.at[at_]
        elif kind == "tensor":
            src, who = view(j, 1 - t, ds(lo(j, i), span(i))), across
            land, at_ = landing(j, i + 1)
            dst = land.at[at_]
        elif kind == "both":
            src, who = view(j, slice(None), ds(lo(j, 0) + (1 - bit[way[1]]) * span(1), span(1))), mate(way[1])
            land, at_ = landing(j, 1)
            dst = land.at[at_]
        elif kind == "half":
            src = view(j, t, ds(lo(j, i - 1) + (1 - bit[way[i]]) * span(i), span(i)))
            who = mate(way[i])
            land, at_ = landing(j, i + 1)
            dst = land.at[at_]
        elif kind == "swap":
            src, who = view(j, t, ds(lo(j, split - 1), span(split - 1))), mate(split + i)
            dst = RX.at[i, k, :, pl.ds(first, width)]
        else:
            r = ds(lo(j, i), span(i))
            dst, who = grad_hbm.at[k, r, pl.ds(first, width)], mate(way[i])
            src = view(j, t, r) if i == split - 1 and i > 0 else dst
        return pltpu.make_async_remote_copy(
            src_ref=src, dst_ref=dst, send_sem=gsend.at[s, j], recv_sem=grecv.at[s, j],
            device_id=who, device_id_type=MESH,
        )

    def keep_copy(j):
        k, first, width = PARTS[j]
        r = ds(lo(j, split - 1), span(split - 1))
        return pltpu.make_async_copy(view(j, t, r), grad_hbm.at[k, r, pl.ds(first, width)], fsem.at[j])

    def settle(j, s):
        names = names_of(j)
        kind, i = names[s]
        k, first, width = PARTS[j]
        if kind in ("spread", "share"):
            for p in others:
                peer_copy(j, s, p).wait()
        else:
            piece_copy(j, s).wait()
        if kind == "core":
            land, at_ = landing(j, 0)
            add_in(j, slice(None), ds(lo(j, 0), span(0)), land[at_])
        elif kind == "tensor":
            land, at_ = landing(j, i + 1)
            add_in(j, t, ds(lo(j, i), span(i)), land[at_])
        elif kind == "both":
            land, at_ = landing(j, 1)
            add_in(j, slice(None), ds(lo(j, 1), span(1)), land[at_])
        elif kind == "half":
            land, at_ = landing(j, i + 1)
            add_in(j, t, ds(lo(j, i), span(i)), land[at_])
        elif kind == "spread":
            total = None
            for p in others:
                piece = RD[DIRECT.index(j), p - 1, :, 0:width].astype(F32)
                total = piece if total is None else total + piece
            ref, at_ = held(j, t, ds(lo(j, split - 1), span(split - 1)))
            ref[at_] = (ref[at_].astype(F32) + total).astype(BF)
        elif kind == "swap":
            add_in(j, t, ds(lo(j, split - 1), span(split - 1)), RX[i, k, :, pl.ds(first, width)])
        elif kind == "share" or i == split - 1:
            keep_copy(j).wait()
        if s + 1 < len(names) and names[s + 1] in (("gather", split - 1), ("share", 0)):
            keep_copy(j).start()

    place = [0] * len(PARTS)

    def adv(*which):
        for k in which:
            s = place[k]
            names = names_of(k)
            if s > len(names):
                continue
            if s > 0:
                settle(k, s - 1)
            if s < len(names):
                begin(k, s)
            place[k] = s + 1

    swaps = [across] + [mate(i) for i in range(bits)]
    vec_place = [0]

    def adv_vec():
        s = vec_place[0]

        def cp(j):
            return pltpu.make_async_remote_copy(
                src_ref=sums.at[j], dst_ref=got.at[j], send_sem=vsend.at[j], recv_sem=vrecv.at[j],
                device_id=swaps[j], device_id_type=MESH,
            )

        if s > len(swaps):
            return
        if s > 0:
            cp(s - 1).wait()
            sums[s] = sums[s - 1] + got[s - 1]
        if s < len(swaps):
            cp(s).start()
        vec_place[0] = s + 1

    def transpose_into(dst, get):
        for b in range(BLOCKS):
            dst[:, b * ROWS : (b + 1) * ROWS] = get(b).T

    def rows_of(b):
        return slice(b * ROWS, (b + 1) * ROWS)

    def chunk_loop(name, first, count, left):
        def one(j, carry):
            k = first + j
            full = mm(left[...], joined(k, slice(None)))
            for h in range(2):
                part = full[:, h * HALF : (h + 1) * HALF].astype(BF)
                if first < 9:
                    A[k, h, 0:WIDTH, :] = part
                else:
                    w1[h, :, pl.ds(pl.multiple_of(j * HALF, HALF), HALF)] = part
            hook(name, j)
            return carry

        if count:
            lax.fori_loop(0, count, one, 0)

    transpose_into(GT, lambda b: acc[rows_of(b), :].astype(BF))
    chunk_loop("dw2", 0, 4, GT)
    transpose_into(FLT, lambda b: low_rows(rows_of(b)))
    hook("mid")

    def feed_back(b, carry):
        rows = block_rows(b)
        gs = acc[rows, :]
        gl = gs.astype(BF)
        gf = gs
        for h in range(2):
            da = mm_nt(gl, w2[h])
            gis = []
            for k in range(4):
                gi = (da[:, k * HALF : (k + 1) * HALF] * A[4 + k, h, rows, :].astype(F32)).astype(BF)
                A[4 + k, h, rows, :] = gi
                sums[0, 16 + 4 * h + k : 17 + 4 * h + k, :] += col_sum(gi.astype(F32))
                gis.append(gi)
            gf = gf + mm_nt(jnp.concatenate(gis, axis=1), w1[h])
        n = normed[rows, :]
        add_vec(6, col_sum(gf * n))
        add_vec(8, col_sum(gf))
        u = gf * gain1
        gh = spread[rows, :] * (u - row_mean(u) - n * row_mean(u * n))
        add_vec(4, col_sum(gh))
        acc[rows, :] = gh
        gm = gh.astype(BF)
        FL[0, rows, :] = mm_nt(gm, wo[0]).astype(BF)
        FL[1, rows, :] = mm_nt(gm, wo[1]).astype(BF)
        hook("back", b)
        return carry

    lax.fori_loop(0, BLOCKS, feed_back, 0)
    transpose_into(GT, lambda b: x_ref[b])
    chunk_loop("dw1", 4, FIRST_EXPAND, FLT)

    def attend_back(i, carry):
        h, b = i // BLOCKS, lax.rem(i, BLOCKS)

        def rows_at(wi):
            return pl.ds(pl.multiple_of(b * ROWS + wi * WIN, WIN), WIN)

        def at_(p):
            return slice(p * 128, (p + 1) * 128)

        sums_ = {}
        units = [(wi, p) for p in range(3) for wi in range(2)]
        for g in range(0, 6, 6):
            part = units[g : g + 6]
            do2 = [stacked(FL[h, rows_at(wi), at_(p)], mask0, mask1) for wi, p in part]
            dp = [mm_nt(A[11, h, rows_at(wi), at_(p)], d) for (wi, p), d in zip(part, do2)]
            dv = [mm(probs[b * 2 + wi, h, p], d).astype(BF) for (wi, p), d in zip(part, do2)]
            pf = [probs[b * 2 + wi, h, p].astype(F32) for wi, p in part]
            dsc = [(f * (d - jnp.sum(f * d, axis=0, keepdims=True))).astype(BF) for f, d in zip(pf, dp)]
            dk = [mm(d, stacked(A[9, h, rows_at(wi), at_(p)], sc0, sc1)).astype(BF) for (wi, p), d in zip(part, dsc)]
            dq = [mm_tn(d, A[10, h, rows_at(wi), at_(p)]) for (wi, p), d in zip(part, dsc)]
            for (wi, p), q_, k_, v_ in zip(part, dq, dk, dv):
                q_ = (jnp.where(low, q_[:WIN], q_[WIN:]) * 0.125).astype(BF)
                A[9, h, rows_at(wi), at_(p)] = q_
                A[10, h, rows_at(wi), at_(p)] = k_
                A[11, h, rows_at(wi), at_(p)] = v_
                add = col_sum(q_.astype(F32)), col_sum(v_.astype(F32))
                sums_[p] = add if p not in sums_ else (sums_[p][0] + add[0], sums_[p][1] + add[1])
        for p in range(3):
            hsum[h, 0:1, at_(p)] += sums_[p][0]
            hsum[h, 1:2, at_(p)] += sums_[p][1]
        hook("attb", i)
        return carry

    lax.fori_loop(0, 2 * BLOCKS, attend_back, 0)
    for h in range(2):
        sums[0, h : h + 1, :] = hsum[h, 0:1, :]
        sums[0, 2 + h : 3 + h, :] = hsum[h, 1:2, :]
    adv_vec()
    chunk_loop("dwq", 9, 3, GT)
    chunk_loop("dw1b", 4 + FIRST_EXPAND, 4 - FIRST_EXPAND, FLT)
    transpose_into(FLT, lambda b: acc[rows_of(b), :].astype(BF))
    chunk_loop("dwo", 8, 1, FLT)

    def input_grad(b, carry):
        rows = block_rows(b)
        g = acc[rows, :]
        for h in range(2):
            gp = jnp.concatenate([A[9 + i, h, rows, :] for i in range(3)], axis=1)
            g = g + mm_nt(gp, wqkv[h])
        slot = lax.rem(b, 2)

        @pl.when(b >= 2)
        def _():
            pltpu.make_async_copy(stage.at[slot], gin_hbm.at[b - 2], osem.at[slot]).wait()

        stage[slot] = g
        pltpu.make_async_copy(stage.at[slot], gin_hbm.at[b], osem.at[slot]).start()
        hook("gin", b)
        return carry

    lax.fori_loop(0, BLOCKS, input_grad, 0)
    hook("tail")
    for b in range(2):
        pltpu.make_async_copy(stage.at[b], gin_hbm.at[b + 2], osem.at[b]).wait()
    left = lambda: [j for j in range(len(PARTS)) if place[j] <= len(names_of(j))]
    while left():
        adv_vec()
        adv(*left())
    while vec_place[0] <= len(swaps):
        adv_vec()
    vec_out[...] = sums[len(swaps)]


def layer(n_dp, *operands):
    vm = pl.BlockSpec(memory_space=pltpu.VMEM)
    hbm = pl.BlockSpec(memory_space=pl.ANY)
    bits = n_dp.bit_length() - 1
    split = min(bits, 4)
    stages = 1 + bits + split
    dma = pltpu.SemaphoreType.DMA
    return pl.pallas_call(
        functools.partial(kernel, bits),
        out_shape=(
            jax.ShapeDtypeStruct((BLOCKS, ROWS, WIDTH), F32),
            jax.ShapeDtypeStruct((BLOCKS, ROWS, WIDTH), F32),
            jax.ShapeDtypeStruct((CHUNKS, WIDTH, HALF), BF),
            jax.ShapeDtypeStruct((24, HALF), F32),
        ),
        in_specs=[hbm, hbm] + [vm] * 11 + [hbm] * 6,
        out_specs=(hbm, hbm, hbm, vm),
        scratch_shapes=[
            pltpu.VMEM((BLOCKS, ROWS, WIDTH), BF),
            pltpu.VMEM((2, WIDTH, 3 * HALF), BF),
            pltpu.VMEM((2, HALF, WIDTH), BF),
            pltpu.VMEM((2, WIDTH, HIDDEN), BF),
            pltpu.VMEM((2, HIDDEN, WIDTH), BF),
            pltpu.VMEM((2, 8, HIDDEN), F32),
            pltpu.VMEM((CHUNKS, 2, TOTAL, HALF), BF),
            pltpu.VMEM((2 * BLOCKS, 2, 3, WIN, 2 * WIN), BF),
            pltpu.VMEM((TOTAL, WIDTH), F32),
            pltpu.VMEM((TOTAL, 1), F32),
            pltpu.VMEM((TOTAL, WIDTH), F32),
            pltpu.VMEM((2, TOTAL, HALF), BF),
            pltpu.VMEM((WIDTH, TOTAL), BF),
            pltpu.VMEM((WIDTH, TOTAL), BF),
            pltpu.VMEM((2 * BLOCKS, WIN, WIN), F32),
            pltpu.VMEM((2, ROWS, WIDTH), F32),
            pltpu.VMEM((2, ROWS, WIDTH), BF),
            pltpu.VMEM((bits + 2, 24, HALF), F32),
            pltpu.VMEM((bits + 1, 24, HALF), F32),
            pltpu.VMEM((2, 8, HALF), F32),
            pltpu.VMEM((4, 2, WIDTH // 2, HALF), BF),
            pltpu.VMEM((CHUNKS - len(LATE), WIDTH // 2, HALF), BF),
            pltpu.VMEM((max(len(LATE), 1), 2, WIDTH // 4, HALF), BF),
            pltpu.VMEM((CHUNKS, WIDTH // 4, HALF), BF),
            pltpu.VMEM((CHUNKS, WIDTH // 8, HALF), BF),
            pltpu.VMEM((CHUNKS, WIDTH // 16, HALF), BF),
            pltpu.VMEM((max(bits - split, 1), CHUNKS, WIDTH >> split, HALF), BF),
            pltpu.VMEM((max(len(DIRECT), 1), 7, WIDTH >> split, DIRECT_WIDTH), BF),
            dma((7,)),
            dma((2,)),
            dma((len(PARTS),)),
            dma((4, 12)),
            dma((4, 12)),
            dma((stages, len(PARTS))),
            dma((stages, len(PARTS))),
            dma((bits + 1,)),
            dma((bits + 1,)),
            dma((2,)),
            dma((2,)),
            dma((2 * max(len(DIRECT), 1), 7)),
            dma((2 * max(len(DIRECT), 1), 7)),
        ],
        compiler_params=pltpu.CompilerParams(
            vmem_limit_bytes=67043328, collective_id=0, has_side_effects=True
        ),
    )(*operands)


def finish_kernel(
    grad_hbm, out_low, gin_low, vec, outg, ging, wqg, wkg, wvg, wog, w1g, w2g, qbg, vbg, obg, g1g, s1g, ebg, rbg, g2g, s2g,
    low, wide, turned, rows, isem, osem, rsem, ssem,
):
    t = lax.axis_index("tensor")
    fetch = [pltpu.make_async_copy(grad_hbm.at[k], low.at[k], isem.at[k]) for k in range(CHUNKS)]
    order = list(range(9, 12)) + list(range(4, 8)) + [8] + list(range(4))
    for k in order:
        fetch[k].start()
    passed = []
    for i, ref in enumerate((out_low, gin_low)):
        cp = pltpu.make_async_copy(ref, rows.at[i], rsem.at[i])
        cp.start()
        passed.append(cp)

    def pick(r):
        return jnp.where(t == 0, vec[r : r + 1, :], vec[r + 1 : r + 2, :]).reshape(HALF)

    def whole(r):
        return jnp.concatenate([vec[r : r + 1, :], vec[r + 1 : r + 2, :]], axis=1).reshape(WIDTH)

    qbg[...] = pick(0)
    vbg[...] = pick(2)
    for ref, r in ((obg, 4), (g1g, 6), (s1g, 8), (rbg, 10), (g2g, 12), (s2g, 14)):
        ref[...] = whole(r)
    lines = [jnp.where(t == 0, vec[16 + k : 17 + k, :], vec[20 + k : 21 + k, :]) for k in range(4)]
    ebg[...] = jnp.concatenate(lines, axis=1).reshape(HIDDEN)

    sends = []
    for k in order:
        fetch[k].wait()
        if k >= 9:
            wide[k - 5] = low[k].astype(F32)
            src, dst = wide.at[k - 5], (wqg, wkg, wvg)[k - 9]
        elif k >= 4 and k < 8:
            wide[k - 4] = low[k].astype(F32)
            src, dst = wide.at[k - 4], w1g.at[:, pl.ds((k - 4) * HALF, HALF)]
        elif k == 8:
            turned[4] = low[k].astype(F32).T
            src, dst = turned.at[4], wog
        else:
            turned[k] = low[k].astype(F32).T
            src, dst = turned.at[k], w2g.at[pl.ds(k * HALF, HALF), :]
        cp = pltpu.make_async_copy(src, dst, osem.at[k])
        cp.start()
        sends.append(cp)
    for i, ref in enumerate((outg, ging)):
        passed[i].wait()
        cp = pltpu.make_async_copy(rows.at[i], ref, ssem.at[i])
        cp.start()
        sends.append(cp)
    for cp in sends:
        cp.wait()


def finish(out, gin, grads, vec):
    vm = pl.BlockSpec(memory_space=pltpu.VMEM)
    hbm = pl.BlockSpec(memory_space=pltpu.HBM)
    f = lambda *shape: jax.ShapeDtypeStruct(shape, F32)
    return pl.pallas_call(
        finish_kernel,
        out_shape=(f(BLOCKS, ROWS, WIDTH), f(BLOCKS, ROWS, WIDTH), f(WIDTH, HALF), f(WIDTH, HALF), f(WIDTH, HALF), f(HALF, WIDTH), f(WIDTH, HIDDEN), f(HIDDEN, WIDTH),
                   f(HALF), f(HALF), f(WIDTH), f(WIDTH), f(WIDTH), f(HIDDEN), f(WIDTH), f(WIDTH), f(WIDTH)),
        in_specs=[hbm, hbm, hbm, vm],
        out_specs=(hbm,) * 8 + (vm,) * 9,
        scratch_shapes=[
            pltpu.VMEM((CHUNKS, WIDTH, HALF), BF),
            pltpu.VMEM((7, WIDTH, HALF), F32),
            pltpu.VMEM((5, HALF, WIDTH), F32),
            pltpu.VMEM((2, BLOCKS, ROWS, WIDTH), F32),
            pltpu.SemaphoreType.DMA((CHUNKS,)),
            pltpu.SemaphoreType.DMA((CHUNKS,)),
            pltpu.SemaphoreType.DMA((2,)),
            pltpu.SemaphoreType.DMA((2,)),
        ],
        compiler_params=pltpu.CompilerParams(vmem_limit_bytes=50 * 1024 * 1024),
    )(grads, out, gin, vec)


def local(
    n_dp, inputs, segments, padding, query_weight, query_bias, key_weight, value_weight, value_bias,
    output_weight, output_bias, first_gain, first_shift, expand_weight, expand_bias,
    reduce_weight, reduce_bias, second_gain, second_shift, cotangent,
):
    out, gin, grads, vec = layer(
        n_dp, inputs, cotangent, segments, padding, query_bias, value_bias, expand_bias, output_bias, first_gain,
        first_shift, reduce_bias, second_gain, second_shift, query_weight, key_weight, value_weight,
        output_weight, expand_weight, reduce_weight,
    )
    out, gin, wq, wk, wv, wo, w1, w2, qb, vb, ob, g1, s1, eb, rb, g2, s2 = finish(out, gin, grads, vec)
    return (out, gin, wq, qb, wk, wv, vb, wo, ob, g1, s1, w1, eb, w2, rb, g2, s2)


def solution(mesh):
    tokens = P(None, ("dp", "tensor"), None)
    return jax.shard_map(
        functools.partial(local, mesh.shape["dp"]),
        mesh=mesh,
        in_specs=(
            tokens, P(None, "dp"), P(None, "dp"), P(None, "tensor"), P("tensor"), P(None, "tensor"),
            P(None, "tensor"), P("tensor"), P("tensor", None), P(), P(), P(), P(None, "tensor"),
            P("tensor"), P("tensor", None), P(), P(), P(), tokens,
        ),
        out_specs=(
            tokens, tokens, P(None, "tensor"), P("tensor"), P(None, "tensor"), P(None, "tensor"),
            P("tensor"), P("tensor", None), P(), P(), P(), P(None, "tensor"), P("tensor"),
            P("tensor", None), P(), P(), P(),
        ),
        check_vma=False,
    )
```

```python
import functools

import jax
import jax.numpy as jnp
from jax import lax
from jax.experimental import pallas as pl
from jax.experimental.pallas import tpu as pltpu
from jax.sharding import PartitionSpec as P

WIN = 128
BLOCKS = 4
ROWS = 256
TOTAL = BLOCKS * ROWS
WIDTH = 768
HALF = 384
HIDDEN = 1536
CHUNKS = 12
EPS = 1e-12
BF = jnp.bfloat16
F32 = jnp.float32
MESH = pl.DeviceIdType.MESH


def mm(a, b):
    return lax.dot_general(a, b, (((1,), (0,)), ((), ())), preferred_element_type=F32)


def mm_nt(a, b):
    return lax.dot_general(a, b, (((1,), (1,)), ((), ())), preferred_element_type=F32)


def mm_tn(a, b):
    return lax.dot_general(a, b, (((0,), (0,)), ((), ())), preferred_element_type=F32)


def row_mean(a):
    return jnp.sum(a, axis=-1, keepdims=True) * (1.0 / WIDTH)


def col_sum(a):
    return jnp.sum(a, axis=0, keepdims=True)

WAYS = ((1, 2, 0), (2, 1, 0), (2, 1, 0), (2, 1, 0), (2, 1, 0), (2, 1, 0), (2, 0), (0,), (1, 2, 0), (0,), (2, 1, 0), (1, 2, 0))
FIRST = (1, 0, 2, 3, 6, 10, 4, 8, 11, 5, 7, 9)
PARTS = ((0, 0, 384), (1, 0, 384), (2, 0, 384), (3, 0, 384), (4, 0, 384), (5, 0, 384), (6, 0, 384), (7, 0, 384), (8, 0, 128), (8, 128, 128), (8, 256, 128), (9, 0, 384), (10, 0, 384), (11, 0, 128), (11, 128, 128), (11, 256, 128))
ORDERS = ((0, 1, 2, 3), (0, 1, 2, 3), (0, 1, 2, 3), (0, 1, 2, 3), (0, 1, 2, 3), (0, 1, 2, 3), (0, 1, 2, 3), (0, 1, 2, 3), (0, 1, 2, 3), (0, 1, 2, 3), (0, 1, 2, 3), (0, 1, 2, 3), (0, 1, 2, 3), (0, 1, 2, 3), (0, 1, 2, 3), (0, 1, 2, 3))
LATE = (1, 3, 4, 6)
SEQUENCE = (0, 1, 2, 3, 4, 5, 6, 7, 9, 10, 11, 8)
FIRST_EXPAND = 4
DIRECT = ()
DIRECT_WIDTH = 128
PLAN = {
    "attend": ((2, (1,)), (3, (0, 2, 1, 3, 0, 2, 6, 3, 1, 10, 1, 4, 0, 2, 8, 0, 2)), (4, (3, 6, 11)), (5, (3, 5, 8, 10)), (6, (4, 6)), (7, (11,)),),
    "norm1": ((0, (5,)), (2, (10,)), (3, (7,)),),
    "own": ((0, (7, 8, 10)), (1, (4, 8, 11)), (2, (4, 5, 11, 9)), (3, (5, 9)),),
    "dw2": ((0, (20,)), (1, (21,)), (2, (20, 22)), (3, (21, 23)),),
    "back": ((0, (22, 23)), (1, (20, 21)), (3, (21, 22, 23)),),
    "dw1": ((0, (24, 20)), (1, (25,)), (2, (24, 26, 21)), (3, (25, 27, 20, 22, 23)),),
    "attb": ((0, (26,)), (1, (27,)), (2, (21,)), (3, (20, 22)), (5, (23, 24)), (7, (21, 25)),),
    "dwq": ((0, (31, 20)), (1, (32,)), (2, (31, 33, 34, 35, 22, 26, 21, 32, 23)),),
    "dwo": ((0, (33, 34, 35, 28, 29, 30, 20, 25, 27)),),
    "gin": ((0, (28, 29, 30, 22, 24, 40)), (1, (21, 23, 25, 40)), (3, (21, 22)),),
    "tail": ((0, (20, 24, 20, 23, 31, 27, 40, 25, 26, 24, 27, 22, 40, 22, 25, 26, 23, 32, 23, 24, 31, 27, 33, 40, 25, 34, 32, 26, 33, 24, 35, 31, 28, 25, 27, 32, 34, 29, 25, 33, 26, 30, 24, 31, 27, 35, 24, 28, 34, 32, 29, 33, 30, 26, 35, 28, 31, 27, 34, 29, 27, 32, 30, 33, 35, 26, 28, 31, 26, 34, 29, 32, 33, 30, 35, 34, 31, 28, 29, 31, 30, 35, 28, 32, 29, 30, 33, 32, 34, 33, 35, 34, 28, 35, 29, 28, 30, 29, 30)),),
}
LANDED = {
    "c": (0, 1, 2, 3, 0, 1, 2, 3, 0, 5, 6, 0, 1, 2, 3, 4),
    "g0": (8, 7, 7, 8, 8, 7, 8, 7, 8, 9, 7, 7, 8, 9, 7, 10),
    "g1": (12, 11, 13, 14, 12, 11, 14, 13, 14, 17, 18, 11, 12, 15, 16, 13),
    "g2": (20, 19, 21, 22, 20, 19, 22, 21, 19, 24, 25, 19, 20, 23, 21, 22),
    "g3": (27, 26, 28, 29, 27, 26, 29, 28, 31, 26, 32, 26, 27, 30, 28, 29),
    "r1": (35, 33, 36, 34, 37, 34, 33, 35, 36, 38, 39, 36, 33, 34, 37, 35),
    "r2": (41, 40, 42, 43, 41, 40, 43, 42, 45, 40, 41, 40, 41, 44, 42, 43),
    "r3": (47, 46, 48, 49, 47, 46, 49, 48, 51, 46, 52, 46, 47, 50, 48, 49),
    "y": (53, 55, 54, 53, 55, 56, 58, 54, 53, 63, 64, 57, 59, 60, 61, 62),
}
LANDED_COUNT = 65
KEPT = (1, 0, 0, 1, 1, 0, 1, 0, 2, 0, 3, 0, 1, 2, 0, 1)


def kernel(
    bits,
    x_hbm, cot_hbm, seg_hbm, pad_hbm, qb_hbm, vb_hbm, eb_hbm, ob_hbm, g1_hbm, s1_hbm, rb_hbm, g2_hbm, s2_hbm,
    wq_hbm, wk_hbm, wv_hbm, wo_hbm, w1_hbm, w2_hbm,
    out_hbm, gin_hbm, grad_hbm, vec_out,
    seg_ref, pad_ref, qb_ref, vb_ref, eb_ref, ob_ref, g1_ref, s1_ref, rb_ref, g2_ref, s2_ref,
    x_ref, wqkv, wo, w1, w2, hv, A, probs, normed, spread, acc, FL, FLT, GT, bias, stage, cot, sums, got, hsum,
    R0, R1, RB, R2, R3, R4, RX,
    isem, lsem, osem, fsem, wsend, wrecv, gsend, grecv, vsend, vrecv, bsem, psem, xrecv,
):
    t = lax.axis_index("tensor")
    me = lax.axis_index("dp")
    bit = [lax.rem(me // (1 << i), 2) for i in range(bits)]
    split = min(bits, 4)

    def mate(i):
        return (me + (1 << i) * (1 - 2 * bit[i]), t)

    across = (me, 1 - t)
    partners = [across] + [mate(i) for i in range(bits)]

    barrier = pltpu.get_barrier_semaphore()
    for who in partners:
        pl.semaphore_signal(barrier, inc=1, device_id=who, device_id_type=MESH)

    smalls = [
        (seg_hbm, seg_ref),
        (pad_hbm, pad_ref),
        (qb_hbm, qb_ref),
        (vb_hbm, vb_ref),
        (eb_hbm, eb_ref),
        (ob_hbm, ob_ref),
        (g1_hbm, g1_ref),
        (s1_hbm, s1_ref),
        (rb_hbm, rb_ref),
        (g2_hbm, g2_ref),
        (s2_hbm, s2_ref),
    ]
    smalls = [pltpu.make_async_copy(s, d, isem.at[i]) for i, (s, d) in enumerate(smalls)]
    for cp in smalls:
        cp.start()

    locals_ = [
        (x_hbm, x_ref),
        (wq_hbm, wqkv.at[t, :, pl.ds(0, HALF)]),
        (wk_hbm, wqkv.at[t, :, pl.ds(HALF, HALF)]),
        (wv_hbm, wqkv.at[t, :, pl.ds(2 * HALF, HALF)]),
        (wo_hbm, wo.at[t]),
        (w1_hbm, w1.at[t]),
        (w2_hbm, w2.at[t]),
    ]
    loads = [pltpu.make_async_copy(s, d, lsem.at[i]) for i, (s, d) in enumerate(locals_)]
    for cp in loads:
        cp.start()

    for cp in smalls:
        cp.wait()

    def row(ref):
        return ref[...].astype(F32).reshape(1, ref.shape[0])

    hv[t] = jnp.zeros((8, HIDDEN), F32)
    hv[t, 0:1, :] = row(eb_ref)
    hv[t, 1:2, 0:HALF] = row(qb_ref)
    hv[t, 1:2, HALF : 2 * HALF] = row(vb_ref)
    out_b, gain1, shift1 = row(ob_ref), row(g1_ref), row(s1_ref)
    red_b, gain2, shift2 = row(rb_ref), row(g2_ref), row(s2_ref)
    sums[0] = jnp.zeros((24, HALF), F32)
    hsum[...] = jnp.zeros_like(hsum)
    lane = lax.broadcasted_iota(jnp.int32, (1, 128), 1)
    low = lane < 64
    mask0 = jnp.where(low, 1.0, 0.0).astype(BF)
    mask1 = jnp.where(low, 0.0, 1.0).astype(BF)
    sc0 = jnp.where(low, 0.125, 0.0).astype(BF)
    sc1 = jnp.where(low, 0.0, 0.125).astype(BF)

    for b in range(BLOCKS):
        for wi in range(2):
            cols = pl.ds(pl.multiple_of(t * ROWS + wi * WIN, WIN), WIN)
            seg = jnp.broadcast_to(seg_ref[b : b + 1, cols].astype(F32), (WIN, WIN))
            live = jnp.broadcast_to(pad_ref[b : b + 1, cols].astype(F32), (WIN, WIN))
            bias[2 * b + wi] = jnp.where((seg == seg.T) & (live.T > 0.5), 0.0, -1e30)

    pl.semaphore_wait(barrier, len(partners))

    def part_rows(base, n, ways, fixed):
        size = n // (1 << len(ways))
        at_ = sum((bit[w] * (size << j) for j, w in enumerate(ways)), 0)
        free = len(ways) - fixed
        at_ = sum((bit[w] * (size << j) for j, w in enumerate(ways) if j >= free), 0)
        return pl.ds(pl.multiple_of(base + at_, 16), size << free)

    def cols(i):
        return pl.ds(i * HALF, HALF)

    every = pl.ds(0, WIDTH)
    pieces = [(src, every, wqkv, cols(i), 0, WIDTH) for i, src in enumerate((wq_hbm, wk_hbm, wv_hbm))]
    pieces = [(src, pl.ds(0, HALF), dst, c, base, n) for src, _, dst, c, base, n in pieces]
    pieces += [(wo_hbm, every, wo, every, 0, HALF)]
    pieces += [(w1_hbm, cols(i), w1, cols(i), 0, WIDTH) for i in range(4)]
    pieces += [(w2_hbm, every, w2, every, i * HALF, HALF) for i in range(4)]

    def weight_copy(g, s):
        hbm, hc, dst, dc, base, n = pieces[g]
        ways = WAYS[g]
        r = part_rows(base, n, ways, len(ways) - max(s - 1, 0))
        if s == 0:
            src, to, who = hbm.at[r, hc], dst.at[t, r, dc], across
        else:
            src = to = dst.at[1 - t, r, dc]
            who = mate(ways[s - 1])
        return pltpu.make_async_remote_copy(
            src_ref=src, dst_ref=to, send_sem=wsend.at[g], recv_sem=wrecv.at[s, g],
            device_id=who, device_id_type=MESH,
        )

    wplace = [0] * len(pieces)

    def adv_weight(g):
        s, last = wplace[g], len(WAYS[g])
        if s > 0:
            weight_copy(g, s - 1).wait()
        if s <= last:
            weight_copy(g, s).start()
        wplace[g] = s + 1

    def weights_ready(which):
        while min(wplace[g] - len(WAYS[g]) for g in which) < 2:
            for g in which:
                if wplace[g] < len(WAYS[g]) + 2:
                    adv_weight(g)

    bias_copy = pltpu.make_async_remote_copy(
        src_ref=hv.at[t], dst_ref=hv.at[t], send_sem=bsem.at[0], recv_sem=bsem.at[1],
        device_id=across, device_id_type=MESH,
    )
    bias_copy.start()
    for g in FIRST:
        adv_weight(g)

    def run(ops):
        for op in ops:
            if op < 20:
                adv_weight(op)
            elif op < 40:
                adv(op - 20)
            else:
                adv_vec()

    def at(loop_index, step, action):
        @pl.when(loop_index == step)
        def _():
            action()

    def hook(name, loop_index=None):
        for step, ops in PLAN.get(name, ()):
            if loop_index is None:
                run(ops)
            else:
                at(loop_index, step, lambda ops=ops: run(ops))

    def stacked(a, m0, m1):
        return jnp.concatenate([a * m0, a * m1], axis=0)

    def block_rows(b):
        return pl.ds(pl.multiple_of(b * ROWS, ROWS), ROWS)

    for cp in loads[:4]:
        cp.wait()

    def attend(i, carry):
        b = lax.rem(i, BLOCKS)
        h = t + (i // BLOCKS) * (1 - 2 * t)
        rows = block_rows(b)
        pr = mm(x_ref[b], wqkv[h])
        q = (pr[:, :HALF] + hv[h, 1:2, 0:HALF]).astype(BF)
        k = pr[:, HALF : 2 * HALF].astype(BF)
        v = (pr[:, 2 * HALF :] + hv[h, 1:2, HALF : 2 * HALF]).astype(BF)
        A[9, h, rows, :] = q
        A[10, h, rows, :] = k
        A[11, h, rows, :] = v
        units = [(wi, p) for wi in range(2) for p in range(3)]
        for g in range(0, 6, 6):
            part = units[g : g + 6]
            scores = []
            for wi, p in part:
                r, c = slice(wi * WIN, (wi + 1) * WIN), slice(p * 128, (p + 1) * 128)
                bb = bias[b * 2 + wi]
                scores.append(mm_nt(k[r, c], stacked(q[r, c], sc0, sc1)) + jnp.concatenate([bb, bb], axis=1))
            expo = [jnp.exp(s - jnp.max(s, axis=0, keepdims=True)) for s in scores]
            pbs = [(e * (1.0 / jnp.sum(e, axis=0, keepdims=True))).astype(BF) for e in expo]
            for (wi, p), pb in zip(part, pbs):
                r, c = slice(wi * WIN, (wi + 1) * WIN), slice(p * 128, (p + 1) * 128)
                probs[b * 2 + wi, h, p] = pb
                o = mm_tn(pb, v[r, c])
                o = jnp.where(low, o[:WIN], o[WIN:])
                A[8, h, pl.ds(pl.multiple_of(b * ROWS + wi * WIN, WIN), WIN), c] = o.astype(BF)

        hook("attend", i)
        at(i, 3, own_done)
        return carry

    def own_done():
        weights_ready([0, 1, 2])
        bias_copy.wait()

    lax.fori_loop(0, 2 * BLOCKS, attend, 0)

    def joined(k, rows):
        return jnp.concatenate([A[k, 0, rows, :], A[k, 1, rows, :]], axis=1)

    def normalize(hidden):
        center = hidden - row_mean(hidden)
        rs = lax.rsqrt(row_mean(center * center) + EPS)
        return center * rs, rs

    def add_vec(row, value):
        sums[0, row : row + 1, :] += value[:, :HALF]
        sums[0, row + 1 : row + 2, :] += value[:, HALF:]


    loads[4].wait()
    hook("pre_norm")
    weights_ready([3])

    def first_norm(b, carry):
        rows = block_rows(b)
        mixed = joined(8, rows)
        att = mm(mixed[:, :HALF], wo[0]) + mm(mixed[:, HALF:], wo[1])
        n, rs = normalize(x_ref[b].astype(F32) + att + out_b)
        normed[rows, :] = n
        spread[rows, :] = rs
        first = n * gain1 + shift1
        FL[0, rows, :] = first[:, :HALF].astype(BF)
        FL[1, rows, :] = first[:, HALF:].astype(BF)
        hook("norm1", b)
        return carry

    lax.fori_loop(0, BLOCKS, first_norm, 0)
    loads[5].wait()
    loads[6].wait()

    def low_rows(rows):
        return jnp.concatenate([FL[0, rows, :], FL[1, rows, :]], axis=1)

    def half_feed(b, h):
        rows = block_rows(b)
        inner_all = mm(low_rows(rows), w1[h]) + hv[h, 0:1, :]
        acts = []
        for k in range(4):
            inner = inner_all[:, k * HALF : (k + 1) * HALF]
            phi = 0.5 + 0.5 * lax.erf(inner * 0.7071067811865476)
            slope = phi + inner * jnp.exp(-0.5 * inner * inner) * 0.3989422804014327
            act = (inner * phi).astype(BF)
            A[k, h, rows, :] = act
            A[4 + k, h, rows, :] = slope.astype(BF)
            acts.append(act)
        return mm(jnp.concatenate(acts, axis=1), w2[h])

    def cot_copy(b):
        return pltpu.make_async_copy(cot_hbm.at[b], cot.at[lax.rem(b, 2)], psem.at[lax.rem(b, 2)])

    cot_copy(0).start()
    cot_copy(1).start()

    def feed_own(b, carry):
        acc[block_rows(b), :] = half_feed(b, t)
        hook("own", b)
        return carry

    lax.fori_loop(0, BLOCKS, feed_own, 0)
    hook("pre_other")
    weights_ready([4, 5, 6, 7, 8, 9, 10, 11])

    def second_norm(b, carry):
        rows = block_rows(b)
        red = acc[rows, :] + half_feed(b, 1 - t)
        n, rs = normalize(normed[rows, :] * gain1 + shift1 + red + red_b)
        slot = lax.rem(b, 2)

        @pl.when(b >= 2)
        def _():
            pltpu.make_async_copy(stage.at[slot], out_hbm.at[b - 2], osem.at[slot]).wait()

        stage[slot] = n * gain2 + shift2
        pltpu.make_async_copy(stage.at[slot], out_hbm.at[b], osem.at[slot]).start()
        cot_copy(b).wait()
        c = cot[slot].astype(F32)

        @pl.when(b + 2 < BLOCKS)
        def _():
            cot_copy(b + 2).start()

        add_vec(14, col_sum(c))
        add_vec(12, col_sum(c * n))
        u = c * gain2
        gs = rs * (u - row_mean(u) - n * row_mean(u * n))
        add_vec(10, col_sum(gs))
        acc[rows, :] = gs
        return carry

    lax.fori_loop(0, BLOCKS, second_norm, 0)
    for b in range(2):
        pltpu.make_async_copy(stage.at[b], out_hbm.at[b + 2], osem.at[b]).wait()

    def span(i):
        return WIDTH >> (i + 1)

    def lo(j, i):
        return sum((bit[ORDERS[j][n]] * span(n) for n in range(i + 1)), 0)

    def ds(at_, n):
        return pl.ds(pl.multiple_of(at_, 16), n)

    def held(j, h, r):
        k, first, width = PARTS[j]
        if k < 9:
            return A, (k, h, r, pl.ds(first, width))
        return w1, (h, r, pl.ds((k - 9) * HALF + first, width))

    def add_in(j, h, r, value):
        ref, at_ = held(j, h, r)
        ref[at_] = ref[at_] + value

    def view(j, h, r):
        ref, at_ = held(j, h, r)
        return ref.at[at_]

    def landing(j, p):
        k, first, width = PARTS[j]
        c = pl.ds(first, width)
        if p == 0:
            return R0, (SEQUENCE.index(k) % 4, slice(None), slice(None), c)
        if p == 1 and k in LATE:
            return RB, (LATE.index(k), slice(None), slice(None), c)
        if p == 1:
            return R1, (k - sum(n < k for n in LATE), slice(None), c)
        return (R2, R3, R4)[p - 2], (k, slice(None), c)

    halves = [("half", i) for i in range(1, split)]
    swaps_ = [("swap", i) for i in range(bits - split)]
    gathers = [("gather", i) for i in reversed(range(1, split))]

    def names_of(j):
        mid = halves + swaps_ + gathers
        if PARTS[j][0] in LATE:
            return [("core", 0), ("both", 1), ("tensor", 1)] + mid[1:] + [("gather", 0)]
        return [("core", 0), ("tensor", 0)] + mid + [("gather", 0)]

    def begin(j, s):
        piece_copy(j, s).start()

    def piece_copy(j, s):
        kind, i = names_of(j)[s]
        way = ORDERS[j]
        k, first, width = PARTS[j]
        if kind == "core":
            src, who = view(j, slice(None), ds((1 - bit[way[0]]) * span(0), span(0))), mate(way[0])
            land, at_ = landing(j, 0)
            dst = land.at[at_]
        elif kind == "tensor":
            src, who = view(j, 1 - t, ds(lo(j, i), span(i))), across
            land, at_ = landing(j, i + 1)
            dst = land.at[at_]
        elif kind == "both":
            src, who = view(j, slice(None), ds(lo(j, 0) + (1 - bit[way[1]]) * span(1), span(1))), mate(way[1])
            land, at_ = landing(j, 1)
            dst = land.at[at_]
        elif kind == "half":
            src = view(j, t, ds(lo(j, i - 1) + (1 - bit[way[i]]) * span(i), span(i)))
            who = mate(way[i])
            land, at_ = landing(j, i + 1)
            dst = land.at[at_]
        elif kind == "swap":
            src, who = view(j, t, ds(lo(j, split - 1), span(split - 1))), mate(split + i)
            dst = RX.at[i, k, :, pl.ds(first, width)]
        else:
            r = ds(lo(j, i), span(i))
            dst, who = grad_hbm.at[k, r, pl.ds(first, width)], mate(way[i])
            src = view(j, t, r) if i == split - 1 and i > 0 else dst
        if kind == "swap":
            landed = xrecv.at[i, j]
        else:
            key = {"core": "c", "tensor": "y", "gather": "g"}.get(kind, "r")
            landed = grecv.at[LANDED[key if kind in ("core", "tensor") else f"{key}{way[i]}"][j]]
        return pltpu.make_async_remote_copy(
            src_ref=src, dst_ref=dst, send_sem=gsend.at[j], recv_sem=landed, device_id=who, device_id_type=MESH
        )

    def keep_copy(j):
        k, first, width = PARTS[j]
        r = ds(lo(j, split - 1), span(split - 1))
        return pltpu.make_async_copy(view(j, t, r), grad_hbm.at[k, r, pl.ds(first, width)], fsem.at[KEPT[j]])

    def settle(j, s):
        names = names_of(j)
        kind, i = names[s]
        k, first, width = PARTS[j]
        piece_copy(j, s).wait()
        if kind == "core":
            land, at_ = landing(j, 0)
            add_in(j, slice(None), ds(lo(j, 0), span(0)), land[at_])
        elif kind == "tensor":
            land, at_ = landing(j, i + 1)
            add_in(j, t, ds(lo(j, i), span(i)), land[at_])
        elif kind == "both":
            land, at_ = landing(j, 1)
            add_in(j, slice(None), ds(lo(j, 1), span(1)), land[at_])
        elif kind == "half":
            land, at_ = landing(j, i + 1)
            add_in(j, t, ds(lo(j, i), span(i)), land[at_])
        elif kind == "swap":
            add_in(j, t, ds(lo(j, split - 1), span(split - 1)), RX[i, k, :, pl.ds(first, width)])
        elif i == split - 1:
            keep_copy(j).wait()
        if s + 1 < len(names) and names[s + 1] == ("gather", split - 1):
            keep_copy(j).start()

    place = [0] * len(PARTS)

    def adv(*which):
        for k in which:
            s = place[k]
            names = names_of(k)
            if s > len(names):
                continue
            if s > 0:
                settle(k, s - 1)
            if s < len(names):
                begin(k, s)
            place[k] = s + 1

    swaps = [across] + [mate(i) for i in range(bits)]
    vec_place = [0]

    def adv_vec():
        s = vec_place[0]

        def cp(j):
            return pltpu.make_async_remote_copy(
                src_ref=sums.at[j], dst_ref=got.at[j], send_sem=vsend.at[j], recv_sem=vrecv.at[j],
                device_id=swaps[j], device_id_type=MESH,
            )

        if s > len(swaps):
            return
        if s > 0:
            cp(s - 1).wait()
            sums[s] = sums[s - 1] + got[s - 1]
        if s < len(swaps):
            cp(s).start()
        vec_place[0] = s + 1

    def transpose_into(dst, get):
        for b in range(BLOCKS):
            dst[:, b * ROWS : (b + 1) * ROWS] = get(b).T

    def rows_of(b):
        return slice(b * ROWS, (b + 1) * ROWS)

    def chunk_loop(name, first, count, left):
        def one(j, carry):
            k = first + j
            full = mm(left[...], joined(k, slice(None)))
            for h in range(2):
                part = full[:, h * HALF : (h + 1) * HALF].astype(BF)
                if first < 9:
                    A[k, h, 0:WIDTH, :] = part
                else:
                    w1[h, :, pl.ds(pl.multiple_of(j * HALF, HALF), HALF)] = part
            hook(name, j)
            return carry

        if count:
            lax.fori_loop(0, count, one, 0)

    transpose_into(GT, lambda b: acc[rows_of(b), :].astype(BF))
    chunk_loop("dw2", 0, 4, GT)
    transpose_into(FLT, lambda b: low_rows(rows_of(b)))
    hook("mid")

    def feed_back(b, carry):
        rows = block_rows(b)
        gs = acc[rows, :]
        gl = gs.astype(BF)
        gf = gs
        for h in range(2):
            da = mm_nt(gl, w2[h])
            gis = []
            for k in range(4):
                gi = (da[:, k * HALF : (k + 1) * HALF] * A[4 + k, h, rows, :].astype(F32)).astype(BF)
                A[4 + k, h, rows, :] = gi
                sums[0, 16 + 4 * h + k : 17 + 4 * h + k, :] += col_sum(gi.astype(F32))
                gis.append(gi)
            gf = gf + mm_nt(jnp.concatenate(gis, axis=1), w1[h])
        n = normed[rows, :]
        add_vec(6, col_sum(gf * n))
        add_vec(8, col_sum(gf))
        u = gf * gain1
        gh = spread[rows, :] * (u - row_mean(u) - n * row_mean(u * n))
        add_vec(4, col_sum(gh))
        acc[rows, :] = gh
        gm = gh.astype(BF)
        FL[0, rows, :] = mm_nt(gm, wo[0]).astype(BF)
        FL[1, rows, :] = mm_nt(gm, wo[1]).astype(BF)
        hook("back", b)
        return carry

    lax.fori_loop(0, BLOCKS, feed_back, 0)
    transpose_into(GT, lambda b: x_ref[b])
    chunk_loop("dw1", 4, FIRST_EXPAND, FLT)

    def attend_back(i, carry):
        h, b = i // BLOCKS, lax.rem(i, BLOCKS)

        def rows_at(wi):
            return pl.ds(pl.multiple_of(b * ROWS + wi * WIN, WIN), WIN)

        def at_(p):
            return slice(p * 128, (p + 1) * 128)

        sums_ = {}
        units = [(wi, p) for p in range(3) for wi in range(2)]
        for g in range(0, 6, 6):
            part = units[g : g + 6]
            do2 = [stacked(FL[h, rows_at(wi), at_(p)], mask0, mask1) for wi, p in part]
            dp = [mm_nt(A[11, h, rows_at(wi), at_(p)], d) for (wi, p), d in zip(part, do2)]
            dv = [mm(probs[b * 2 + wi, h, p], d).astype(BF) for (wi, p), d in zip(part, do2)]
            pf = [probs[b * 2 + wi, h, p].astype(F32) for wi, p in part]
            dsc = [(f * (d - jnp.sum(f * d, axis=0, keepdims=True))).astype(BF) for f, d in zip(pf, dp)]
            dk = [mm(d, stacked(A[9, h, rows_at(wi), at_(p)], sc0, sc1)).astype(BF) for (wi, p), d in zip(part, dsc)]
            dq = [mm_tn(d, A[10, h, rows_at(wi), at_(p)]) for (wi, p), d in zip(part, dsc)]
            for (wi, p), q_, k_, v_ in zip(part, dq, dk, dv):
                q_ = (jnp.where(low, q_[:WIN], q_[WIN:]) * 0.125).astype(BF)
                A[9, h, rows_at(wi), at_(p)] = q_
                A[10, h, rows_at(wi), at_(p)] = k_
                A[11, h, rows_at(wi), at_(p)] = v_
                add = col_sum(q_.astype(F32)), col_sum(v_.astype(F32))
                sums_[p] = add if p not in sums_ else (sums_[p][0] + add[0], sums_[p][1] + add[1])
        for p in range(3):
            hsum[h, 0:1, at_(p)] += sums_[p][0]
            hsum[h, 1:2, at_(p)] += sums_[p][1]
        hook("attb", i)
        return carry

    lax.fori_loop(0, 2 * BLOCKS, attend_back, 0)
    for h in range(2):
        sums[0, h : h + 1, :] = hsum[h, 0:1, :]
        sums[0, 2 + h : 3 + h, :] = hsum[h, 1:2, :]
    adv_vec()
    chunk_loop("dwq", 9, 3, GT)
    chunk_loop("dw1b", 4 + FIRST_EXPAND, 4 - FIRST_EXPAND, FLT)
    transpose_into(FLT, lambda b: acc[rows_of(b), :].astype(BF))
    chunk_loop("dwo", 8, 1, FLT)

    def input_grad(b, carry):
        rows = block_rows(b)
        g = acc[rows, :]
        for h in range(2):
            gp = jnp.concatenate([A[9 + i, h, rows, :] for i in range(3)], axis=1)
            g = g + mm_nt(gp, wqkv[h])
        slot = lax.rem(b, 2)

        @pl.when(b >= 2)
        def _():
            pltpu.make_async_copy(stage.at[slot], gin_hbm.at[b - 2], osem.at[slot]).wait()

        stage[slot] = g
        pltpu.make_async_copy(stage.at[slot], gin_hbm.at[b], osem.at[slot]).start()
        hook("gin", b)
        return carry

    lax.fori_loop(0, BLOCKS, input_grad, 0)
    hook("tail")
    for b in range(2):
        pltpu.make_async_copy(stage.at[b], gin_hbm.at[b + 2], osem.at[b]).wait()
    left = lambda: [j for j in range(len(PARTS)) if place[j] <= len(names_of(j))]
    while left():
        adv_vec()
        adv(*left())
    while vec_place[0] <= len(swaps):
        adv_vec()
    vec_out[...] = sums[len(swaps)]


def layer(n_dp, *operands):
    vm = pl.BlockSpec(memory_space=pltpu.VMEM)
    hbm = pl.BlockSpec(memory_space=pl.ANY)
    bits = n_dp.bit_length() - 1
    split = min(bits, 4)
    dma = pltpu.SemaphoreType.DMA
    return pl.pallas_call(
        functools.partial(kernel, bits),
        out_shape=(
            jax.ShapeDtypeStruct((BLOCKS, ROWS, WIDTH), F32),
            jax.ShapeDtypeStruct((BLOCKS, ROWS, WIDTH), F32),
            jax.ShapeDtypeStruct((CHUNKS, WIDTH, HALF), BF),
            jax.ShapeDtypeStruct((24, HALF), F32),
        ),
        in_specs=[hbm] * 19,
        out_specs=(hbm, hbm, hbm, vm),
        scratch_shapes=[
            pltpu.VMEM((BLOCKS, 2 * ROWS), jnp.int32),
            pltpu.VMEM((BLOCKS, 2 * ROWS), jnp.int32),
            pltpu.VMEM((HALF,), BF),
            pltpu.VMEM((HALF,), BF),
            pltpu.VMEM((HIDDEN,), BF),
            pltpu.VMEM((WIDTH,), BF),
            pltpu.VMEM((WIDTH,), BF),
            pltpu.VMEM((WIDTH,), BF),
            pltpu.VMEM((WIDTH,), BF),
            pltpu.VMEM((WIDTH,), BF),
            pltpu.VMEM((WIDTH,), BF),
            pltpu.VMEM((BLOCKS, ROWS, WIDTH), BF),
            pltpu.VMEM((2, WIDTH, 3 * HALF), BF),
            pltpu.VMEM((2, HALF, WIDTH), BF),
            pltpu.VMEM((2, WIDTH, HIDDEN), BF),
            pltpu.VMEM((2, HIDDEN, WIDTH), BF),
            pltpu.VMEM((2, 8, HIDDEN), F32),
            pltpu.VMEM((CHUNKS, 2, TOTAL, HALF), BF),
            pltpu.VMEM((2 * BLOCKS, 2, 3, WIN, 2 * WIN), BF),
            pltpu.VMEM((TOTAL, WIDTH), F32),
            pltpu.VMEM((TOTAL, 1), F32),
            pltpu.VMEM((TOTAL, WIDTH), F32),
            pltpu.VMEM((2, TOTAL, HALF), BF),
            pltpu.VMEM((WIDTH, TOTAL), BF),
            pltpu.VMEM((WIDTH, TOTAL), BF),
            pltpu.VMEM((2 * BLOCKS, WIN, WIN), F32),
            pltpu.VMEM((2, ROWS, WIDTH), F32),
            pltpu.VMEM((2, ROWS, WIDTH), BF),
            pltpu.VMEM((bits + 2, 24, HALF), F32),
            pltpu.VMEM((bits + 1, 24, HALF), F32),
            pltpu.VMEM((2, 8, HALF), F32),
            pltpu.VMEM((4, 2, WIDTH // 2, HALF), BF),
            pltpu.VMEM((CHUNKS - len(LATE), WIDTH // 2, HALF), BF),
            pltpu.VMEM((max(len(LATE), 1), 2, WIDTH // 4, HALF), BF),
            pltpu.VMEM((CHUNKS, WIDTH // 4, HALF), BF),
            pltpu.VMEM((CHUNKS, WIDTH // 8, HALF), BF),
            pltpu.VMEM((CHUNKS, WIDTH // 16, HALF), BF),
            pltpu.VMEM((max(bits - split, 1), CHUNKS, WIDTH >> split, HALF), BF),
            dma((11,)),
            dma((7,)),
            dma((2,)),
            dma((max(KEPT) + 1,)),
            dma((12,)),
            dma((4, 12)),
            dma((len(PARTS),)),
            dma((LANDED_COUNT,)),
            dma((bits + 1,)),
            dma((bits + 1,)),
            dma((2,)),
            dma((2,)),
            dma((max(bits - split, 1), len(PARTS) if bits > split else 1)),
        ],
        compiler_params=pltpu.CompilerParams(
            vmem_limit_bytes=67043328, collective_id=0, has_side_effects=True
        ),
    )(*operands)


def finish_kernel(
    grad_hbm, out_low, gin_low, vec_hbm, outg, ging, wqg, wkg, wvg, wog, w1g, w2g, qbg, vbg, obg, g1g, s1g, ebg, rbg, g2g, s2g,
    low, wide, turned, rows, vec, isem, osem, rsem, ssem, vsem,
):
    t = lax.axis_index("tensor")
    vec_copy = pltpu.make_async_copy(vec_hbm, vec, vsem.at[0])
    vec_copy.start()
    fetch = [pltpu.make_async_copy(grad_hbm.at[k], low.at[k], isem.at[k]) for k in range(CHUNKS)]
    order = [0, 1, 2, 3, 8] + list(range(4, 8)) + list(range(9, 12))
    for k in order:
        fetch[k].start()
    passed = []
    for i, ref in enumerate((out_low, gin_low)):
        cp = pltpu.make_async_copy(ref, rows.at[i], rsem.at[i])
        cp.start()
        passed.append(cp)

    sends = []
    for k in order:
        fetch[k].wait()
        if k >= 9:
            wide[k - 5] = low[k].astype(F32)
            src, dst = wide.at[k - 5], (wqg, wkg, wvg)[k - 9]
        elif k >= 4 and k < 8:
            wide[k - 4] = low[k].astype(F32)
            src, dst = wide.at[k - 4], w1g.at[:, pl.ds((k - 4) * HALF, HALF)]
        elif k == 8:
            turned[4] = low[k].astype(F32).T
            src, dst = turned.at[4], wog
        else:
            turned[k] = low[k].astype(F32).T
            src, dst = turned.at[k], w2g.at[pl.ds(k * HALF, HALF), :]
        cp = pltpu.make_async_copy(src, dst, osem.at[k])
        cp.start()
        sends.append(cp)
    for i, ref in enumerate((outg, ging)):
        passed[i].wait()
        cp = pltpu.make_async_copy(rows.at[i], ref, ssem.at[i])
        cp.start()
        sends.append(cp)
    vec_copy.wait()

    def pick(r):
        return jnp.where(t == 0, vec[r : r + 1, :], vec[r + 1 : r + 2, :]).reshape(HALF)

    def whole(r):
        return jnp.concatenate([vec[r : r + 1, :], vec[r + 1 : r + 2, :]], axis=1).reshape(WIDTH)

    qbg[...] = pick(0)
    vbg[...] = pick(2)
    for ref, r in ((obg, 4), (g1g, 6), (s1g, 8), (rbg, 10), (g2g, 12), (s2g, 14)):
        ref[...] = whole(r)
    lines = [jnp.where(t == 0, vec[16 + k : 17 + k, :], vec[20 + k : 21 + k, :]) for k in range(4)]
    ebg[...] = jnp.concatenate(lines, axis=1).reshape(HIDDEN)

    for cp in sends:
        cp.wait()


def finish(out, gin, grads, vec):
    vm = pl.BlockSpec(memory_space=pltpu.VMEM)
    hbm = pl.BlockSpec(memory_space=pltpu.HBM)
    f = lambda *shape: jax.ShapeDtypeStruct(shape, F32)
    return pl.pallas_call(
        finish_kernel,
        out_shape=(f(BLOCKS, ROWS, WIDTH), f(BLOCKS, ROWS, WIDTH), f(WIDTH, HALF), f(WIDTH, HALF), f(WIDTH, HALF), f(HALF, WIDTH), f(WIDTH, HIDDEN), f(HIDDEN, WIDTH),
                   f(HALF), f(HALF), f(WIDTH), f(WIDTH), f(WIDTH), f(HIDDEN), f(WIDTH), f(WIDTH), f(WIDTH)),
        in_specs=[hbm, hbm, hbm, hbm],
        out_specs=(hbm,) * 8 + (vm,) * 9,
        scratch_shapes=[
            pltpu.VMEM((CHUNKS, WIDTH, HALF), BF),
            pltpu.VMEM((7, WIDTH, HALF), F32),
            pltpu.VMEM((5, HALF, WIDTH), F32),
            pltpu.VMEM((2, BLOCKS, ROWS, WIDTH), F32),
            pltpu.VMEM((24, HALF), F32),
            pltpu.SemaphoreType.DMA((CHUNKS,)),
            pltpu.SemaphoreType.DMA((CHUNKS,)),
            pltpu.SemaphoreType.DMA((2,)),
            pltpu.SemaphoreType.DMA((2,)),
            pltpu.SemaphoreType.DMA((1,)),
        ],
        compiler_params=pltpu.CompilerParams(vmem_limit_bytes=67043328),
    )(grads, out, gin, vec)


def local(
    n_dp, inputs, segments, padding, query_weight, query_bias, key_weight, value_weight, value_bias,
    output_weight, output_bias, first_gain, first_shift, expand_weight, expand_bias,
    reduce_weight, reduce_bias, second_gain, second_shift, cotangent,
):
    out, gin, grads, vec = layer(
        n_dp, inputs, cotangent, segments, padding, query_bias, value_bias, expand_bias, output_bias, first_gain,
        first_shift, reduce_bias, second_gain, second_shift, query_weight, key_weight, value_weight,
        output_weight, expand_weight, reduce_weight,
    )
    out, gin, wq, wk, wv, wo, w1, w2, qb, vb, ob, g1, s1, eb, rb, g2, s2 = finish(out, gin, grads, vec)
    return (out, gin, wq, qb, wk, wv, vb, wo, ob, g1, s1, w1, eb, w2, rb, g2, s2)


def solution(mesh):
    tokens = P(None, ("dp", "tensor"), None)
    return jax.shard_map(
        functools.partial(local, mesh.shape["dp"]),
        mesh=mesh,
        in_specs=(
            tokens, P(None, "dp"), P(None, "dp"), P(None, "tensor"), P("tensor"), P(None, "tensor"),
            P(None, "tensor"), P("tensor"), P("tensor", None), P(), P(), P(), P(None, "tensor"),
            P("tensor"), P("tensor", None), P(), P(), P(), tokens,
        ),
        out_specs=(
            tokens, tokens, P(None, "tensor"), P("tensor"), P(None, "tensor"), P(None, "tensor"),
            P("tensor"), P("tensor", None), P(), P(), P(), P(None, "tensor"), P("tensor"),
            P("tensor", None), P(), P(), P(),
        ),
        check_vma=False,
    )
```

```python
import functools

import jax
import jax.numpy as jnp
from jax import lax
from jax.experimental import pallas as pl
from jax.experimental.pallas import tpu as pltpu
from jax.sharding import PartitionSpec as P

WIN = 128
BLOCKS = 4
ROWS = 256
TOTAL = BLOCKS * ROWS
WIDTH = 768
HALF = 384
HIDDEN = 1536
CHUNKS = 12
EPS = 1e-12
BF = jnp.bfloat16
F32 = jnp.float32
MESH = pl.DeviceIdType.MESH


def mm(a, b):
    return lax.dot_general(a, b, (((1,), (0,)), ((), ())), preferred_element_type=F32)


def mm_nt(a, b):
    return lax.dot_general(a, b, (((1,), (1,)), ((), ())), preferred_element_type=F32)


def mm_tn(a, b):
    return lax.dot_general(a, b, (((0,), (0,)), ((), ())), preferred_element_type=F32)


def row_mean(a):
    return jnp.sum(a, axis=-1, keepdims=True) * (1.0 / WIDTH)


def col_sum(a):
    return jnp.sum(a, axis=0, keepdims=True)

WAYS = ((2, 1, 0), (2, 1, 0), (2, 1, 0), (2, 1, 0), (1, 2, 0), (1, 2, 0), (2, 1, 0), (2, 0), (2, 0), (2, 1, 0), (2, 1, 0), (2, 1, 0), (2, 1, 0), (0,), (2, 0))
FIRST = (1, 4, 0, 3, 5, 2, 6, 11, 10, 12, 9, 7, 14, 8, 13)
PARTS = ((0, 0, 384), (1, 0, 384), (2, 0, 384), (3, 0, 384), (4, 0, 384), (5, 0, 384), (6, 0, 384), (7, 0, 384), (8, 0, 128), (8, 128, 128), (8, 256, 128), (9, 0, 384), (10, 0, 384), (11, 0, 128), (11, 128, 128), (11, 256, 128))
ORDERS = ((0, 1, 2, 3), (0, 1, 2, 3), (0, 1, 2, 3), (0, 1, 2, 3), (0, 1, 2, 3), (0, 1, 2, 3), (0, 1, 2, 3), (0, 1, 2, 3), (0, 1, 2, 3), (0, 1, 2, 3), (0, 1, 2, 3), (0, 1, 2, 3), (0, 1, 2, 3), (0, 1, 2, 3), (0, 1, 2, 3), (0, 1, 2, 3))
LATE = (1, 3, 4, 6)
SEQUENCE = (0, 1, 2, 3, 4, 5, 6, 7, 9, 10, 11, 8)
FIRST_EXPAND = 4
PLAN = {
    "attend": ((1, (1,)), (2, (4,)), (3, (0, 1, 3, 5, 4, 2, 0, 6, 3, 1, 5, 11, 1, 4, 2, 0, 10, 4, 0, 6, 3, 12, 3, 5, 2, 9, 5, 11, 2)), (5, (6, 7, 10)), (6, (6, 12)), (7, (9, 11, 14)),),
    "norm1": ((0, (11,)), (1, (7, 8, 10)),),
    "own": ((0, (7, 10, 12, 14)), (1, (8, 9, 12, 13, 14)),),
    "pre_other": ((0, (8, 9, 13)),),
    "dw2": ((0, (20,)), (1, (21,)), (2, (20, 22)), (3, (21, 23)),),
    "back": ((0, (22, 23)), (1, (20, 21)), (3, (21, 22, 23)),),
    "dw1": ((0, (24, 20)), (1, (25,)), (2, (24, 26, 21)), (3, (25, 27, 20, 22, 23)),),
    "attb": ((0, (26,)), (1, (27,)), (2, (21,)), (3, (20, 22)), (5, (23, 24)), (7, (21, 25)),),
    "dwq": ((0, (31, 20)), (1, (32,)), (2, (31, 33, 34, 35, 22, 26, 21, 32, 23)),),
    "dwo": ((0, (33, 34, 35, 28, 29, 30, 20, 25, 27)),),
    "gin": ((0, (28, 29, 30, 22, 24, 40)), (1, (21, 23, 25, 40)), (3, (21, 22)),),
    "tail": ((0, (20, 24, 20, 23, 31, 27, 40, 25, 26, 24, 27, 22, 40, 22, 25, 26, 23, 32, 23, 24, 31, 27, 33, 40, 25, 34, 32, 26, 33, 24, 35, 31, 28, 25, 27, 32, 34, 29, 25, 33, 26, 30, 24, 31, 27, 35, 24, 28, 34, 32, 29, 33, 30, 26, 35, 28, 31, 27, 34, 29, 27, 32, 30, 33, 35, 26, 28, 31, 26, 34, 29, 32, 33, 30, 35, 34, 31, 28, 29, 31, 30, 35, 28, 32, 29, 30, 33, 32, 34, 33, 35, 34, 28, 35, 29, 28, 30, 29, 30)),),
}
LANDED = {
    "c": (0, 1, 2, 3, 0, 1, 2, 3, 0, 5, 6, 0, 1, 2, 3, 4),
    "g0": (8, 7, 7, 8, 8, 7, 8, 7, 8, 9, 7, 7, 8, 9, 7, 10),
    "g1": (12, 11, 13, 14, 12, 11, 14, 13, 14, 17, 18, 11, 12, 15, 16, 13),
    "g2": (20, 19, 21, 22, 20, 19, 22, 21, 19, 24, 25, 19, 20, 23, 21, 22),
    "g3": (27, 26, 28, 29, 27, 26, 29, 28, 31, 26, 32, 26, 27, 30, 28, 29),
    "r1": (35, 33, 36, 34, 37, 34, 33, 35, 36, 38, 39, 36, 33, 34, 37, 35),
    "r2": (41, 40, 42, 43, 41, 40, 43, 42, 45, 40, 41, 40, 41, 44, 42, 43),
    "r3": (47, 46, 48, 49, 47, 46, 49, 48, 51, 46, 52, 46, 47, 50, 48, 49),
    "y": (53, 55, 54, 53, 55, 56, 58, 54, 53, 63, 64, 57, 59, 60, 61, 62),
}
LANDED_COUNT = 65
KEPT = (1, 0, 0, 1, 1, 0, 1, 0, 2, 0, 3, 0, 1, 2, 0, 1)


def kernel(
    bits,
    x_hbm, cot_hbm, seg_hbm, pad_hbm, qb_hbm, vb_hbm, eb_hbm, ob_hbm, g1_hbm, s1_hbm, rb_hbm, g2_hbm, s2_hbm,
    wq_hbm, wk_hbm, wv_hbm, wo_hbm, w1_hbm, w2_hbm,
    out_hbm, gin_hbm, grad_hbm, vec_out,
    seg_ref, pad_ref, qb_ref, vb_ref, eb_ref, ob_ref, g1_ref, s1_ref, rb_ref, g2_ref, s2_ref,
    x_ref, wqkv, wo, w1, w2, hv, A, probs, normed, spread, acc, FL, FLT, GT, bias, stage, sums, got, hsum,
    R0, R1, RB, R2, R3, R4, RX,
    isem, lsem, osem, fsem, wsend, wrecv, gsend, grecv, vsend, vrecv, bsem, psem, xrecv,
):
    t = lax.axis_index("tensor")
    me = lax.axis_index("dp")
    bit = [lax.rem(me // (1 << i), 2) for i in range(bits)]
    split = min(bits, 4)

    def mate(i):
        return (me + (1 << i) * (1 - 2 * bit[i]), t)

    across = (me, 1 - t)
    partners = [across] + [mate(i) for i in range(bits)]

    barrier = pltpu.get_barrier_semaphore()
    for who in partners:
        pl.semaphore_signal(barrier, inc=1, device_id=who, device_id_type=MESH)

    smalls = [
        (seg_hbm, seg_ref),
        (pad_hbm, pad_ref),
        (qb_hbm, qb_ref),
        (vb_hbm, vb_ref),
        (eb_hbm, eb_ref),
        (ob_hbm, ob_ref),
        (g1_hbm, g1_ref),
        (s1_hbm, s1_ref),
        (rb_hbm, rb_ref),
        (g2_hbm, g2_ref),
        (s2_hbm, s2_ref),
    ]
    smalls = [pltpu.make_async_copy(s, d, isem.at[i]) for i, (s, d) in enumerate(smalls)]
    for cp in smalls:
        cp.start()

    locals_ = [
        (x_hbm, x_ref),
        (wq_hbm, wqkv.at[t, :, pl.ds(0, HALF)]),
        (wk_hbm, wqkv.at[t, :, pl.ds(HALF, HALF)]),
        (wv_hbm, wqkv.at[t, :, pl.ds(2 * HALF, HALF)]),
        (wo_hbm, wo.at[t]),
        (w1_hbm, w1.at[t]),
        (w2_hbm, w2.at[t]),
    ]
    loads = [pltpu.make_async_copy(s, d, lsem.at[i]) for i, (s, d) in enumerate(locals_)]
    for cp in loads:
        cp.start()

    for cp in smalls:
        cp.wait()

    def row(ref):
        return ref[...].astype(F32).reshape(1, ref.shape[0])

    hv[t] = jnp.zeros((8, HIDDEN), F32)
    hv[t, 0:1, :] = row(eb_ref)
    hv[t, 1:2, 0:HALF] = row(qb_ref)
    hv[t, 1:2, HALF : 2 * HALF] = row(vb_ref)
    out_b, gain1, shift1 = row(ob_ref), row(g1_ref), row(s1_ref)
    red_b, gain2, shift2 = row(rb_ref), row(g2_ref), row(s2_ref)
    sums[0] = jnp.zeros((24, HALF), F32)
    hsum[...] = jnp.zeros_like(hsum)
    lane = lax.broadcasted_iota(jnp.int32, (1, 128), 1)
    low = lane < 64
    mask0 = jnp.where(low, 1.0, 0.0).astype(BF)
    mask1 = jnp.where(low, 0.0, 1.0).astype(BF)
    sc0 = jnp.where(low, 0.125, 0.0).astype(BF)
    sc1 = jnp.where(low, 0.0, 0.125).astype(BF)

    for b in range(BLOCKS):
        for wi in range(2):
            cols = pl.ds(pl.multiple_of(t * ROWS + wi * WIN, WIN), WIN)
            seg = jnp.broadcast_to(seg_ref[b : b + 1, cols].astype(F32), (WIN, WIN))
            live = jnp.broadcast_to(pad_ref[b : b + 1, cols].astype(F32), (WIN, WIN))
            bias[2 * b + wi] = jnp.where((seg == seg.T) & (live.T > 0.5), 0.0, -1e30)

    pl.semaphore_wait(barrier, len(partners))

    def part_rows(base, n, ways, fixed):
        size = n // (1 << len(ways))
        at_ = sum((bit[w] * (size << j) for j, w in enumerate(ways)), 0)
        free = len(ways) - fixed
        at_ = sum((bit[w] * (size << j) for j, w in enumerate(ways) if j >= free), 0)
        return pl.ds(pl.multiple_of(base + at_, 16), size << free)

    def cols(i):
        return pl.ds(i * HALF, HALF)

    every = pl.ds(0, WIDTH)
    pieces = [
        (src, pl.ds(0, HALF), wqkv, cols(i), base, HALF)
        for i, src in enumerate((wq_hbm, wk_hbm, wv_hbm))
        for base in (0, HALF)
    ]
    pieces += [(wo_hbm, every, wo, every, 0, HALF)]
    pieces += [(w1_hbm, cols(i), w1, cols(i), 0, WIDTH) for i in range(4)]
    pieces += [(w2_hbm, every, w2, every, i * HALF, HALF) for i in range(4)]

    def weight_copy(g, s):
        hbm, hc, dst, dc, base, n = pieces[g]
        ways = WAYS[g]
        r = part_rows(base, n, ways, len(ways) - max(s - 1, 0))
        if s == 0:
            src, to, who = hbm.at[r, hc], dst.at[t, r, dc], across
        else:
            src = to = dst.at[1 - t, r, dc]
            who = mate(ways[s - 1])
        return pltpu.make_async_remote_copy(
            src_ref=src, dst_ref=to, send_sem=wsend.at[g], recv_sem=wrecv.at[s, g],
            device_id=who, device_id_type=MESH,
        )

    wplace = [0] * len(pieces)

    def adv_weight(g):
        s, last = wplace[g], len(WAYS[g])
        if s > 0:
            weight_copy(g, s - 1).wait()
        if s <= last:
            weight_copy(g, s).start()
        wplace[g] = s + 1

    def weights_ready(which):
        while min(wplace[g] - len(WAYS[g]) for g in which) < 2:
            for g in which:
                if wplace[g] < len(WAYS[g]) + 2:
                    adv_weight(g)

    bias_copy = pltpu.make_async_remote_copy(
        src_ref=hv.at[t], dst_ref=hv.at[t], send_sem=bsem.at[0], recv_sem=bsem.at[1],
        device_id=across, device_id_type=MESH,
    )
    bias_copy.start()
    for g in FIRST:
        adv_weight(g)

    def run(ops):
        for op in ops:
            if op < 20:
                adv_weight(op)
            elif op < 40:
                adv(op - 20)
            else:
                adv_vec()

    def at(loop_index, step, action):
        @pl.when(loop_index == step)
        def _():
            action()

    def hook(name, loop_index=None):
        for step, ops in PLAN.get(name, ()):
            if loop_index is None:
                run(ops)
            else:
                at(loop_index, step, lambda ops=ops: run(ops))

    def stacked(a, m0, m1):
        return jnp.concatenate([a * m0, a * m1], axis=0)

    def block_rows(b):
        return pl.ds(pl.multiple_of(b * ROWS, ROWS), ROWS)

    for cp in loads[:4]:
        cp.wait()

    def attend(i, carry):
        b = lax.rem(i, BLOCKS)
        h = t + (i // BLOCKS) * (1 - 2 * t)
        rows = block_rows(b)
        pr = mm(x_ref[b], wqkv[h])
        q = (pr[:, :HALF] + hv[h, 1:2, 0:HALF]).astype(BF)
        k = pr[:, HALF : 2 * HALF].astype(BF)
        v = (pr[:, 2 * HALF :] + hv[h, 1:2, HALF : 2 * HALF]).astype(BF)
        A[9, h, rows, :] = q
        A[10, h, rows, :] = k
        A[11, h, rows, :] = v
        units = [(wi, p) for wi in range(2) for p in range(3)]
        for g in range(0, 6, 6):
            part = units[g : g + 6]
            scores = []
            for wi, p in part:
                r, c = slice(wi * WIN, (wi + 1) * WIN), slice(p * 128, (p + 1) * 128)
                bb = bias[b * 2 + wi]
                scores.append(mm_nt(k[r, c], stacked(q[r, c], sc0, sc1)) + jnp.concatenate([bb, bb], axis=1))
            expo = [jnp.exp(s - jnp.max(s, axis=0, keepdims=True)) for s in scores]
            pbs = [(e * (1.0 / jnp.sum(e, axis=0, keepdims=True))).astype(BF) for e in expo]
            for (wi, p), pb in zip(part, pbs):
                r, c = slice(wi * WIN, (wi + 1) * WIN), slice(p * 128, (p + 1) * 128)
                probs[b * 2 + wi, h, p] = pb
                o = mm_tn(pb, v[r, c])
                o = jnp.where(low, o[:WIN], o[WIN:])
                A[8, h, pl.ds(pl.multiple_of(b * ROWS + wi * WIN, WIN), WIN), c] = o.astype(BF)

        hook("attend", i)
        at(i, 3, own_done)
        return carry

    def own_done():
        weights_ready(range(6))
        bias_copy.wait()

    lax.fori_loop(0, 2 * BLOCKS, attend, 0)

    def joined(k, rows):
        return jnp.concatenate([A[k, 0, rows, :], A[k, 1, rows, :]], axis=1)

    def normalize(hidden):
        center = hidden - row_mean(hidden)
        rs = lax.rsqrt(row_mean(center * center) + EPS)
        return center * rs, rs

    def add_vec(row, value):
        sums[0, row : row + 1, :] += value[:, :HALF]
        sums[0, row + 1 : row + 2, :] += value[:, HALF:]


    loads[4].wait()
    hook("pre_norm")
    weights_ready([6])

    def first_norm(i, carry):
        hidden = []
        for n in range(2):
            b = 2 * i + n
            mixed = joined(8, block_rows(b))
            hidden.append(x_ref[b].astype(F32) + mm(mixed[:, :HALF], wo[0]) + mm(mixed[:, HALF:], wo[1]) + out_b)
        for n in range(2):
            rows = block_rows(2 * i + n)
            value, rs = normalize(hidden[n])
            normed[rows, :] = value
            spread[rows, :] = rs
            first = value * gain1 + shift1
            FL[0, rows, :] = first[:, :HALF].astype(BF)
            FL[1, rows, :] = first[:, HALF:].astype(BF)
        hook("norm1", i)
        return carry

    lax.fori_loop(0, BLOCKS // 2, first_norm, 0)
    loads[5].wait()
    loads[6].wait()

    def low_rows(rows):
        return jnp.concatenate([FL[0, rows, :], FL[1, rows, :]], axis=1)

    def half_inner(b, h):
        return mm(low_rows(block_rows(b)), w1[h]) + hv[h, 0:1, :]

    def half_feed(b, h):
        return half_rest(b, h, half_inner(b, h))

    def half_rest(b, h, inner_all):
        rows = block_rows(b)
        acts = []
        for k in range(4):
            inner = inner_all[:, k * HALF : (k + 1) * HALF]
            phi = 0.5 + 0.5 * lax.erf(inner * 0.7071067811865476)
            slope = phi + inner * jnp.exp(-0.5 * inner * inner) * 0.3989422804014327
            act = (inner * phi).astype(BF)
            A[k, h, rows, :] = act
            A[4 + k, h, rows, :] = slope.astype(BF)
            acts.append(act)
        return mm(jnp.concatenate(acts, axis=1), w2[h])

    def cot_copy(b, slot):
        return pltpu.make_async_copy(cot_hbm.at[b], GT.at[pl.ds(slot * ROWS, ROWS), pl.ds(0, WIDTH)], psem.at[slot])

    cot_copy(0, 0).start()
    cot_copy(1, 1).start()

    def feed_own(i, carry):
        both = [half_inner(2 * i + n, t) for n in range(2)]
        for n in range(2):
            acc[block_rows(2 * i + n), :] = half_rest(2 * i + n, t, both[n])
        hook("own", i)
        return carry

    lax.fori_loop(0, BLOCKS // 2, feed_own, 0)
    hook("pre_other")
    weights_ready(range(7, 15))

    def second_norm(i, carry):
        inners = [half_inner(2 * i + n, 1 - t) for n in range(2)]
        reds = [acc[block_rows(2 * i + n), :] + half_rest(2 * i + n, 1 - t, inners[n]) for n in range(2)]
        for n in range(2):
            b = 2 * i + n
            rows = block_rows(b)
            value, rs = normalize(normed[rows, :] * gain1 + shift1 + reds[n] + red_b)

            @pl.when(i >= 1)
            def _(b=b, n=n):
                pltpu.make_async_copy(stage.at[n], out_hbm.at[b - 2], osem.at[n]).wait()

            stage[n] = value * gain2 + shift2
            pltpu.make_async_copy(stage.at[n], out_hbm.at[b], osem.at[n]).start()
            cot_copy(b, n).wait()
            c = GT[n * ROWS : (n + 1) * ROWS, 0:WIDTH].astype(F32)

            @pl.when(i + 1 < BLOCKS // 2)
            def _(b=b, n=n):
                cot_copy(b + 2, n).start()

            add_vec(14, col_sum(c))
            add_vec(12, col_sum(c * value))
            u = c * gain2
            gs = rs * (u - row_mean(u) - value * row_mean(u * value))
            add_vec(10, col_sum(gs))
            acc[rows, :] = gs
        return carry

    lax.fori_loop(0, BLOCKS // 2, second_norm, 0)
    for b in range(2):
        pltpu.make_async_copy(stage.at[b], out_hbm.at[b + 2], osem.at[b]).wait()

    def span(i):
        return WIDTH >> (i + 1)

    def lo(j, i):
        return sum((bit[ORDERS[j][n]] * span(n) for n in range(i + 1)), 0)

    def ds(at_, n):
        return pl.ds(pl.multiple_of(at_, 16), n)

    def held(j, h, r):
        k, first, width = PARTS[j]
        if k < 9:
            return A, (k, h, r, pl.ds(first, width))
        return w1, (h, r, pl.ds((k - 9) * HALF + first, width))

    def add_in(j, h, r, value):
        ref, at_ = held(j, h, r)
        ref[at_] = ref[at_] + value

    def view(j, h, r):
        ref, at_ = held(j, h, r)
        return ref.at[at_]

    def landing(j, p):
        k, first, width = PARTS[j]
        c = pl.ds(first, width)
        if p == 0:
            return R0, (SEQUENCE.index(k) % 4, slice(None), slice(None), c)
        if p == 1 and k in LATE:
            return RB, (LATE.index(k), slice(None), slice(None), c)
        if p == 1:
            return R1, (k - sum(n < k for n in LATE), slice(None), c)
        return (R2, R3, R4)[p - 2], (k, slice(None), c)

    halves = [("half", i) for i in range(1, split)]
    swaps_ = [("swap", i) for i in range(bits - split)]
    gathers = [("gather", i) for i in reversed(range(1, split))]

    def names_of(j):
        mid = halves + swaps_ + gathers
        if PARTS[j][0] in LATE:
            return [("core", 0), ("both", 1), ("tensor", 1)] + mid[1:] + [("gather", 0)]
        return [("core", 0), ("tensor", 0)] + mid + [("gather", 0)]

    def begin(j, s):
        piece_copy(j, s).start()

    def piece_copy(j, s):
        kind, i = names_of(j)[s]
        way = ORDERS[j]
        k, first, width = PARTS[j]
        if kind == "core":
            src, who = view(j, slice(None), ds((1 - bit[way[0]]) * span(0), span(0))), mate(way[0])
            land, at_ = landing(j, 0)
            dst = land.at[at_]
        elif kind == "tensor":
            src, who = view(j, 1 - t, ds(lo(j, i), span(i))), across
            land, at_ = landing(j, i + 1)
            dst = land.at[at_]
        elif kind == "both":
            src, who = view(j, slice(None), ds(lo(j, 0) + (1 - bit[way[1]]) * span(1), span(1))), mate(way[1])
            land, at_ = landing(j, 1)
            dst = land.at[at_]
        elif kind == "half":
            src = view(j, t, ds(lo(j, i - 1) + (1 - bit[way[i]]) * span(i), span(i)))
            who = mate(way[i])
            land, at_ = landing(j, i + 1)
            dst = land.at[at_]
        elif kind == "swap":
            src, who = view(j, t, ds(lo(j, split - 1), span(split - 1))), mate(split + i)
            dst = RX.at[i, k, :, pl.ds(first, width)]
        else:
            r = ds(lo(j, i), span(i))
            dst, who = grad_hbm.at[k, r, pl.ds(first, width)], mate(way[i])
            src = view(j, t, r) if i == split - 1 and i > 0 else dst
        if kind == "swap":
            landed = xrecv.at[i, j]
        else:
            key = {"core": "c", "tensor": "y", "gather": "g"}.get(kind, "r")
            landed = grecv.at[LANDED[key if kind in ("core", "tensor") else f"{key}{way[i]}"][j]]
        return pltpu.make_async_remote_copy(
            src_ref=src, dst_ref=dst, send_sem=gsend.at[j], recv_sem=landed, device_id=who, device_id_type=MESH
        )

    def keep_copy(j):
        k, first, width = PARTS[j]
        r = ds(lo(j, split - 1), span(split - 1))
        return pltpu.make_async_copy(view(j, t, r), grad_hbm.at[k, r, pl.ds(first, width)], fsem.at[KEPT[j]])

    def settle(j, s):
        names = names_of(j)
        kind, i = names[s]
        k, first, width = PARTS[j]
        piece_copy(j, s).wait()
        if kind == "core":
            land, at_ = landing(j, 0)
            add_in(j, slice(None), ds(lo(j, 0), span(0)), land[at_])
        elif kind == "tensor":
            land, at_ = landing(j, i + 1)
            add_in(j, t, ds(lo(j, i), span(i)), land[at_])
        elif kind == "both":
            land, at_ = landing(j, 1)
            add_in(j, slice(None), ds(lo(j, 1), span(1)), land[at_])
        elif kind == "half":
            land, at_ = landing(j, i + 1)
            add_in(j, t, ds(lo(j, i), span(i)), land[at_])
        elif kind == "swap":
            add_in(j, t, ds(lo(j, split - 1), span(split - 1)), RX[i, k, :, pl.ds(first, width)])
        elif i == split - 1:
            keep_copy(j).wait()
        if s + 1 < len(names) and names[s + 1] == ("gather", split - 1):
            keep_copy(j).start()

    place = [0] * len(PARTS)

    def adv(*which):
        for k in which:
            s = place[k]
            names = names_of(k)
            if s > len(names):
                continue
            if s > 0:
                settle(k, s - 1)
            if s < len(names):
                begin(k, s)
            place[k] = s + 1

    swaps = [across] + [mate(i) for i in range(bits)]
    vec_place = [0]

    def adv_vec():
        s = vec_place[0]

        def cp(j):
            return pltpu.make_async_remote_copy(
                src_ref=sums.at[j], dst_ref=got.at[j], send_sem=vsend.at[j], recv_sem=vrecv.at[j],
                device_id=swaps[j], device_id_type=MESH,
            )

        if s > len(swaps):
            return
        if s > 0:
            cp(s - 1).wait()
            sums[s] = sums[s - 1] + got[s - 1]
        if s < len(swaps):
            cp(s).start()
        vec_place[0] = s + 1

    def transpose_into(dst, get):
        for b in range(BLOCKS):
            dst[:, b * ROWS : (b + 1) * ROWS] = get(b).T

    def rows_of(b):
        return slice(b * ROWS, (b + 1) * ROWS)

    def chunk_loop(name, first, count, left):
        def one(j, carry):
            k = first + j
            full = mm(left[...], joined(k, slice(None)))
            for h in range(2):
                part = full[:, h * HALF : (h + 1) * HALF].astype(BF)
                if first < 9:
                    A[k, h, 0:WIDTH, :] = part
                else:
                    w1[h, :, pl.ds(pl.multiple_of(j * HALF, HALF), HALF)] = part
            hook(name, j)
            return carry

        if count:
            lax.fori_loop(0, count, one, 0)

    transpose_into(GT, lambda b: acc[rows_of(b), :].astype(BF))
    chunk_loop("dw2", 0, 4, GT)
    transpose_into(FLT, lambda b: low_rows(rows_of(b)))
    hook("mid")

    def feed_back(b, carry):
        rows = block_rows(b)
        gs = acc[rows, :]
        gl = gs.astype(BF)
        gf = gs
        for h in range(2):
            da = mm_nt(gl, w2[h])
            gis = []
            for k in range(4):
                gi = (da[:, k * HALF : (k + 1) * HALF] * A[4 + k, h, rows, :].astype(F32)).astype(BF)
                A[4 + k, h, rows, :] = gi
                sums[0, 16 + 4 * h + k : 17 + 4 * h + k, :] += col_sum(gi.astype(F32))
                gis.append(gi)
            gf = gf + mm_nt(jnp.concatenate(gis, axis=1), w1[h])
        n = normed[rows, :]
        add_vec(6, col_sum(gf * n))
        add_vec(8, col_sum(gf))
        u = gf * gain1
        gh = spread[rows, :] * (u - row_mean(u) - n * row_mean(u * n))
        add_vec(4, col_sum(gh))
        acc[rows, :] = gh
        gm = gh.astype(BF)
        FL[0, rows, :] = mm_nt(gm, wo[0]).astype(BF)
        FL[1, rows, :] = mm_nt(gm, wo[1]).astype(BF)
        hook("back", b)
        return carry

    lax.fori_loop(0, BLOCKS, feed_back, 0)
    transpose_into(GT, lambda b: x_ref[b])
    chunk_loop("dw1", 4, FIRST_EXPAND, FLT)

    def attend_back(i, carry):
        h, b = i // BLOCKS, lax.rem(i, BLOCKS)

        def rows_at(wi):
            return pl.ds(pl.multiple_of(b * ROWS + wi * WIN, WIN), WIN)

        def at_(p):
            return slice(p * 128, (p + 1) * 128)

        sums_ = {}
        units = [(wi, p) for p in range(3) for wi in range(2)]
        for g in range(0, 6, 6):
            part = units[g : g + 6]
            do2 = [stacked(FL[h, rows_at(wi), at_(p)], mask0, mask1) for wi, p in part]
            dp = [mm_nt(A[11, h, rows_at(wi), at_(p)], d) for (wi, p), d in zip(part, do2)]
            dv = [mm(probs[b * 2 + wi, h, p], d).astype(BF) for (wi, p), d in zip(part, do2)]
            pf = [probs[b * 2 + wi, h, p].astype(F32) for wi, p in part]
            dsc = [(f * (d - jnp.sum(f * d, axis=0, keepdims=True))).astype(BF) for f, d in zip(pf, dp)]
            dk = [mm(d, stacked(A[9, h, rows_at(wi), at_(p)], sc0, sc1)).astype(BF) for (wi, p), d in zip(part, dsc)]
            dq = [mm_tn(d, A[10, h, rows_at(wi), at_(p)]) for (wi, p), d in zip(part, dsc)]
            for (wi, p), q_, k_, v_ in zip(part, dq, dk, dv):
                q_ = (jnp.where(low, q_[:WIN], q_[WIN:]) * 0.125).astype(BF)
                A[9, h, rows_at(wi), at_(p)] = q_
                A[10, h, rows_at(wi), at_(p)] = k_
                A[11, h, rows_at(wi), at_(p)] = v_
                add = col_sum(q_.astype(F32)), col_sum(v_.astype(F32))
                sums_[p] = add if p not in sums_ else (sums_[p][0] + add[0], sums_[p][1] + add[1])
        for p in range(3):
            hsum[h, 0:1, at_(p)] += sums_[p][0]
            hsum[h, 1:2, at_(p)] += sums_[p][1]
        hook("attb", i)
        return carry

    lax.fori_loop(0, 2 * BLOCKS, attend_back, 0)
    for h in range(2):
        sums[0, h : h + 1, :] = hsum[h, 0:1, :]
        sums[0, 2 + h : 3 + h, :] = hsum[h, 1:2, :]
    adv_vec()
    chunk_loop("dwq", 9, 3, GT)
    chunk_loop("dw1b", 4 + FIRST_EXPAND, 4 - FIRST_EXPAND, FLT)
    transpose_into(FLT, lambda b: acc[rows_of(b), :].astype(BF))
    chunk_loop("dwo", 8, 1, FLT)

    def input_grad(b, carry):
        rows = block_rows(b)
        g = acc[rows, :]
        for h in range(2):
            gp = jnp.concatenate([A[9 + i, h, rows, :] for i in range(3)], axis=1)
            g = g + mm_nt(gp, wqkv[h])
        slot = lax.rem(b, 2)

        @pl.when(b >= 2)
        def _():
            pltpu.make_async_copy(stage.at[slot], gin_hbm.at[b - 2], osem.at[slot]).wait()

        stage[slot] = g
        pltpu.make_async_copy(stage.at[slot], gin_hbm.at[b], osem.at[slot]).start()
        hook("gin", b)
        return carry

    lax.fori_loop(0, BLOCKS, input_grad, 0)
    hook("tail")
    for b in range(2):
        pltpu.make_async_copy(stage.at[b], gin_hbm.at[b + 2], osem.at[b]).wait()
    left = lambda: [j for j in range(len(PARTS)) if place[j] <= len(names_of(j))]
    while left():
        adv_vec()
        adv(*left())
    while vec_place[0] <= len(swaps):
        adv_vec()
    vec_out[...] = sums[len(swaps)]


def layer(n_dp, *operands):
    vm = pl.BlockSpec(memory_space=pltpu.VMEM)
    hbm = pl.BlockSpec(memory_space=pl.ANY)
    bits = n_dp.bit_length() - 1
    split = min(bits, 4)
    dma = pltpu.SemaphoreType.DMA
    return pl.pallas_call(
        functools.partial(kernel, bits),
        out_shape=(
            jax.ShapeDtypeStruct((BLOCKS, ROWS, WIDTH), F32),
            jax.ShapeDtypeStruct((BLOCKS, ROWS, WIDTH), F32),
            jax.ShapeDtypeStruct((CHUNKS, WIDTH, HALF), BF),
            jax.ShapeDtypeStruct((24, HALF), F32),
        ),
        in_specs=[hbm] * 19,
        out_specs=(hbm, hbm, hbm, vm),
        scratch_shapes=[
            pltpu.VMEM((BLOCKS, 2 * ROWS), jnp.int32),
            pltpu.VMEM((BLOCKS, 2 * ROWS), jnp.int32),
            pltpu.VMEM((HALF,), BF),
            pltpu.VMEM((HALF,), BF),
            pltpu.VMEM((HIDDEN,), BF),
            pltpu.VMEM((WIDTH,), BF),
            pltpu.VMEM((WIDTH,), BF),
            pltpu.VMEM((WIDTH,), BF),
            pltpu.VMEM((WIDTH,), BF),
            pltpu.VMEM((WIDTH,), BF),
            pltpu.VMEM((WIDTH,), BF),
            pltpu.VMEM((BLOCKS, ROWS, WIDTH), BF),
            pltpu.VMEM((2, WIDTH, 3 * HALF), BF),
            pltpu.VMEM((2, HALF, WIDTH), BF),
            pltpu.VMEM((2, WIDTH, HIDDEN), BF),
            pltpu.VMEM((2, HIDDEN, WIDTH), BF),
            pltpu.VMEM((2, 8, HIDDEN), F32),
            pltpu.VMEM((CHUNKS, 2, TOTAL, HALF), BF),
            pltpu.VMEM((2 * BLOCKS, 2, 3, WIN, 2 * WIN), BF),
            pltpu.VMEM((TOTAL, WIDTH), F32),
            pltpu.VMEM((TOTAL, 1), F32),
            pltpu.VMEM((TOTAL, WIDTH), F32),
            pltpu.VMEM((2, TOTAL, HALF), BF),
            pltpu.VMEM((WIDTH, TOTAL), BF),
            pltpu.VMEM((WIDTH, TOTAL), BF),
            pltpu.VMEM((2 * BLOCKS, WIN, WIN), F32),
            pltpu.VMEM((2, ROWS, WIDTH), F32),
            pltpu.VMEM((bits + 2, 24, HALF), F32),
            pltpu.VMEM((bits + 1, 24, HALF), F32),
            pltpu.VMEM((2, 8, HALF), F32),
            pltpu.VMEM((4, 2, WIDTH // 2, HALF), BF),
            pltpu.VMEM((CHUNKS - len(LATE), WIDTH // 2, HALF), BF),
            pltpu.VMEM((max(len(LATE), 1), 2, WIDTH // 4, HALF), BF),
            pltpu.VMEM((CHUNKS, WIDTH // 4, HALF), BF),
            pltpu.VMEM((CHUNKS, WIDTH // 8, HALF), BF),
            pltpu.VMEM((CHUNKS, WIDTH // 16, HALF), BF),
            pltpu.VMEM((max(bits - split, 1), CHUNKS, WIDTH >> split, HALF), BF),
            dma((11,)),
            dma((7,)),
            dma((2,)),
            dma((max(KEPT) + 1,)),
            dma((15,)),
            dma((4, 15)),
            dma((len(PARTS),)),
            dma((LANDED_COUNT,)),
            dma((bits + 1,)),
            dma((bits + 1,)),
            dma((2,)),
            dma((2,)),
            dma((max(bits - split, 1), len(PARTS) if bits > split else 1)),
        ],
        compiler_params=pltpu.CompilerParams(
            vmem_limit_bytes=67043328, collective_id=0, has_side_effects=True
        ),
    )(*operands)


def finish_kernel(
    grad_hbm, out_low, gin_low, vec_hbm, outg, ging, wqg, wkg, wvg, wog, w1g, w2g, qbg, vbg, obg, g1g, s1g, ebg, rbg, g2g, s2g,
    low, wide, turned, rows, vec, isem, osem, rsem, ssem, vsem,
):
    t = lax.axis_index("tensor")
    vec_copy = pltpu.make_async_copy(vec_hbm, vec, vsem.at[0])
    vec_copy.start()
    fetch = [pltpu.make_async_copy(grad_hbm.at[k], low.at[k], isem.at[k]) for k in range(CHUNKS)]
    order = [0, 1, 2, 3, 8] + list(range(4, 8)) + list(range(9, 12))
    for k in order:
        fetch[k].start()
    passed = []
    for i, ref in enumerate((out_low, gin_low)):
        cp = pltpu.make_async_copy(ref, rows.at[i], rsem.at[i])
        cp.start()
        passed.append(cp)

    sends = []
    for k in order:
        fetch[k].wait()
        if k >= 9:
            wide[k - 5] = low[k].astype(F32)
            src, dst = wide.at[k - 5], (wqg, wkg, wvg)[k - 9]
        elif k >= 4 and k < 8:
            wide[k - 4] = low[k].astype(F32)
            src, dst = wide.at[k - 4], w1g.at[:, pl.ds((k - 4) * HALF, HALF)]
        elif k == 8:
            turned[4] = low[k].astype(F32).T
            src, dst = turned.at[4], wog
        else:
            turned[k] = low[k].astype(F32).T
            src, dst = turned.at[k], w2g.at[pl.ds(k * HALF, HALF), :]
        cp = pltpu.make_async_copy(src, dst, osem.at[k])
        cp.start()
        sends.append(cp)
    for i, ref in enumerate((outg, ging)):
        passed[i].wait()
        cp = pltpu.make_async_copy(rows.at[i], ref, ssem.at[i])
        cp.start()
        sends.append(cp)
    vec_copy.wait()

    def pick(r):
        return jnp.where(t == 0, vec[r : r + 1, :], vec[r + 1 : r + 2, :]).reshape(HALF)

    def whole(r):
        return jnp.concatenate([vec[r : r + 1, :], vec[r + 1 : r + 2, :]], axis=1).reshape(WIDTH)

    qbg[...] = pick(0)
    vbg[...] = pick(2)
    for ref, r in ((obg, 4), (g1g, 6), (s1g, 8), (rbg, 10), (g2g, 12), (s2g, 14)):
        ref[...] = whole(r)
    lines = [jnp.where(t == 0, vec[16 + k : 17 + k, :], vec[20 + k : 21 + k, :]) for k in range(4)]
    ebg[...] = jnp.concatenate(lines, axis=1).reshape(HIDDEN)

    for cp in sends:
        cp.wait()


def finish(out, gin, grads, vec):
    vm = pl.BlockSpec(memory_space=pltpu.VMEM)
    hbm = pl.BlockSpec(memory_space=pltpu.HBM)
    f = lambda *shape: jax.ShapeDtypeStruct(shape, F32)
    return pl.pallas_call(
        finish_kernel,
        out_shape=(f(BLOCKS, ROWS, WIDTH), f(BLOCKS, ROWS, WIDTH), f(WIDTH, HALF), f(WIDTH, HALF), f(WIDTH, HALF), f(HALF, WIDTH), f(WIDTH, HIDDEN), f(HIDDEN, WIDTH),
                   f(HALF), f(HALF), f(WIDTH), f(WIDTH), f(WIDTH), f(HIDDEN), f(WIDTH), f(WIDTH), f(WIDTH)),
        in_specs=[hbm, hbm, hbm, hbm],
        out_specs=(hbm,) * 8 + (vm,) * 9,
        scratch_shapes=[
            pltpu.VMEM((CHUNKS, WIDTH, HALF), BF),
            pltpu.VMEM((7, WIDTH, HALF), F32),
            pltpu.VMEM((5, HALF, WIDTH), F32),
            pltpu.VMEM((2, BLOCKS, ROWS, WIDTH), F32),
            pltpu.VMEM((24, HALF), F32),
            pltpu.SemaphoreType.DMA((CHUNKS,)),
            pltpu.SemaphoreType.DMA((CHUNKS,)),
            pltpu.SemaphoreType.DMA((2,)),
            pltpu.SemaphoreType.DMA((2,)),
            pltpu.SemaphoreType.DMA((1,)),
        ],
        compiler_params=pltpu.CompilerParams(vmem_limit_bytes=67043328),
    )(grads, out, gin, vec)


def local(
    n_dp, inputs, segments, padding, query_weight, query_bias, key_weight, value_weight, value_bias,
    output_weight, output_bias, first_gain, first_shift, expand_weight, expand_bias,
    reduce_weight, reduce_bias, second_gain, second_shift, cotangent,
):
    out, gin, grads, vec = layer(
        n_dp, inputs, cotangent, segments, padding, query_bias, value_bias, expand_bias, output_bias, first_gain,
        first_shift, reduce_bias, second_gain, second_shift, query_weight, key_weight, value_weight,
        output_weight, expand_weight, reduce_weight,
    )
    out, gin, wq, wk, wv, wo, w1, w2, qb, vb, ob, g1, s1, eb, rb, g2, s2 = finish(out, gin, grads, vec)
    return (out, gin, wq, qb, wk, wv, vb, wo, ob, g1, s1, w1, eb, w2, rb, g2, s2)


def solution(mesh):
    tokens = P(None, ("dp", "tensor"), None)
    return jax.shard_map(
        functools.partial(local, mesh.shape["dp"]),
        mesh=mesh,
        in_specs=(
            tokens, P(None, "dp"), P(None, "dp"), P(None, "tensor"), P("tensor"), P(None, "tensor"),
            P(None, "tensor"), P("tensor"), P("tensor", None), P(), P(), P(), P(None, "tensor"),
            P("tensor"), P("tensor", None), P(), P(), P(), tokens,
        ),
        out_specs=(
            tokens, tokens, P(None, "tensor"), P("tensor"), P(None, "tensor"), P(None, "tensor"),
            P("tensor"), P("tensor", None), P(), P(), P(), P(None, "tensor"), P("tensor"),
            P("tensor", None), P(), P(), P(),
        ),
        check_vma=False,
    )
```

```python
import functools

import jax
import jax.numpy as jnp
from jax import lax
from jax.experimental import pallas as pl
from jax.experimental.pallas import tpu as pltpu
from jax.sharding import PartitionSpec as P

WIN = 128
BLOCKS = 4
ROWS = 256
TOTAL = BLOCKS * ROWS
WIDTH = 768
HALF = 384
HIDDEN = 1536
CHUNKS = 12
EPS = 1e-12
BF = jnp.bfloat16
F32 = jnp.float32
MESH = pl.DeviceIdType.MESH


def mm(a, b):
    return lax.dot_general(a, b, (((1,), (0,)), ((), ())), preferred_element_type=F32)


def mm_nt(a, b):
    return lax.dot_general(a, b, (((1,), (1,)), ((), ())), preferred_element_type=F32)


def mm_tn(a, b):
    return lax.dot_general(a, b, (((0,), (0,)), ((), ())), preferred_element_type=F32)


def row_mean(a):
    return jnp.sum(a, axis=-1, keepdims=True) * (1.0 / WIDTH)


def col_sum(a):
    return jnp.sum(a, axis=0, keepdims=True)

WAYS = ((2, 1, 0), (2, 1, 0), (2, 1, 0), (2, 1, 0), (1, 2, 0), (1, 2, 0), (2, 1, 0), (2, 0), (2, 0), (2, 1, 0), (2, 1, 0), (2, 1, 0), (2, 1, 0), (0,), (2, 0))
FIRST = (1, 4, 0, 3, 5, 2, 6, 11, 10, 12, 9, 7, 14, 8, 13)
PARTS = ((0, 0, 384), (1, 0, 384), (2, 0, 384), (3, 0, 384), (4, 0, 384), (5, 0, 384), (6, 0, 384), (7, 0, 384), (8, 0, 128), (8, 128, 128), (8, 256, 128), (9, 0, 384), (10, 0, 384), (11, 0, 128), (11, 128, 128), (11, 256, 128))
ORDERS = ((0, 1, 2, 3), (0, 1, 2, 3), (0, 1, 2, 3), (0, 1, 2, 3), (0, 1, 2, 3), (0, 1, 2, 3), (0, 1, 2, 3), (0, 1, 2, 3), (0, 1, 2, 3), (0, 1, 2, 3), (0, 1, 2, 3), (0, 1, 2, 3), (0, 1, 2, 3), (0, 1, 2, 3), (0, 1, 2, 3), (0, 1, 2, 3))
LATE = (1, 3, 4, 6)
SEQUENCE = (0, 1, 2, 3, 4, 5, 6, 7, 9, 10, 11, 8)
FIRST_EXPAND = 4
PLAN = {
    "attend": ((1, (1,)), (2, (4,)), (3, (0, 1, 3, 5, 4, 2, 0, 6, 3, 1, 5, 11, 1, 4, 2, 0, 10, 4, 0, 6, 3, 12, 3, 5, 2, 9, 5, 11, 2)), (5, (6, 7, 10)), (6, (6, 12)), (7, (9, 11, 14)),),
    "norm1": ((0, (11,)), (1, (7, 8, 10)),),
    "own": ((0, (7, 10, 12, 14)), (1, (8, 9, 12, 13, 14)),),
    "pre_other": ((0, (8, 9, 13)),),
    "dw2": ((0, (20,)), (1, (21,)), (2, (20, 22)), (3, (21, 23)),),
    "back": ((0, (22, 23)), (1, (20, 21)), (3, (21, 22, 23)),),
    "dw1": ((0, (24, 20)), (1, (25,)), (2, (24, 26, 21)), (3, (25, 27, 20, 22, 23)),),
    "attb": ((0, (26,)), (1, (27,)), (2, (21,)), (3, (20, 22)), (5, (23, 24)), (7, (21, 25)),),
    "dwq": ((0, (31, 20)), (1, (32,)), (2, (31, 33, 34, 35, 22, 26, 21, 32, 23)),),
    "dwo": ((0, (33, 34, 35, 28, 29, 30, 20, 25, 27)),),
    "gin": ((0, (28, 29, 30, 22, 24, 40)), (1, (21, 23, 25, 40)), (3, (21, 22)),),
    "tail": ((0, (20, 24, 20, 23, 31, 27, 40, 25, 26, 24, 27, 22, 40, 22, 25, 26, 23, 32, 23, 24, 31, 27, 33, 40, 25, 34, 32, 26, 33, 24, 35, 31, 28, 25, 27, 32, 34, 29, 25, 33, 26, 30, 24, 31, 27, 35, 24, 28, 34, 32, 29, 33, 30, 26, 35, 28, 31, 27, 34, 29, 27, 32, 30, 33, 35, 26, 28, 31, 26, 34, 29, 32, 33, 30, 35, 34, 31, 28, 29, 31, 30, 35, 28, 32, 29, 30, 33, 32, 34, 33, 35, 34, 28, 35, 29, 28, 30, 29, 30)),),
}
LANDED = {
    "c": (0, 1, 2, 3, 0, 1, 2, 3, 0, 5, 6, 0, 1, 2, 3, 4),
    "g0": (8, 7, 7, 8, 8, 7, 8, 7, 8, 9, 7, 7, 8, 9, 7, 10),
    "g1": (12, 11, 13, 14, 12, 11, 14, 13, 14, 17, 18, 11, 12, 15, 16, 13),
    "g2": (20, 19, 21, 22, 20, 19, 22, 21, 19, 24, 25, 19, 20, 23, 21, 22),
    "g3": (27, 26, 28, 29, 27, 26, 29, 28, 31, 26, 32, 26, 27, 30, 28, 29),
    "r1": (35, 33, 36, 34, 37, 34, 33, 35, 36, 38, 39, 36, 33, 34, 37, 35),
    "r2": (41, 40, 42, 43, 41, 40, 43, 42, 45, 40, 41, 40, 41, 44, 42, 43),
    "r3": (47, 46, 48, 49, 47, 46, 49, 48, 51, 46, 52, 46, 47, 50, 48, 49),
    "y": (53, 55, 54, 53, 55, 56, 58, 54, 53, 63, 64, 57, 59, 60, 61, 62),
}
LANDED_COUNT = 65
KEPT = (1, 0, 0, 1, 1, 0, 1, 0, 2, 0, 3, 0, 1, 2, 0, 1)


def kernel(
    bits,
    x_hbm, cot_hbm, seg_hbm, pad_hbm, qb_hbm, vb_hbm, eb_hbm, ob_hbm, g1_hbm, s1_hbm, rb_hbm, g2_hbm, s2_hbm,
    wq_hbm, wk_hbm, wv_hbm, wo_hbm, w1_hbm, w2_hbm,
    out_hbm, gin_hbm, grad_hbm, vec_out,
    seg_ref, pad_ref, qb_ref, vb_ref, eb_ref, ob_ref, g1_ref, s1_ref, rb_ref, g2_ref, s2_ref,
    x_ref, wqkv, wo, w1, w2, hv, A, probs, normed, spread, acc, FL, FLT, GT, bias, stage, sums, got, hsum,
    R0, R1, RB, R2, R3, R4, RX,
    isem, lsem, osem, fsem, wsend, wrecv, gsend, grecv, vsend, vrecv, bsem, psem, xrecv,
):
    t = lax.axis_index("tensor")
    me = lax.axis_index("dp")
    bit = [lax.rem(me // (1 << i), 2) for i in range(bits)]
    split = min(bits, 4)

    def mate(i):
        return (me + (1 << i) * (1 - 2 * bit[i]), t)

    across = (me, 1 - t)
    partners = [across] + [mate(i) for i in range(bits)]

    barrier = pltpu.get_barrier_semaphore()
    for who in partners:
        pl.semaphore_signal(barrier, inc=1, device_id=who, device_id_type=MESH)

    smalls = [
        (seg_hbm, seg_ref),
        (pad_hbm, pad_ref),
        (qb_hbm, qb_ref),
        (vb_hbm, vb_ref),
        (eb_hbm, eb_ref),
        (ob_hbm, ob_ref),
        (g1_hbm, g1_ref),
        (s1_hbm, s1_ref),
        (rb_hbm, rb_ref),
        (g2_hbm, g2_ref),
        (s2_hbm, s2_ref),
    ]
    smalls = [pltpu.make_async_copy(s, d, isem.at[i]) for i, (s, d) in enumerate(smalls)]
    for cp in smalls:
        cp.start()

    locals_ = [
        (x_hbm, x_ref),
        (wq_hbm, wqkv.at[t, :, pl.ds(0, HALF)]),
        (wk_hbm, wqkv.at[t, :, pl.ds(HALF, HALF)]),
        (wv_hbm, wqkv.at[t, :, pl.ds(2 * HALF, HALF)]),
        (wo_hbm, wo.at[t]),
        (w1_hbm, w1.at[t]),
        (w2_hbm, w2.at[t]),
    ]
    loads = [pltpu.make_async_copy(s, d, lsem.at[i]) for i, (s, d) in enumerate(locals_)]
    for cp in loads:
        cp.start()

    for cp in smalls:
        cp.wait()

    def row(ref):
        return ref[...].astype(F32).reshape(1, ref.shape[0])

    hv[t] = jnp.zeros((8, HIDDEN), F32)
    hv[t, 0:1, :] = row(eb_ref)
    hv[t, 1:2, 0:HALF] = row(qb_ref)
    hv[t, 1:2, HALF : 2 * HALF] = row(vb_ref)
    out_b, gain1, shift1 = row(ob_ref), row(g1_ref), row(s1_ref)
    red_b, gain2, shift2 = row(rb_ref), row(g2_ref), row(s2_ref)
    sums[0] = jnp.zeros((24, HALF), F32)
    hsum[...] = jnp.zeros_like(hsum)
    lane = lax.broadcasted_iota(jnp.int32, (1, 128), 1)
    low = lane < 64
    mask0 = jnp.where(low, 1.0, 0.0).astype(BF)
    mask1 = jnp.where(low, 0.0, 1.0).astype(BF)
    sc0 = jnp.where(low, 0.125, 0.0).astype(BF)
    sc1 = jnp.where(low, 0.0, 0.125).astype(BF)

    for b in range(BLOCKS):
        for wi in range(2):
            cols = pl.ds(pl.multiple_of(t * ROWS + wi * WIN, WIN), WIN)
            seg = jnp.broadcast_to(seg_ref[b : b + 1, cols].astype(F32), (WIN, WIN))
            live = jnp.broadcast_to(pad_ref[b : b + 1, cols].astype(F32), (WIN, WIN))
            bias[2 * b + wi] = jnp.where((seg == seg.T) & (live.T > 0.5), 0.0, -1e30)

    pl.semaphore_wait(barrier, len(partners))

    def part_rows(base, n, ways, fixed):
        size = n // (1 << len(ways))
        at_ = sum((bit[w] * (size << j) for j, w in enumerate(ways)), 0)
        free = len(ways) - fixed
        at_ = sum((bit[w] * (size << j) for j, w in enumerate(ways) if j >= free), 0)
        return pl.ds(pl.multiple_of(base + at_, 16), size << free)

    def cols(i):
        return pl.ds(i * HALF, HALF)

    every = pl.ds(0, WIDTH)
    pieces = [
        (src, pl.ds(0, HALF), wqkv, cols(i), base, HALF)
        for i, src in enumerate((wq_hbm, wk_hbm, wv_hbm))
        for base in (0, HALF)
    ]
    pieces += [(wo_hbm, every, wo, every, 0, HALF)]
    pieces += [(w1_hbm, cols(i), w1, cols(i), 0, WIDTH) for i in range(4)]
    pieces += [(w2_hbm, every, w2, every, i * HALF, HALF) for i in range(4)]

    def weight_copy(g, s):
        hbm, hc, dst, dc, base, n = pieces[g]
        ways = WAYS[g]
        r = part_rows(base, n, ways, len(ways) - max(s - 1, 0))
        if s == 0:
            src, to, who = hbm.at[r, hc], dst.at[t, r, dc], across
        else:
            src = to = dst.at[1 - t, r, dc]
            who = mate(ways[s - 1])
        return pltpu.make_async_remote_copy(
            src_ref=src, dst_ref=to, send_sem=wsend.at[g], recv_sem=wrecv.at[s, g],
            device_id=who, device_id_type=MESH,
        )

    wplace = [0] * len(pieces)

    def adv_weight(g):
        s, last = wplace[g], len(WAYS[g])
        if s > 0:
            weight_copy(g, s - 1).wait()
        if s <= last:
            weight_copy(g, s).start()
        wplace[g] = s + 1

    def weights_ready(which):
        while min(wplace[g] - len(WAYS[g]) for g in which) < 2:
            for g in which:
                if wplace[g] < len(WAYS[g]) + 2:
                    adv_weight(g)

    bias_copy = pltpu.make_async_remote_copy(
        src_ref=hv.at[t], dst_ref=hv.at[t], send_sem=bsem.at[0], recv_sem=bsem.at[1],
        device_id=across, device_id_type=MESH,
    )
    bias_copy.start()
    for g in FIRST:
        adv_weight(g)

    def run(ops):
        for op in ops:
            if op < 20:
                adv_weight(op)
            elif op < 40:
                adv(op - 20)
            else:
                adv_vec()

    def at(loop_index, step, action):
        @pl.when(loop_index == step)
        def _():
            action()

    def hook(name, loop_index=None):
        for step, ops in PLAN.get(name, ()):
            if loop_index is None:
                run(ops)
            else:
                at(loop_index, step, lambda ops=ops: run(ops))

    def stacked(a, m0, m1):
        return jnp.concatenate([a * m0, a * m1], axis=0)

    def block_rows(b):
        return pl.ds(pl.multiple_of(b * ROWS, ROWS), ROWS)

    for cp in loads[:4]:
        cp.wait()

    def attend(i, carry):
        b = lax.rem(i, BLOCKS)
        h = t + (i // BLOCKS) * (1 - 2 * t)
        rows = block_rows(b)
        pr = mm(x_ref[b], wqkv[h])
        q = (pr[:, :HALF] + hv[h, 1:2, 0:HALF]).astype(BF)
        k = pr[:, HALF : 2 * HALF].astype(BF)
        v = (pr[:, 2 * HALF :] + hv[h, 1:2, HALF : 2 * HALF]).astype(BF)
        A[9, h, rows, :] = q
        A[10, h, rows, :] = k
        A[11, h, rows, :] = v
        units = [(wi, p) for wi in range(2) for p in range(3)]
        for g in range(0, 6, 6):
            part = units[g : g + 6]
            scores = []
            for wi, p in part:
                r, c = slice(wi * WIN, (wi + 1) * WIN), slice(p * 128, (p + 1) * 128)
                bb = bias[b * 2 + wi]
                scores.append(mm_nt(k[r, c], stacked(q[r, c], sc0, sc1)) + jnp.concatenate([bb, bb], axis=1))
            expo = [jnp.exp(s - jnp.max(s, axis=0, keepdims=True)) for s in scores]
            pbs = [(e * (1.0 / jnp.sum(e, axis=0, keepdims=True))).astype(BF) for e in expo]
            for (wi, p), pb in zip(part, pbs):
                r, c = slice(wi * WIN, (wi + 1) * WIN), slice(p * 128, (p + 1) * 128)
                probs[b * 2 + wi, h, p] = pb
                o = mm_tn(pb, v[r, c])
                o = jnp.where(low, o[:WIN], o[WIN:])
                A[8, h, pl.ds(pl.multiple_of(b * ROWS + wi * WIN, WIN), WIN), c] = o.astype(BF)

        hook("attend", i)
        at(i, 3, own_done)
        return carry

    def own_done():
        weights_ready(range(6))
        bias_copy.wait()

    lax.fori_loop(0, 2 * BLOCKS, attend, 0)

    def joined(k, rows):
        return jnp.concatenate([A[k, 0, rows, :], A[k, 1, rows, :]], axis=1)

    def normalize(hidden):
        center = hidden - row_mean(hidden)
        rs = lax.rsqrt(row_mean(center * center) + EPS)
        return center * rs, rs

    def add_vec(row, value):
        sums[0, row : row + 1, :] += value[:, :HALF]
        sums[0, row + 1 : row + 2, :] += value[:, HALF:]


    loads[4].wait()
    hook("pre_norm")
    weights_ready([6])

    def first_norm(i, carry):
        hidden = []
        for n in range(2):
            b = 2 * i + n
            mixed = joined(8, block_rows(b))
            hidden.append(x_ref[b].astype(F32) + mm(mixed[:, :HALF], wo[0]) + mm(mixed[:, HALF:], wo[1]) + out_b)
        for n in range(2):
            rows = block_rows(2 * i + n)
            value, rs = normalize(hidden[n])
            normed[rows, :] = value
            spread[rows, :] = rs
            first = value * gain1 + shift1
            FL[0, rows, :] = first[:, :HALF].astype(BF)
            FL[1, rows, :] = first[:, HALF:].astype(BF)
        hook("norm1", i)
        return carry

    lax.fori_loop(0, BLOCKS // 2, first_norm, 0)
    loads[5].wait()
    loads[6].wait()

    def low_rows(rows):
        return jnp.concatenate([FL[0, rows, :], FL[1, rows, :]], axis=1)

    def half_inner(b, h):
        return mm(low_rows(block_rows(b)), w1[h]) + hv[h, 0:1, :]

    def half_feed(b, h):
        return half_rest(b, h, half_inner(b, h))

    def half_rest(b, h, inner_all):
        rows = block_rows(b)
        acts = []
        for k in range(4):
            inner = inner_all[:, k * HALF : (k + 1) * HALF]
            phi = 0.5 + 0.5 * lax.erf(inner * 0.7071067811865476)
            slope = phi + inner * jnp.exp(-0.5 * inner * inner) * 0.3989422804014327
            act = (inner * phi).astype(BF)
            A[k, h, rows, :] = act
            A[4 + k, h, rows, :] = slope.astype(BF)
            acts.append(act)
        return mm(jnp.concatenate(acts, axis=1), w2[h])

    def cot_copy(b, slot):
        return pltpu.make_async_copy(cot_hbm.at[b], GT.at[pl.ds(slot * ROWS, ROWS), pl.ds(0, WIDTH)], psem.at[slot])

    cot_copy(0, 0).start()
    cot_copy(1, 1).start()

    def feed_own(i, carry):
        both = [half_inner(2 * i + n, t) for n in range(2)]
        for n in range(2):
            acc[block_rows(2 * i + n), :] = half_rest(2 * i + n, t, both[n])
        hook("own", i)
        return carry

    lax.fori_loop(0, BLOCKS // 2, feed_own, 0)
    hook("pre_other")
    weights_ready(range(7, 15))

    def second_norm(i, carry):
        inners = [half_inner(2 * i + n, 1 - t) for n in range(2)]
        reds = [acc[block_rows(2 * i + n), :] + half_rest(2 * i + n, 1 - t, inners[n]) for n in range(2)]
        for n in range(2):
            b = 2 * i + n
            rows = block_rows(b)
            value, rs = normalize(normed[rows, :] * gain1 + shift1 + reds[n] + red_b)

            @pl.when(i >= 1)
            def _(b=b, n=n):
                pltpu.make_async_copy(stage.at[n], out_hbm.at[b - 2], osem.at[n]).wait()

            stage[n] = (value * gain2 + shift2).astype(BF)
            pltpu.make_async_copy(stage.at[n], out_hbm.at[b], osem.at[n]).start()
            cot_copy(b, n).wait()
            c = GT[n * ROWS : (n + 1) * ROWS, 0:WIDTH].astype(F32)

            @pl.when(i + 1 < BLOCKS // 2)
            def _(b=b, n=n):
                cot_copy(b + 2, n).start()

            add_vec(14, col_sum(c))
            add_vec(12, col_sum(c * value))
            u = c * gain2
            gs = rs * (u - row_mean(u) - value * row_mean(u * value))
            add_vec(10, col_sum(gs))
            acc[rows, :] = gs
        return carry

    lax.fori_loop(0, BLOCKS // 2, second_norm, 0)
    for b in range(2):
        pltpu.make_async_copy(stage.at[b], out_hbm.at[b + 2], osem.at[b]).wait()

    def span(i):
        return WIDTH >> (i + 1)

    def lo(j, i):
        return sum((bit[ORDERS[j][n]] * span(n) for n in range(i + 1)), 0)

    def ds(at_, n):
        return pl.ds(pl.multiple_of(at_, 16), n)

    def held(j, h, r):
        k, first, width = PARTS[j]
        if k < 9:
            return A, (k, h, r, pl.ds(first, width))
        return w1, (h, r, pl.ds((k - 9) * HALF + first, width))

    def add_in(j, h, r, value):
        ref, at_ = held(j, h, r)
        ref[at_] = ref[at_] + value

    def view(j, h, r):
        ref, at_ = held(j, h, r)
        return ref.at[at_]

    def landing(j, p):
        k, first, width = PARTS[j]
        c = pl.ds(first, width)
        if p == 0:
            return R0, (SEQUENCE.index(k) % 4, slice(None), slice(None), c)
        if p == 1 and k in LATE:
            return RB, (LATE.index(k), slice(None), slice(None), c)
        if p == 1:
            return R1, (k - sum(n < k for n in LATE), slice(None), c)
        return (R2, R3, R4)[p - 2], (k, slice(None), c)

    halves = [("half", i) for i in range(1, split)]
    swaps_ = [("swap", i) for i in range(bits - split)]
    gathers = [("gather", i) for i in reversed(range(1, split))]

    def names_of(j):
        mid = halves + swaps_ + gathers
        if PARTS[j][0] in LATE:
            return [("core", 0), ("both", 1), ("tensor", 1)] + mid[1:] + [("gather", 0)]
        return [("core", 0), ("tensor", 0)] + mid + [("gather", 0)]

    def begin(j, s):
        piece_copy(j, s).start()

    def piece_copy(j, s):
        kind, i = names_of(j)[s]
        way = ORDERS[j]
        k, first, width = PARTS[j]
        if kind == "core":
            src, who = view(j, slice(None), ds((1 - bit[way[0]]) * span(0), span(0))), mate(way[0])
            land, at_ = landing(j, 0)
            dst = land.at[at_]
        elif kind == "tensor":
            src, who = view(j, 1 - t, ds(lo(j, i), span(i))), across
            land, at_ = landing(j, i + 1)
            dst = land.at[at_]
        elif kind == "both":
            src, who = view(j, slice(None), ds(lo(j, 0) + (1 - bit[way[1]]) * span(1), span(1))), mate(way[1])
            land, at_ = landing(j, 1)
            dst = land.at[at_]
        elif kind == "half":
            src = view(j, t, ds(lo(j, i - 1) + (1 - bit[way[i]]) * span(i), span(i)))
            who = mate(way[i])
            land, at_ = landing(j, i + 1)
            dst = land.at[at_]
        elif kind == "swap":
            src, who = view(j, t, ds(lo(j, split - 1), span(split - 1))), mate(split + i)
            dst = RX.at[i, k, :, pl.ds(first, width)]
        else:
            r = ds(lo(j, i), span(i))
            dst, who = grad_hbm.at[k, r, pl.ds(first, width)], mate(way[i])
            src = view(j, t, r) if i == split - 1 and i > 0 else dst
        if kind == "swap":
            landed = xrecv.at[i, j]
        else:
            key = {"core": "c", "tensor": "y", "gather": "g"}.get(kind, "r")
            landed = grecv.at[LANDED[key if kind in ("core", "tensor") else f"{key}{way[i]}"][j]]
        return pltpu.make_async_remote_copy(
            src_ref=src, dst_ref=dst, send_sem=gsend.at[j], recv_sem=landed, device_id=who, device_id_type=MESH
        )

    def keep_copy(j):
        k, first, width = PARTS[j]
        r = ds(lo(j, split - 1), span(split - 1))
        return pltpu.make_async_copy(view(j, t, r), grad_hbm.at[k, r, pl.ds(first, width)], fsem.at[KEPT[j]])

    def settle(j, s):
        names = names_of(j)
        kind, i = names[s]
        k, first, width = PARTS[j]
        piece_copy(j, s).wait()
        if kind == "core":
            land, at_ = landing(j, 0)
            add_in(j, slice(None), ds(lo(j, 0), span(0)), land[at_])
        elif kind == "tensor":
            land, at_ = landing(j, i + 1)
            add_in(j, t, ds(lo(j, i), span(i)), land[at_])
        elif kind == "both":
            land, at_ = landing(j, 1)
            add_in(j, slice(None), ds(lo(j, 1), span(1)), land[at_])
        elif kind == "half":
            land, at_ = landing(j, i + 1)
            add_in(j, t, ds(lo(j, i), span(i)), land[at_])
        elif kind == "swap":
            add_in(j, t, ds(lo(j, split - 1), span(split - 1)), RX[i, k, :, pl.ds(first, width)])
        elif i == split - 1:
            keep_copy(j).wait()
        if s + 1 < len(names) and names[s + 1] == ("gather", split - 1):
            keep_copy(j).start()

    place = [0] * len(PARTS)

    def adv(*which):
        for k in which:
            s = place[k]
            names = names_of(k)
            if s > len(names):
                continue
            if s > 0:
                settle(k, s - 1)
            if s < len(names):
                begin(k, s)
            place[k] = s + 1

    swaps = [across] + [mate(i) for i in range(bits)]
    vec_place = [0]

    def adv_vec():
        s = vec_place[0]

        def cp(j):
            return pltpu.make_async_remote_copy(
                src_ref=sums.at[j], dst_ref=got.at[j], send_sem=vsend.at[j], recv_sem=vrecv.at[j],
                device_id=swaps[j], device_id_type=MESH,
            )

        if s > len(swaps):
            return
        if s > 0:
            cp(s - 1).wait()
            sums[s] = sums[s - 1] + got[s - 1]
        if s < len(swaps):
            cp(s).start()
        vec_place[0] = s + 1

    def transpose_into(dst, get):
        for b in range(BLOCKS):
            dst[:, b * ROWS : (b + 1) * ROWS] = get(b).T

    def rows_of(b):
        return slice(b * ROWS, (b + 1) * ROWS)

    def chunk_loop(name, first, count, left):
        def one(j, carry):
            k = first + j
            full = mm(left[...], joined(k, slice(None)))
            for h in range(2):
                part = full[:, h * HALF : (h + 1) * HALF].astype(BF)
                if first < 9:
                    A[k, h, 0:WIDTH, :] = part
                else:
                    w1[h, :, pl.ds(pl.multiple_of(j * HALF, HALF), HALF)] = part
            hook(name, j)
            return carry

        if count:
            lax.fori_loop(0, count, one, 0)

    transpose_into(GT, lambda b: acc[rows_of(b), :].astype(BF))
    chunk_loop("dw2", 0, 4, GT)
    transpose_into(FLT, lambda b: low_rows(rows_of(b)))
    hook("mid")

    def feed_back(b, carry):
        rows = block_rows(b)
        gs = acc[rows, :]
        gl = gs.astype(BF)
        gf = gs
        for h in range(2):
            da = mm_nt(gl, w2[h])
            gis = []
            for k in range(4):
                gi = (da[:, k * HALF : (k + 1) * HALF] * A[4 + k, h, rows, :].astype(F32)).astype(BF)
                A[4 + k, h, rows, :] = gi
                sums[0, 16 + 4 * h + k : 17 + 4 * h + k, :] += col_sum(gi.astype(F32))
                gis.append(gi)
            gf = gf + mm_nt(jnp.concatenate(gis, axis=1), w1[h])
        n = normed[rows, :]
        add_vec(6, col_sum(gf * n))
        add_vec(8, col_sum(gf))
        u = gf * gain1
        gh = spread[rows, :] * (u - row_mean(u) - n * row_mean(u * n))
        add_vec(4, col_sum(gh))
        acc[rows, :] = gh
        gm = gh.astype(BF)
        FL[0, rows, :] = mm_nt(gm, wo[0]).astype(BF)
        FL[1, rows, :] = mm_nt(gm, wo[1]).astype(BF)
        hook("back", b)
        return carry

    lax.fori_loop(0, BLOCKS, feed_back, 0)
    transpose_into(GT, lambda b: x_ref[b])
    chunk_loop("dw1", 4, FIRST_EXPAND, FLT)

    def attend_back(i, carry):
        h, b = i // BLOCKS, lax.rem(i, BLOCKS)

        def rows_at(wi):
            return pl.ds(pl.multiple_of(b * ROWS + wi * WIN, WIN), WIN)

        def at_(p):
            return slice(p * 128, (p + 1) * 128)

        sums_ = {}
        units = [(wi, p) for p in range(3) for wi in range(2)]
        for g in range(0, 6, 6):
            part = units[g : g + 6]
            do2 = [stacked(FL[h, rows_at(wi), at_(p)], mask0, mask1) for wi, p in part]
            dp = [mm_nt(A[11, h, rows_at(wi), at_(p)], d) for (wi, p), d in zip(part, do2)]
            dv = [mm(probs[b * 2 + wi, h, p], d).astype(BF) for (wi, p), d in zip(part, do2)]
            pf = [probs[b * 2 + wi, h, p].astype(F32) for wi, p in part]
            dsc = [(f * (d - jnp.sum(f * d, axis=0, keepdims=True))).astype(BF) for f, d in zip(pf, dp)]
            dk = [mm(d, stacked(A[9, h, rows_at(wi), at_(p)], sc0, sc1)).astype(BF) for (wi, p), d in zip(part, dsc)]
            dq = [mm_tn(d, A[10, h, rows_at(wi), at_(p)]) for (wi, p), d in zip(part, dsc)]
            for (wi, p), q_, k_, v_ in zip(part, dq, dk, dv):
                q_ = (jnp.where(low, q_[:WIN], q_[WIN:]) * 0.125).astype(BF)
                A[9, h, rows_at(wi), at_(p)] = q_
                A[10, h, rows_at(wi), at_(p)] = k_
                A[11, h, rows_at(wi), at_(p)] = v_
                add = col_sum(q_.astype(F32)), col_sum(v_.astype(F32))
                sums_[p] = add if p not in sums_ else (sums_[p][0] + add[0], sums_[p][1] + add[1])
        for p in range(3):
            hsum[h, 0:1, at_(p)] += sums_[p][0]
            hsum[h, 1:2, at_(p)] += sums_[p][1]
        hook("attb", i)
        return carry

    lax.fori_loop(0, 2 * BLOCKS, attend_back, 0)
    for h in range(2):
        sums[0, h : h + 1, :] = hsum[h, 0:1, :]
        sums[0, 2 + h : 3 + h, :] = hsum[h, 1:2, :]
    adv_vec()
    chunk_loop("dwq", 9, 3, GT)
    chunk_loop("dw1b", 4 + FIRST_EXPAND, 4 - FIRST_EXPAND, FLT)
    transpose_into(FLT, lambda b: acc[rows_of(b), :].astype(BF))
    chunk_loop("dwo", 8, 1, FLT)

    def input_grad(b, carry):
        rows = block_rows(b)
        g = acc[rows, :]
        for h in range(2):
            gp = jnp.concatenate([A[9 + i, h, rows, :] for i in range(3)], axis=1)
            g = g + mm_nt(gp, wqkv[h])
        slot = lax.rem(b, 2)

        @pl.when(b >= 2)
        def _():
            pltpu.make_async_copy(stage.at[slot], gin_hbm.at[b - 2], osem.at[slot]).wait()

        stage[slot] = g.astype(BF)
        pltpu.make_async_copy(stage.at[slot], gin_hbm.at[b], osem.at[slot]).start()
        hook("gin", b)
        return carry

    lax.fori_loop(0, BLOCKS, input_grad, 0)
    hook("tail")
    for b in range(2):
        pltpu.make_async_copy(stage.at[b], gin_hbm.at[b + 2], osem.at[b]).wait()
    left = lambda: [j for j in range(len(PARTS)) if place[j] <= len(names_of(j))]
    while left():
        adv_vec()
        adv(*left())
    while vec_place[0] <= len(swaps):
        adv_vec()
    vec_out[...] = sums[len(swaps)]


def layer(n_dp, *operands):
    vm = pl.BlockSpec(memory_space=pltpu.VMEM)
    hbm = pl.BlockSpec(memory_space=pl.ANY)
    bits = n_dp.bit_length() - 1
    split = min(bits, 4)
    dma = pltpu.SemaphoreType.DMA
    return pl.pallas_call(
        functools.partial(kernel, bits),
        out_shape=(
            jax.ShapeDtypeStruct((BLOCKS, ROWS, WIDTH), BF),
            jax.ShapeDtypeStruct((BLOCKS, ROWS, WIDTH), BF),
            jax.ShapeDtypeStruct((CHUNKS, WIDTH, HALF), BF),
            jax.ShapeDtypeStruct((24, HALF), F32),
        ),
        in_specs=[hbm] * 19,
        out_specs=(hbm, hbm, hbm, vm),
        scratch_shapes=[
            pltpu.VMEM((BLOCKS, 2 * ROWS), jnp.int32),
            pltpu.VMEM((BLOCKS, 2 * ROWS), jnp.int32),
            pltpu.VMEM((HALF,), BF),
            pltpu.VMEM((HALF,), BF),
            pltpu.VMEM((HIDDEN,), BF),
            pltpu.VMEM((WIDTH,), BF),
            pltpu.VMEM((WIDTH,), BF),
            pltpu.VMEM((WIDTH,), BF),
            pltpu.VMEM((WIDTH,), BF),
            pltpu.VMEM((WIDTH,), BF),
            pltpu.VMEM((WIDTH,), BF),
            pltpu.VMEM((BLOCKS, ROWS, WIDTH), BF),
            pltpu.VMEM((2, WIDTH, 3 * HALF), BF),
            pltpu.VMEM((2, HALF, WIDTH), BF),
            pltpu.VMEM((2, WIDTH, HIDDEN), BF),
            pltpu.VMEM((2, HIDDEN, WIDTH), BF),
            pltpu.VMEM((2, 8, HIDDEN), F32),
            pltpu.VMEM((CHUNKS, 2, TOTAL, HALF), BF),
            pltpu.VMEM((2 * BLOCKS, 2, 3, WIN, 2 * WIN), BF),
            pltpu.VMEM((TOTAL, WIDTH), F32),
            pltpu.VMEM((TOTAL, 1), F32),
            pltpu.VMEM((TOTAL, WIDTH), F32),
            pltpu.VMEM((2, TOTAL, HALF), BF),
            pltpu.VMEM((WIDTH, TOTAL), BF),
            pltpu.VMEM((WIDTH, TOTAL), BF),
            pltpu.VMEM((2 * BLOCKS, WIN, WIN), F32),
            pltpu.VMEM((2, ROWS, WIDTH), BF),
            pltpu.VMEM((bits + 2, 24, HALF), F32),
            pltpu.VMEM((bits + 1, 24, HALF), F32),
            pltpu.VMEM((2, 8, HALF), F32),
            pltpu.VMEM((4, 2, WIDTH // 2, HALF), BF),
            pltpu.VMEM((CHUNKS - len(LATE), WIDTH // 2, HALF), BF),
            pltpu.VMEM((max(len(LATE), 1), 2, WIDTH // 4, HALF), BF),
            pltpu.VMEM((CHUNKS, WIDTH // 4, HALF), BF),
            pltpu.VMEM((CHUNKS, WIDTH // 8, HALF), BF),
            pltpu.VMEM((CHUNKS, WIDTH // 16, HALF), BF),
            pltpu.VMEM((max(bits - split, 1), CHUNKS, WIDTH >> split, HALF), BF),
            dma((11,)),
            dma((7,)),
            dma((2,)),
            dma((max(KEPT) + 1,)),
            dma((15,)),
            dma((4, 15)),
            dma((len(PARTS),)),
            dma((LANDED_COUNT,)),
            dma((bits + 1,)),
            dma((bits + 1,)),
            dma((2,)),
            dma((2,)),
            dma((max(bits - split, 1), len(PARTS) if bits > split else 1)),
        ],
        compiler_params=pltpu.CompilerParams(
            vmem_limit_bytes=67043328, collective_id=0, has_side_effects=True
        ),
    )(*operands)


def finish_kernel(
    grad_hbm, out_low, gin_low, vec_hbm, outg, ging, wqg, wkg, wvg, wog, w1g, w2g, qbg, vbg, obg, g1g, s1g, ebg, rbg, g2g, s2g,
    low, wide, turned, rows, full, vec, isem, osem, rsem, ssem, vsem,
):
    t = lax.axis_index("tensor")
    vec_copy = pltpu.make_async_copy(vec_hbm, vec, vsem.at[0])
    vec_copy.start()
    fetch = [pltpu.make_async_copy(grad_hbm.at[k], low.at[k], isem.at[k]) for k in range(CHUNKS)]
    order = [0, 1, 2, 3, 8] + list(range(4, 8)) + list(range(9, 12))
    pairs = [(i, b) for i in range(2) for b in range(BLOCKS)]
    refs = ((out_low, outg), (gin_low, ging))
    passed = [pltpu.make_async_copy(refs[i][0].at[b], rows.at[i, b], rsem.at[i, b]) for i, b in pairs]
    for cp in passed:
        cp.start()
    for k in order:
        fetch[k].start()

    sends = []
    for n, (i, b) in enumerate(pairs):
        passed[n].wait()
        full[i, b] = rows[i, b].astype(F32)
        cp = pltpu.make_async_copy(full.at[i, b], refs[i][1].at[b], ssem.at[i, b])
        cp.start()
        sends.append(cp)
    for k in order:
        fetch[k].wait()
        if k >= 9:
            wide[k - 5] = low[k].astype(F32)
            src, dst = wide.at[k - 5], (wqg, wkg, wvg)[k - 9]
        elif k >= 4 and k < 8:
            wide[k - 4] = low[k].astype(F32)
            src, dst = wide.at[k - 4], w1g.at[:, pl.ds((k - 4) * HALF, HALF)]
        elif k == 8:
            turned[4] = low[k].T.astype(F32)
            src, dst = turned.at[4], wog
        else:
            turned[k] = low[k].T.astype(F32)
            src, dst = turned.at[k], w2g.at[pl.ds(k * HALF, HALF), :]
        cp = pltpu.make_async_copy(src, dst, osem.at[k])
        cp.start()
        sends.append(cp)
    vec_copy.wait()

    def pick(r):
        return jnp.where(t == 0, vec[r : r + 1, :], vec[r + 1 : r + 2, :]).reshape(HALF)

    def whole(r):
        return jnp.concatenate([vec[r : r + 1, :], vec[r + 1 : r + 2, :]], axis=1).reshape(WIDTH)

    qbg[...] = pick(0)
    vbg[...] = pick(2)
    for ref, r in ((obg, 4), (g1g, 6), (s1g, 8), (rbg, 10), (g2g, 12), (s2g, 14)):
        ref[...] = whole(r)
    lines = [jnp.where(t == 0, vec[16 + k : 17 + k, :], vec[20 + k : 21 + k, :]) for k in range(4)]
    ebg[...] = jnp.concatenate(lines, axis=1).reshape(HIDDEN)

    for cp in sends:
        cp.wait()


def finish(out, gin, grads, vec):
    vm = pl.BlockSpec(memory_space=pltpu.VMEM)
    hbm = pl.BlockSpec(memory_space=pltpu.HBM)
    f = lambda *shape: jax.ShapeDtypeStruct(shape, F32)
    return pl.pallas_call(
        finish_kernel,
        out_shape=(f(BLOCKS, ROWS, WIDTH), f(BLOCKS, ROWS, WIDTH), f(WIDTH, HALF), f(WIDTH, HALF), f(WIDTH, HALF), f(HALF, WIDTH), f(WIDTH, HIDDEN), f(HIDDEN, WIDTH),
                   f(HALF), f(HALF), f(WIDTH), f(WIDTH), f(WIDTH), f(HIDDEN), f(WIDTH), f(WIDTH), f(WIDTH)),
        in_specs=[hbm, hbm, hbm, hbm],
        out_specs=(hbm,) * 8 + (vm,) * 9,
        scratch_shapes=[
            pltpu.VMEM((CHUNKS, WIDTH, HALF), BF),
            pltpu.VMEM((7, WIDTH, HALF), F32),
            pltpu.VMEM((5, HALF, WIDTH), F32),
            pltpu.VMEM((2, BLOCKS, ROWS, WIDTH), BF),
            pltpu.VMEM((2, BLOCKS, ROWS, WIDTH), F32),
            pltpu.VMEM((24, HALF), F32),
            pltpu.SemaphoreType.DMA((CHUNKS,)),
            pltpu.SemaphoreType.DMA((CHUNKS,)),
            pltpu.SemaphoreType.DMA((2, BLOCKS)),
            pltpu.SemaphoreType.DMA((2, BLOCKS)),
            pltpu.SemaphoreType.DMA((1,)),
        ],
        compiler_params=pltpu.CompilerParams(vmem_limit_bytes=67043328),
    )(grads, out, gin, vec)


def local(
    n_dp, inputs, segments, padding, query_weight, query_bias, key_weight, value_weight, value_bias,
    output_weight, output_bias, first_gain, first_shift, expand_weight, expand_bias,
    reduce_weight, reduce_bias, second_gain, second_shift, cotangent,
):
    out, gin, grads, vec = layer(
        n_dp, inputs, cotangent, segments, padding, query_bias, value_bias, expand_bias, output_bias, first_gain,
        first_shift, reduce_bias, second_gain, second_shift, query_weight, key_weight, value_weight,
        output_weight, expand_weight, reduce_weight,
    )
    out, gin, wq, wk, wv, wo, w1, w2, qb, vb, ob, g1, s1, eb, rb, g2, s2 = finish(out, gin, grads, vec)
    return (out, gin, wq, qb, wk, wv, vb, wo, ob, g1, s1, w1, eb, w2, rb, g2, s2)


def solution(mesh):
    tokens = P(None, ("dp", "tensor"), None)
    return jax.shard_map(
        functools.partial(local, mesh.shape["dp"]),
        mesh=mesh,
        in_specs=(
            tokens, P(None, "dp"), P(None, "dp"), P(None, "tensor"), P("tensor"), P(None, "tensor"),
            P(None, "tensor"), P("tensor"), P("tensor", None), P(), P(), P(), P(None, "tensor"),
            P("tensor"), P("tensor", None), P(), P(), P(), tokens,
        ),
        out_specs=(
            tokens, tokens, P(None, "tensor"), P("tensor"), P(None, "tensor"), P(None, "tensor"),
            P("tensor"), P("tensor", None), P(), P(), P(), P(None, "tensor"), P("tensor"),
            P("tensor", None), P(), P(), P(),
        ),
        check_vma=False,
    )
```

```python
import functools

import jax
import jax.numpy as jnp
from jax import lax
from jax.experimental import pallas as pl
from jax.experimental.pallas import tpu as pltpu
from jax.sharding import PartitionSpec as P

WIN = 128
BLOCKS = 4
ROWS = 256
TOTAL = BLOCKS * ROWS
WIDTH = 768
HALF = 384
HIDDEN = 1536
CHUNKS = 12
EPS = 1e-12
BF = jnp.bfloat16
F32 = jnp.float32
MESH = pl.DeviceIdType.MESH


def mm(a, b):
    return lax.dot_general(a, b, (((1,), (0,)), ((), ())), preferred_element_type=F32)


def mm_nt(a, b):
    return lax.dot_general(a, b, (((1,), (1,)), ((), ())), preferred_element_type=F32)


def mm_tn(a, b):
    return lax.dot_general(a, b, (((0,), (0,)), ((), ())), preferred_element_type=F32)


def row_mean(a):
    return jnp.sum(a, axis=-1, keepdims=True) * (1.0 / WIDTH)


def col_sum(a):
    return jnp.sum(a, axis=0, keepdims=True)

WAYS = ((2, 1, 0), (2, 1, 0), (2, 1, 0), (2, 1, 0), (1, 2, 0), (1, 2, 0), (2, 1, 0), (2, 0), (2, 0), (2, 1, 0), (2, 1, 0), (2, 1, 0), (2, 1, 0), (0,), (2, 0))
FIRST = (1, 4, 0, 3, 5, 2, 6, 11, 10, 12, 9, 7, 14, 8, 13)
PARTS = ((0, 0, 384), (1, 0, 384), (2, 0, 384), (3, 0, 384), (4, 0, 384), (5, 0, 384), (6, 0, 384), (7, 0, 384), (8, 0, 128), (8, 128, 128), (8, 256, 128), (9, 0, 384), (10, 0, 384), (11, 0, 128), (11, 128, 128), (11, 256, 128))
ORDERS = ((0, 1, 2, 3), (0, 1, 2, 3), (0, 1, 2, 3), (0, 1, 2, 3), (0, 1, 2, 3), (0, 1, 2, 3), (0, 1, 2, 3), (0, 1, 2, 3), (0, 1, 2, 3), (0, 1, 2, 3), (0, 1, 2, 3), (0, 1, 2, 3), (0, 1, 2, 3), (0, 1, 2, 3), (0, 1, 2, 3), (0, 1, 2, 3))
LATE = (1, 3, 4, 6)
SEQUENCE = (0, 1, 2, 3, 4, 5, 6, 7, 9, 10, 11, 8)
FIRST_EXPAND = 4
PLAN = {
    "attend": ((1, (1,)), (2, (4,)), (3, (0, 1, 3, 5, 4, 2, 0, 6, 3, 1, 5, 11, 1, 4, 2, 0, 10, 4, 0, 6, 3, 12, 3, 5, 2, 9, 5, 11, 2)), (5, (6, 7, 10)), (6, (6, 12)), (7, (9, 11, 14)),),
    "norm1": ((0, (11,)), (1, (7, 8, 10)),),
    "own": ((0, (7, 10, 12, 14)), (1, (8, 9, 12, 13, 14)),),
    "pre_other": ((0, (8, 9, 13)),),
    "dw2": ((0, (20,)), (1, (21,)), (2, (20, 22)), (3, (21, 23)),),
    "back": ((0, (22, 23)), (1, (20, 21)), (3, (21, 22, 23)),),
    "dw1": ((0, (24, 20)), (1, (25,)), (2, (24, 26, 21)), (3, (25, 27, 20, 22, 23)),),
    "attb": ((0, (26,)), (1, (27,)), (2, (21,)), (3, (20, 22)), (5, (23, 24)), (7, (21, 25)),),
    "dwq": ((0, (31, 20)), (1, (32,)), (2, (31, 33, 34, 35, 22, 26, 21, 32, 23)),),
    "dwo": ((0, (33, 34, 35, 28, 29, 30, 20, 25, 27)),),
    "gin": ((0, (28, 29, 30, 22, 24, 40)), (1, (21, 23, 25, 40)), (3, (21, 22)),),
    "tail": ((0, (20, 24, 20, 23, 31, 27, 40, 25, 26, 24, 27, 22, 40, 22, 25, 26, 23, 32, 23, 24, 31, 27, 33, 40, 25, 34, 32, 26, 33, 24, 35, 31, 28, 25, 27, 32, 34, 29, 25, 33, 26, 30, 24, 31, 27, 35, 24, 28, 34, 32, 29, 33, 30, 26, 35, 28, 31, 27, 34, 29, 27, 32, 30, 33, 35, 26, 28, 31, 26, 34, 29, 32, 33, 30, 35, 34, 31, 28, 29, 31, 30, 35, 28, 32, 29, 30, 33, 32, 34, 33, 35, 34, 28, 35, 29, 28, 30, 29, 30)),),
}
LANDED = {
    "c": (0, 1, 2, 3, 0, 1, 2, 3, 0, 5, 6, 0, 1, 2, 3, 4),
    "g0": (8, 7, 7, 8, 8, 7, 8, 7, 8, 9, 7, 7, 8, 9, 7, 10),
    "g1": (12, 11, 13, 14, 12, 11, 14, 13, 14, 17, 18, 11, 12, 15, 16, 13),
    "g2": (20, 19, 21, 22, 20, 19, 22, 21, 19, 24, 25, 19, 20, 23, 21, 22),
    "g3": (27, 26, 28, 29, 27, 26, 29, 28, 31, 26, 32, 26, 27, 30, 28, 29),
    "r1": (35, 33, 36, 34, 37, 34, 33, 35, 36, 38, 39, 36, 33, 34, 37, 35),
    "r2": (41, 40, 42, 43, 41, 40, 43, 42, 45, 40, 41, 40, 41, 44, 42, 43),
    "r3": (47, 46, 48, 49, 47, 46, 49, 48, 51, 46, 52, 46, 47, 50, 48, 49),
    "y": (53, 55, 54, 53, 55, 56, 58, 54, 53, 63, 64, 57, 59, 60, 61, 62),
}
LANDED_COUNT = 65
KEPT = (1, 0, 0, 1, 1, 0, 1, 0, 2, 0, 3, 0, 1, 2, 0, 1)


def kernel(
    bits,
    x_hbm, cot_hbm, seg_hbm, pad_hbm, qb_hbm, vb_hbm, eb_hbm, ob_hbm, g1_hbm, s1_hbm, rb_hbm, g2_hbm, s2_hbm,
    wq_hbm, wk_hbm, wv_hbm, wo_hbm, w1_hbm, w2_hbm,
    out_hbm, gin_hbm, grad_hbm, vec_out,
    seg_ref, pad_ref, qb_ref, vb_ref, eb_ref, ob_ref, g1_ref, s1_ref, rb_ref, g2_ref, s2_ref,
    x_ref, wqkv, wo, w1, w2, hv, A, probs, normed, spread, acc, FL, FLT, GT, bias, stage, sums, got, hsum,
    R0, R1, RB, R2, R3, R4, RX,
    isem, lsem, osem, fsem, wsend, wrecv, gsend, grecv, vsend, vrecv, bsem, psem, xrecv,
):
    t = lax.axis_index("tensor")
    me = lax.axis_index("dp")
    bit = [lax.rem(me // (1 << i), 2) for i in range(bits)]
    split = min(bits, 4)

    def mate(i):
        return (me + (1 << i) * (1 - 2 * bit[i]), t)

    across = (me, 1 - t)
    partners = [across] + [mate(i) for i in range(bits)]

    barrier = pltpu.get_barrier_semaphore()
    for who in partners:
        pl.semaphore_signal(barrier, inc=1, device_id=who, device_id_type=MESH)

    smalls = [
        (seg_hbm, seg_ref),
        (pad_hbm, pad_ref),
        (qb_hbm, qb_ref),
        (vb_hbm, vb_ref),
        (eb_hbm, eb_ref),
        (ob_hbm, ob_ref),
        (g1_hbm, g1_ref),
        (s1_hbm, s1_ref),
        (rb_hbm, rb_ref),
        (g2_hbm, g2_ref),
        (s2_hbm, s2_ref),
    ]
    smalls = [pltpu.make_async_copy(s, d, isem.at[i]) for i, (s, d) in enumerate(smalls)]
    for cp in smalls:
        cp.start()

    locals_ = [
        (x_hbm, x_ref),
        (wq_hbm, wqkv.at[t, :, pl.ds(0, HALF)]),
        (wk_hbm, wqkv.at[t, :, pl.ds(HALF, HALF)]),
        (wv_hbm, wqkv.at[t, :, pl.ds(2 * HALF, HALF)]),
        (wo_hbm, wo.at[t]),
        (w1_hbm, w1.at[t]),
        (w2_hbm, w2.at[t]),
    ]
    loads = [pltpu.make_async_copy(s, d, lsem.at[i]) for i, (s, d) in enumerate(locals_)]
    for cp in loads:
        cp.start()

    for cp in smalls:
        cp.wait()

    def row(ref):
        return ref[...].astype(F32).reshape(1, ref.shape[0])

    hv[t] = jnp.zeros((8, HIDDEN), F32)
    hv[t, 0:1, :] = row(eb_ref)
    hv[t, 1:2, 0:HALF] = row(qb_ref)
    hv[t, 1:2, HALF : 2 * HALF] = row(vb_ref)
    out_b, gain1, shift1 = row(ob_ref), row(g1_ref), row(s1_ref)
    red_b, gain2, shift2 = row(rb_ref), row(g2_ref), row(s2_ref)
    sums[0] = jnp.zeros((24, HALF), F32)
    hsum[...] = jnp.zeros_like(hsum)
    lane = lax.broadcasted_iota(jnp.int32, (1, 128), 1)
    low = lane < 64
    mask0 = jnp.where(low, 1.0, 0.0).astype(BF)
    mask1 = jnp.where(low, 0.0, 1.0).astype(BF)
    sc0 = jnp.where(low, 0.125, 0.0).astype(BF)
    sc1 = jnp.where(low, 0.0, 0.125).astype(BF)

    for b in range(BLOCKS):
        for wi in range(2):
            cols = pl.ds(pl.multiple_of(t * ROWS + wi * WIN, WIN), WIN)
            seg = jnp.broadcast_to(seg_ref[b : b + 1, cols].astype(F32), (WIN, WIN))
            live = jnp.broadcast_to(pad_ref[b : b + 1, cols].astype(F32), (WIN, WIN))
            bias[2 * b + wi] = jnp.where((seg == seg.T) & (live.T > 0.5), 0.0, -1e30)

    pl.semaphore_wait(barrier, len(partners))

    def part_rows(base, n, ways, fixed):
        size = n // (1 << len(ways))
        at_ = sum((bit[w] * (size << j) for j, w in enumerate(ways)), 0)
        free = len(ways) - fixed
        at_ = sum((bit[w] * (size << j) for j, w in enumerate(ways) if j >= free), 0)
        return pl.ds(pl.multiple_of(base + at_, 16), size << free)

    def cols(i):
        return pl.ds(i * HALF, HALF)

    every = pl.ds(0, WIDTH)
    pieces = [
        (src, pl.ds(0, HALF), wqkv, cols(i), base, HALF)
        for i, src in enumerate((wq_hbm, wk_hbm, wv_hbm))
        for base in (0, HALF)
    ]
    pieces += [(wo_hbm, every, wo, every, 0, HALF)]
    pieces += [(w1_hbm, cols(i), w1, cols(i), 0, WIDTH) for i in range(4)]
    pieces += [(w2_hbm, every, w2, every, i * HALF, HALF) for i in range(4)]

    def weight_copy(g, s):
        hbm, hc, dst, dc, base, n = pieces[g]
        ways = WAYS[g]
        r = part_rows(base, n, ways, len(ways) - max(s - 1, 0))
        if s == 0:
            src, to, who = hbm.at[r, hc], dst.at[t, r, dc], across
        else:
            src = to = dst.at[1 - t, r, dc]
            who = mate(ways[s - 1])
        return pltpu.make_async_remote_copy(
            src_ref=src, dst_ref=to, send_sem=wsend.at[g], recv_sem=wrecv.at[s, g],
            device_id=who, device_id_type=MESH,
        )

    wplace = [0] * len(pieces)

    def adv_weight(g):
        s, last = wplace[g], len(WAYS[g])
        if s > 0:
            weight_copy(g, s - 1).wait()
        if s <= last:
            weight_copy(g, s).start()
        wplace[g] = s + 1

    def weights_ready(which):
        while min(wplace[g] - len(WAYS[g]) for g in which) < 2:
            for g in which:
                if wplace[g] < len(WAYS[g]) + 2:
                    adv_weight(g)

    bias_copy = pltpu.make_async_remote_copy(
        src_ref=hv.at[t], dst_ref=hv.at[t], send_sem=bsem.at[0], recv_sem=bsem.at[1],
        device_id=across, device_id_type=MESH,
    )
    for g in FIRST[:6]:
        adv_weight(g)
    bias_copy.start()
    for g in FIRST[6:]:
        adv_weight(g)

    def run(ops):
        for op in ops:
            if op < 20:
                adv_weight(op)
            elif op < 40:
                adv(op - 20)
            else:
                adv_vec()

    def at(loop_index, step, action):
        @pl.when(loop_index == step)
        def _():
            action()

    def hook(name, loop_index=None):
        for step, ops in PLAN.get(name, ()):
            if loop_index is None:
                run(ops)
            else:
                at(loop_index, step, lambda ops=ops: run(ops))

    def stacked(a, m0, m1):
        return jnp.concatenate([a * m0, a * m1], axis=0)

    def block_rows(b):
        return pl.ds(pl.multiple_of(b * ROWS, ROWS), ROWS)

    for cp in loads[:4]:
        cp.wait()

    def attend(i, carry):
        b = lax.rem(i, BLOCKS)
        h = t + (i // BLOCKS) * (1 - 2 * t)
        rows = block_rows(b)
        pr = mm(x_ref[b], wqkv[h])
        q = (pr[:, :HALF] + hv[h, 1:2, 0:HALF]).astype(BF)
        k = pr[:, HALF : 2 * HALF].astype(BF)
        v = (pr[:, 2 * HALF :] + hv[h, 1:2, HALF : 2 * HALF]).astype(BF)
        A[9, h, rows, :] = q
        A[10, h, rows, :] = k
        A[11, h, rows, :] = v
        units = [(wi, p) for wi in range(2) for p in range(3)]
        for g in range(0, 6, 6):
            part = units[g : g + 6]
            scores = []
            for wi, p in part:
                r, c = slice(wi * WIN, (wi + 1) * WIN), slice(p * 128, (p + 1) * 128)
                bb = bias[b * 2 + wi]
                scores.append(mm_nt(k[r, c], stacked(q[r, c], sc0, sc1)) + jnp.concatenate([bb, bb], axis=1))
            expo = [jnp.exp(s - jnp.max(s, axis=0, keepdims=True)) for s in scores]
            pbs = [(e * (1.0 / jnp.sum(e, axis=0, keepdims=True))).astype(BF) for e in expo]
            for (wi, p), pb in zip(part, pbs):
                r, c = slice(wi * WIN, (wi + 1) * WIN), slice(p * 128, (p + 1) * 128)
                probs[b * 2 + wi, h, p] = pb
                o = mm_tn(pb, v[r, c])
                o = jnp.where(low, o[:WIN], o[WIN:])
                A[8, h, pl.ds(pl.multiple_of(b * ROWS + wi * WIN, WIN), WIN), c] = o.astype(BF)

        hook("attend", i)
        at(i, 3, own_done)
        return carry

    def own_done():
        weights_ready(range(6))
        bias_copy.wait()

    lax.fori_loop(0, 2 * BLOCKS, attend, 0)

    def joined(k, rows):
        return jnp.concatenate([A[k, 0, rows, :], A[k, 1, rows, :]], axis=1)

    def normalize(hidden):
        center = hidden - row_mean(hidden)
        rs = lax.rsqrt(row_mean(center * center) + EPS)
        return center * rs, rs

    def add_vec(row, value):
        sums[0, row : row + 1, :] += value[:, :HALF]
        sums[0, row + 1 : row + 2, :] += value[:, HALF:]


    loads[4].wait()
    hook("pre_norm")
    weights_ready([6])

    def first_norm(i, carry):
        hidden = []
        for n in range(2):
            b = 2 * i + n
            mixed = joined(8, block_rows(b))
            hidden.append(x_ref[b].astype(F32) + mm(mixed[:, :HALF], wo[0]) + mm(mixed[:, HALF:], wo[1]) + out_b)
        for n in range(2):
            rows = block_rows(2 * i + n)
            value, rs = normalize(hidden[n])
            normed[rows, :] = value
            spread[rows, :] = rs
            first = value * gain1 + shift1
            FL[0, rows, :] = first[:, :HALF].astype(BF)
            FL[1, rows, :] = first[:, HALF:].astype(BF)
        hook("norm1", i)
        return carry

    lax.fori_loop(0, BLOCKS // 2, first_norm, 0)
    loads[5].wait()
    loads[6].wait()

    def low_rows(rows):
        return jnp.concatenate([FL[0, rows, :], FL[1, rows, :]], axis=1)

    def half_inner(b, h):
        return mm(low_rows(block_rows(b)), w1[h]) + hv[h, 0:1, :]

    def half_feed(b, h):
        return half_rest(b, h, half_inner(b, h))

    def half_rest(b, h, inner_all):
        rows = block_rows(b)
        acts = []
        for k in range(4):
            inner = inner_all[:, k * HALF : (k + 1) * HALF]
            phi = 0.5 + 0.5 * lax.erf(inner * 0.7071067811865476)
            slope = phi + inner * jnp.exp(-0.5 * inner * inner) * 0.3989422804014327
            act = (inner * phi).astype(BF)
            A[k, h, rows, :] = act
            A[4 + k, h, rows, :] = slope.astype(BF)
            acts.append(act)
        return mm(jnp.concatenate(acts, axis=1), w2[h])

    def cot_copy(b, slot):
        return pltpu.make_async_copy(cot_hbm.at[b], GT.at[pl.ds(slot * ROWS, ROWS), pl.ds(0, WIDTH)], psem.at[slot])

    cot_copy(0, 0).start()
    cot_copy(1, 1).start()

    def feed_own(i, carry):
        both = [half_inner(2 * i + n, t) for n in range(2)]
        for n in range(2):
            acc[block_rows(2 * i + n), :] = half_rest(2 * i + n, t, both[n])
        hook("own", i)
        return carry

    lax.fori_loop(0, BLOCKS // 2, feed_own, 0)
    hook("pre_other")
    weights_ready(range(7, 15))

    def second_norm(i, carry):
        inners = [half_inner(2 * i + n, 1 - t) for n in range(2)]
        reds = [acc[block_rows(2 * i + n), :] + half_rest(2 * i + n, 1 - t, inners[n]) for n in range(2)]
        for n in range(2):
            b = 2 * i + n
            rows = block_rows(b)
            value, rs = normalize(normed[rows, :] * gain1 + shift1 + reds[n] + red_b)

            @pl.when(i >= 1)
            def _(b=b, n=n):
                pltpu.make_async_copy(stage.at[n], out_hbm.at[b - 2], osem.at[n]).wait()

            stage[n] = (value * gain2 + shift2).astype(BF)
            pltpu.make_async_copy(stage.at[n], out_hbm.at[b], osem.at[n]).start()
            cot_copy(b, n).wait()
            c = GT[n * ROWS : (n + 1) * ROWS, 0:WIDTH].astype(F32)

            @pl.when(i + 1 < BLOCKS // 2)
            def _(b=b, n=n):
                cot_copy(b + 2, n).start()

            add_vec(14, col_sum(c))
            add_vec(12, col_sum(c * value))
            u = c * gain2
            gs = rs * (u - row_mean(u) - value * row_mean(u * value))
            add_vec(10, col_sum(gs))
            acc[rows, :] = gs
        return carry

    lax.fori_loop(0, BLOCKS // 2, second_norm, 0)
    for b in range(2):
        pltpu.make_async_copy(stage.at[b], out_hbm.at[b + 2], osem.at[b]).wait()

    def span(i):
        return WIDTH >> (i + 1)

    def lo(j, i):
        return sum((bit[ORDERS[j][n]] * span(n) for n in range(i + 1)), 0)

    def ds(at_, n):
        return pl.ds(pl.multiple_of(at_, 16), n)

    def held(j, h, r):
        k, first, width = PARTS[j]
        if k < 9:
            return A, (k, h, r, pl.ds(first, width))
        return w1, (h, r, pl.ds((k - 9) * HALF + first, width))

    def add_in(j, h, r, value):
        ref, at_ = held(j, h, r)
        ref[at_] = ref[at_] + value

    def view(j, h, r):
        ref, at_ = held(j, h, r)
        return ref.at[at_]

    def landing(j, p):
        k, first, width = PARTS[j]
        c = pl.ds(first, width)
        if p == 0:
            return R0, (SEQUENCE.index(k) % 4, slice(None), slice(None), c)
        if p == 1 and k in LATE:
            return RB, (LATE.index(k), slice(None), slice(None), c)
        if p == 1:
            return R1, (k - sum(n < k for n in LATE), slice(None), c)
        return (R2, R3, R4)[p - 2], (k, slice(None), c)

    halves = [("half", i) for i in range(1, split)]
    swaps_ = [("swap", i) for i in range(bits - split)]
    gathers = [("gather", i) for i in reversed(range(1, split))]

    def names_of(j):
        mid = halves + swaps_ + gathers
        if PARTS[j][0] in LATE:
            return [("core", 0), ("both", 1), ("tensor", 1)] + mid[1:] + [("gather", 0)]
        return [("core", 0), ("tensor", 0)] + mid + [("gather", 0)]

    def begin(j, s):
        piece_copy(j, s).start()

    def piece_copy(j, s):
        kind, i = names_of(j)[s]
        way = ORDERS[j]
        k, first, width = PARTS[j]
        if kind == "core":
            src, who = view(j, slice(None), ds((1 - bit[way[0]]) * span(0), span(0))), mate(way[0])
            land, at_ = landing(j, 0)
            dst = land.at[at_]
        elif kind == "tensor":
            src, who = view(j, 1 - t, ds(lo(j, i), span(i))), across
            land, at_ = landing(j, i + 1)
            dst = land.at[at_]
        elif kind == "both":
            src, who = view(j, slice(None), ds(lo(j, 0) + (1 - bit[way[1]]) * span(1), span(1))), mate(way[1])
            land, at_ = landing(j, 1)
            dst = land.at[at_]
        elif kind == "half":
            src = view(j, t, ds(lo(j, i - 1) + (1 - bit[way[i]]) * span(i), span(i)))
            who = mate(way[i])
            land, at_ = landing(j, i + 1)
            dst = land.at[at_]
        elif kind == "swap":
            src, who = view(j, t, ds(lo(j, split - 1), span(split - 1))), mate(split + i)
            dst = RX.at[i, k, :, pl.ds(first, width)]
        else:
            r = ds(lo(j, i), span(i))
            dst, who = grad_hbm.at[k, r, pl.ds(first, width)], mate(way[i])
            src = view(j, t, r) if i == split - 1 and i > 0 else dst
        if kind == "swap":
            landed = xrecv.at[i, j]
        else:
            key = {"core": "c", "tensor": "y", "gather": "g"}.get(kind, "r")
            landed = grecv.at[LANDED[key if kind in ("core", "tensor") else f"{key}{way[i]}"][j]]
        return pltpu.make_async_remote_copy(
            src_ref=src, dst_ref=dst, send_sem=gsend.at[j], recv_sem=landed, device_id=who, device_id_type=MESH
        )

    def keep_copy(j):
        k, first, width = PARTS[j]
        r = ds(lo(j, split - 1), span(split - 1))
        return pltpu.make_async_copy(view(j, t, r), grad_hbm.at[k, r, pl.ds(first, width)], fsem.at[KEPT[j]])

    def settle(j, s):
        names = names_of(j)
        kind, i = names[s]
        k, first, width = PARTS[j]
        piece_copy(j, s).wait()
        if kind == "core":
            land, at_ = landing(j, 0)
            add_in(j, slice(None), ds(lo(j, 0), span(0)), land[at_])
        elif kind == "tensor":
            land, at_ = landing(j, i + 1)
            add_in(j, t, ds(lo(j, i), span(i)), land[at_])
        elif kind == "both":
            land, at_ = landing(j, 1)
            add_in(j, slice(None), ds(lo(j, 1), span(1)), land[at_])
        elif kind == "half":
            land, at_ = landing(j, i + 1)
            add_in(j, t, ds(lo(j, i), span(i)), land[at_])
        elif kind == "swap":
            add_in(j, t, ds(lo(j, split - 1), span(split - 1)), RX[i, k, :, pl.ds(first, width)])
        elif i == split - 1:
            keep_copy(j).wait()
        if s + 1 < len(names) and names[s + 1] == ("gather", split - 1):
            keep_copy(j).start()

    place = [0] * len(PARTS)

    def adv(*which):
        for k in which:
            s = place[k]
            names = names_of(k)
            if s > len(names):
                continue
            if s > 0:
                settle(k, s - 1)
            if s < len(names):
                begin(k, s)
            place[k] = s + 1

    swaps = [across] + [mate(i) for i in range(bits)]
    vec_place = [0]

    def adv_vec():
        s = vec_place[0]

        def cp(j):
            return pltpu.make_async_remote_copy(
                src_ref=sums.at[j], dst_ref=got.at[j], send_sem=vsend.at[j], recv_sem=vrecv.at[j],
                device_id=swaps[j], device_id_type=MESH,
            )

        if s > len(swaps):
            return
        if s > 0:
            cp(s - 1).wait()
            sums[s] = sums[s - 1] + got[s - 1]
        if s < len(swaps):
            cp(s).start()
        vec_place[0] = s + 1

    def transpose_into(dst, get):
        for b in range(BLOCKS):
            dst[:, b * ROWS : (b + 1) * ROWS] = get(b).T

    def rows_of(b):
        return slice(b * ROWS, (b + 1) * ROWS)

    def chunk_loop(name, first, count, left):
        def one(j, carry):
            k = first + j
            full = mm(left[...], joined(k, slice(None)))
            for h in range(2):
                part = full[:, h * HALF : (h + 1) * HALF].astype(BF)
                if first < 9:
                    A[k, h, 0:WIDTH, :] = part
                else:
                    w1[h, :, pl.ds(pl.multiple_of(j * HALF, HALF), HALF)] = part
            hook(name, j)
            return carry

        if count:
            lax.fori_loop(0, count, one, 0)

    transpose_into(GT, lambda b: acc[rows_of(b), :].astype(BF))
    chunk_loop("dw2", 0, 4, GT)
    transpose_into(FLT, lambda b: low_rows(rows_of(b)))
    hook("mid")

    def feed_back(b, carry):
        rows = block_rows(b)
        gs = acc[rows, :]
        gl = gs.astype(BF)
        gf = gs
        for h in range(2):
            da = mm_nt(gl, w2[h])
            gis = []
            for k in range(4):
                gi = (da[:, k * HALF : (k + 1) * HALF] * A[4 + k, h, rows, :].astype(F32)).astype(BF)
                A[4 + k, h, rows, :] = gi
                sums[0, 16 + 4 * h + k : 17 + 4 * h + k, :] += col_sum(gi.astype(F32))
                gis.append(gi)
            gf = gf + mm_nt(jnp.concatenate(gis, axis=1), w1[h])
        n = normed[rows, :]
        add_vec(6, col_sum(gf * n))
        add_vec(8, col_sum(gf))
        u = gf * gain1
        gh = spread[rows, :] * (u - row_mean(u) - n * row_mean(u * n))
        add_vec(4, col_sum(gh))
        acc[rows, :] = gh
        gm = gh.astype(BF)
        FL[0, rows, :] = mm_nt(gm, wo[0]).astype(BF)
        FL[1, rows, :] = mm_nt(gm, wo[1]).astype(BF)
        hook("back", b)
        return carry

    lax.fori_loop(0, BLOCKS, feed_back, 0)
    transpose_into(GT, lambda b: x_ref[b])
    chunk_loop("dw1", 4, FIRST_EXPAND, FLT)

    def attend_back(i, carry):
        h, b = i // BLOCKS, lax.rem(i, BLOCKS)

        def rows_at(wi):
            return pl.ds(pl.multiple_of(b * ROWS + wi * WIN, WIN), WIN)

        def at_(p):
            return slice(p * 128, (p + 1) * 128)

        sums_ = {}
        units = [(wi, p) for p in range(3) for wi in range(2)]
        for g in range(0, 6, 6):
            part = units[g : g + 6]
            do2 = [stacked(FL[h, rows_at(wi), at_(p)], mask0, mask1) for wi, p in part]
            dp = [mm_nt(A[11, h, rows_at(wi), at_(p)], d) for (wi, p), d in zip(part, do2)]
            dv = [mm(probs[b * 2 + wi, h, p], d).astype(BF) for (wi, p), d in zip(part, do2)]
            pf = [probs[b * 2 + wi, h, p].astype(F32) for wi, p in part]
            dsc = [(f * (d - jnp.sum(f * d, axis=0, keepdims=True))).astype(BF) for f, d in zip(pf, dp)]
            dk = [mm(d, stacked(A[9, h, rows_at(wi), at_(p)], sc0, sc1)).astype(BF) for (wi, p), d in zip(part, dsc)]
            dq = [mm_tn(d, A[10, h, rows_at(wi), at_(p)]) for (wi, p), d in zip(part, dsc)]
            for (wi, p), q_, k_, v_ in zip(part, dq, dk, dv):
                q_ = (jnp.where(low, q_[:WIN], q_[WIN:]) * 0.125).astype(BF)
                A[9, h, rows_at(wi), at_(p)] = q_
                A[10, h, rows_at(wi), at_(p)] = k_
                A[11, h, rows_at(wi), at_(p)] = v_
                add = col_sum(q_.astype(F32)), col_sum(v_.astype(F32))
                sums_[p] = add if p not in sums_ else (sums_[p][0] + add[0], sums_[p][1] + add[1])
        for p in range(3):
            hsum[h, 0:1, at_(p)] += sums_[p][0]
            hsum[h, 1:2, at_(p)] += sums_[p][1]
        hook("attb", i)
        return carry

    lax.fori_loop(0, 2 * BLOCKS, attend_back, 0)
    for h in range(2):
        sums[0, h : h + 1, :] = hsum[h, 0:1, :]
        sums[0, 2 + h : 3 + h, :] = hsum[h, 1:2, :]
    adv_vec()
    chunk_loop("dwq", 9, 3, GT)
    chunk_loop("dw1b", 4 + FIRST_EXPAND, 4 - FIRST_EXPAND, FLT)
    transpose_into(FLT, lambda b: acc[rows_of(b), :].astype(BF))
    chunk_loop("dwo", 8, 1, FLT)

    def input_grad(b, carry):
        rows = block_rows(b)
        g = acc[rows, :]
        for h in range(2):
            gp = jnp.concatenate([A[9 + i, h, rows, :] for i in range(3)], axis=1)
            g = g + mm_nt(gp, wqkv[h])
        slot = lax.rem(b, 2)

        @pl.when(b >= 2)
        def _():
            pltpu.make_async_copy(stage.at[slot], gin_hbm.at[b - 2], osem.at[slot]).wait()

        stage[slot] = g.astype(BF)
        pltpu.make_async_copy(stage.at[slot], gin_hbm.at[b], osem.at[slot]).start()
        hook("gin", b)
        return carry

    lax.fori_loop(0, BLOCKS, input_grad, 0)
    hook("tail")
    for b in range(2):
        pltpu.make_async_copy(stage.at[b], gin_hbm.at[b + 2], osem.at[b]).wait()
    left = lambda: [j for j in range(len(PARTS)) if place[j] <= len(names_of(j))]
    while left():
        adv_vec()
        adv(*left())
    while vec_place[0] <= len(swaps):
        adv_vec()
    vec_out[...] = sums[len(swaps)]


def layer(n_dp, *operands):
    vm = pl.BlockSpec(memory_space=pltpu.VMEM)
    hbm = pl.BlockSpec(memory_space=pl.ANY)
    bits = n_dp.bit_length() - 1
    split = min(bits, 4)
    dma = pltpu.SemaphoreType.DMA
    return pl.pallas_call(
        functools.partial(kernel, bits),
        out_shape=(
            jax.ShapeDtypeStruct((BLOCKS, ROWS, WIDTH), BF),
            jax.ShapeDtypeStruct((BLOCKS, ROWS, WIDTH), BF),
            jax.ShapeDtypeStruct((CHUNKS, WIDTH, HALF), BF),
            jax.ShapeDtypeStruct((24, HALF), F32),
        ),
        in_specs=[hbm] * 19,
        out_specs=(hbm, hbm, hbm, vm),
        scratch_shapes=[
            pltpu.VMEM((BLOCKS, 2 * ROWS), jnp.int32),
            pltpu.VMEM((BLOCKS, 2 * ROWS), jnp.int32),
            pltpu.VMEM((HALF,), BF),
            pltpu.VMEM((HALF,), BF),
            pltpu.VMEM((HIDDEN,), BF),
            pltpu.VMEM((WIDTH,), BF),
            pltpu.VMEM((WIDTH,), BF),
            pltpu.VMEM((WIDTH,), BF),
            pltpu.VMEM((WIDTH,), BF),
            pltpu.VMEM((WIDTH,), BF),
            pltpu.VMEM((WIDTH,), BF),
            pltpu.VMEM((BLOCKS, ROWS, WIDTH), BF),
            pltpu.VMEM((2, WIDTH, 3 * HALF), BF),
            pltpu.VMEM((2, HALF, WIDTH), BF),
            pltpu.VMEM((2, WIDTH, HIDDEN), BF),
            pltpu.VMEM((2, HIDDEN, WIDTH), BF),
            pltpu.VMEM((2, 8, HIDDEN), F32),
            pltpu.VMEM((CHUNKS, 2, TOTAL, HALF), BF),
            pltpu.VMEM((2 * BLOCKS, 2, 3, WIN, 2 * WIN), BF),
            pltpu.VMEM((TOTAL, WIDTH), F32),
            pltpu.VMEM((TOTAL, 1), F32),
            pltpu.VMEM((TOTAL, WIDTH), F32),
            pltpu.VMEM((2, TOTAL, HALF), BF),
            pltpu.VMEM((WIDTH, TOTAL), BF),
            pltpu.VMEM((WIDTH, TOTAL), BF),
            pltpu.VMEM((2 * BLOCKS, WIN, WIN), F32),
            pltpu.VMEM((2, ROWS, WIDTH), BF),
            pltpu.VMEM((bits + 2, 24, HALF), F32),
            pltpu.VMEM((bits + 1, 24, HALF), F32),
            pltpu.VMEM((2, 8, HALF), F32),
            pltpu.VMEM((4, 2, WIDTH // 2, HALF), BF),
            pltpu.VMEM((CHUNKS - len(LATE), WIDTH // 2, HALF), BF),
            pltpu.VMEM((max(len(LATE), 1), 2, WIDTH // 4, HALF), BF),
            pltpu.VMEM((CHUNKS, WIDTH // 4, HALF), BF),
            pltpu.VMEM((CHUNKS, WIDTH // 8, HALF), BF),
            pltpu.VMEM((CHUNKS, WIDTH // 16, HALF), BF),
            pltpu.VMEM((max(bits - split, 1), CHUNKS, WIDTH >> split, HALF), BF),
            dma((11,)),
            dma((7,)),
            dma((2,)),
            dma((max(KEPT) + 1,)),
            dma((15,)),
            dma((4, 15)),
            dma((len(PARTS),)),
            dma((LANDED_COUNT,)),
            dma((bits + 1,)),
            dma((bits + 1,)),
            dma((2,)),
            dma((2,)),
            dma((max(bits - split, 1), len(PARTS) if bits > split else 1)),
        ],
        compiler_params=pltpu.CompilerParams(
            vmem_limit_bytes=67043328, collective_id=0, has_side_effects=True
        ),
    )(*operands)


def finish_kernel(
    grad_hbm, out_low, gin_low, vec_hbm, outg, ging, wqg, wkg, wvg, wog, w1g, w2g, qbg, vbg, obg, g1g, s1g, ebg, rbg, g2g, s2g,
    low, wide, turned, rows, full, vec, isem, osem, rsem, ssem, vsem,
):
    t = lax.axis_index("tensor")
    vec_copy = pltpu.make_async_copy(vec_hbm, vec, vsem.at[0])
    vec_copy.start()
    fetch = [pltpu.make_async_copy(grad_hbm.at[k], low.at[k], isem.at[k]) for k in range(CHUNKS)]
    order = [0, 1, 2, 3, 8] + list(range(4, 8)) + list(range(9, 12))
    pairs = [(i, b) for i in range(2) for b in range(BLOCKS)]
    refs = ((out_low, outg), (gin_low, ging))
    passed = [pltpu.make_async_copy(refs[i][0].at[b], rows.at[i, b], rsem.at[i, b]) for i, b in pairs]
    for cp in passed:
        cp.start()
    for k in order:
        fetch[k].start()

    sends = []
    for n, (i, b) in enumerate(pairs):
        passed[n].wait()
        full[i, b] = rows[i, b].astype(F32)
        cp = pltpu.make_async_copy(full.at[i, b], refs[i][1].at[b], ssem.at[i, b])
        cp.start()
        sends.append(cp)
    for k in order:
        fetch[k].wait()
        if k >= 9:
            wide[k - 5] = low[k].astype(F32)
            src, dst = wide.at[k - 5], (wqg, wkg, wvg)[k - 9]
        elif k >= 4 and k < 8:
            wide[k - 4] = low[k].astype(F32)
            src, dst = wide.at[k - 4], w1g.at[:, pl.ds((k - 4) * HALF, HALF)]
        elif k == 8:
            turned[4] = low[k].T.astype(F32)
            src, dst = turned.at[4], wog
        else:
            turned[k] = low[k].T.astype(F32)
            src, dst = turned.at[k], w2g.at[pl.ds(k * HALF, HALF), :]
        cp = pltpu.make_async_copy(src, dst, osem.at[k])
        cp.start()
        sends.append(cp)
    vec_copy.wait()

    def pick(r):
        return jnp.where(t == 0, vec[r : r + 1, :], vec[r + 1 : r + 2, :]).reshape(HALF)

    def whole(r):
        return jnp.concatenate([vec[r : r + 1, :], vec[r + 1 : r + 2, :]], axis=1).reshape(WIDTH)

    qbg[...] = pick(0)
    vbg[...] = pick(2)
    for ref, r in ((obg, 4), (g1g, 6), (s1g, 8), (rbg, 10), (g2g, 12), (s2g, 14)):
        ref[...] = whole(r)
    lines = [jnp.where(t == 0, vec[16 + k : 17 + k, :], vec[20 + k : 21 + k, :]) for k in range(4)]
    ebg[...] = jnp.concatenate(lines, axis=1).reshape(HIDDEN)

    for cp in sends:
        cp.wait()


def finish(out, gin, grads, vec):
    vm = pl.BlockSpec(memory_space=pltpu.VMEM)
    hbm = pl.BlockSpec(memory_space=pltpu.HBM)
    f = lambda *shape: jax.ShapeDtypeStruct(shape, F32)
    return pl.pallas_call(
        finish_kernel,
        out_shape=(f(BLOCKS, ROWS, WIDTH), f(BLOCKS, ROWS, WIDTH), f(WIDTH, HALF), f(WIDTH, HALF), f(WIDTH, HALF), f(HALF, WIDTH), f(WIDTH, HIDDEN), f(HIDDEN, WIDTH),
                   f(HALF), f(HALF), f(WIDTH), f(WIDTH), f(WIDTH), f(HIDDEN), f(WIDTH), f(WIDTH), f(WIDTH)),
        in_specs=[hbm, hbm, hbm, hbm],
        out_specs=(hbm,) * 8 + (vm,) * 9,
        scratch_shapes=[
            pltpu.VMEM((CHUNKS, WIDTH, HALF), BF),
            pltpu.VMEM((7, WIDTH, HALF), F32),
            pltpu.VMEM((5, HALF, WIDTH), F32),
            pltpu.VMEM((2, BLOCKS, ROWS, WIDTH), BF),
            pltpu.VMEM((2, BLOCKS, ROWS, WIDTH), F32),
            pltpu.VMEM((24, HALF), F32),
            pltpu.SemaphoreType.DMA((CHUNKS,)),
            pltpu.SemaphoreType.DMA((CHUNKS,)),
            pltpu.SemaphoreType.DMA((2, BLOCKS)),
            pltpu.SemaphoreType.DMA((2, BLOCKS)),
            pltpu.SemaphoreType.DMA((1,)),
        ],
        compiler_params=pltpu.CompilerParams(vmem_limit_bytes=67043328),
    )(grads, out, gin, vec)


def local(
    n_dp, inputs, segments, padding, query_weight, query_bias, key_weight, value_weight, value_bias,
    output_weight, output_bias, first_gain, first_shift, expand_weight, expand_bias,
    reduce_weight, reduce_bias, second_gain, second_shift, cotangent,
):
    out, gin, grads, vec = layer(
        n_dp, inputs, cotangent, segments, padding, query_bias, value_bias, expand_bias, output_bias, first_gain,
        first_shift, reduce_bias, second_gain, second_shift, query_weight, key_weight, value_weight,
        output_weight, expand_weight, reduce_weight,
    )
    out, gin, wq, wk, wv, wo, w1, w2, qb, vb, ob, g1, s1, eb, rb, g2, s2 = finish(out, gin, grads, vec)
    return (out, gin, wq, qb, wk, wv, vb, wo, ob, g1, s1, w1, eb, w2, rb, g2, s2)


def solution(mesh):
    tokens = P(None, ("dp", "tensor"), None)
    return jax.shard_map(
        functools.partial(local, mesh.shape["dp"]),
        mesh=mesh,
        in_specs=(
            tokens, P(None, "dp"), P(None, "dp"), P(None, "tensor"), P("tensor"), P(None, "tensor"),
            P(None, "tensor"), P("tensor"), P("tensor", None), P(), P(), P(), P(None, "tensor"),
            P("tensor"), P("tensor", None), P(), P(), P(), tokens,
        ),
        out_specs=(
            tokens, tokens, P(None, "tensor"), P("tensor"), P(None, "tensor"), P(None, "tensor"),
            P("tensor"), P("tensor", None), P(), P(), P(), P(None, "tensor"), P("tensor"),
            P("tensor", None), P(), P(), P(),
        ),
        check_vma=False,
    )
```
